32 devices in a mesh: dp: 8 (over z, y), mp: 4 (over x, core).
Axes of the slice: x: 2, y: 2, z: 4, core: 2. Of those that a mesh axis runs over, the one named last changes fastest.
Arguments:
- tokens: bfloat16 [16560, 1024], P('dp'), may hold values from -6 to 6
- offsets: int32 [48, 5], P('dp'), may hold values from 0 to 308, as said below
- first_gain: float32 [1024], replicated, may hold values from 0.1 to 1.9
- first_shift: float32 [1024], replicated, may hold values from -1.8 to 1.8
- qkv_weight: float32 [1024, 3, 1024], P('dp', None, 'mp'), may hold values from -0.1875 to 0.1875
- qv_bias: float32 [2, 1024], P(None, 'mp'), may hold values from -1.8 to 1.8
- proj_weight: float32 [1024, 1024], P('mp', 'dp'), may hold values from -0.5 to 0.5
- proj_bias: float32 [1024], replicated, may hold values from -1.8 to 1.8
- second_gain: float32 [1024], replicated, may hold values from 0.1 to 1.9
- second_shift: float32 [1024], replicated, may hold values from -1.8 to 1.8
- expand_weight: float32 [1024, 4096], P('dp', 'mp'), may hold values from -0.1875 to 0.1875
- expand_bias: float32 [4096], P('mp'), may hold values from -1.8 to 1.8
- shrink_weight: float32 [4096, 1024], P('mp', 'dp'), may hold values from -0.09375 to 0.09375
- shrink_bias: float32 [1024], replicated, may hold values from -1.8 to 1.8
- cotangent: bfloat16 [16560, 1024], P('dp'), may hold values from -6 to 6
Outputs:
- out: bfloat16 [16560, 1024], P('dp')
- d_tokens: float32 [16560, 1024], P('dp')
- d_first_gain: float32 [1024], replicated
- d_first_shift: float32 [1024], replicated
- d_qkv_weight: float32 [1024, 3, 1024], P('dp', None, 'mp')
- d_qv_bias: float32 [2, 1024], P(None, 'mp')
- d_proj_weight: float32 [1024, 1024], P('mp', 'dp')
- d_proj_bias: float32 [1024], replicated
- d_second_gain: float32 [1024], replicated
- d_second_shift: float32 [1024], replicated
- d_expand_weight: float32 [1024, 4096], P('dp', 'mp')
- d_expand_bias: float32 [4096], P('mp')
- d_shrink_weight: float32 [4096, 1024], P('mp', 'dp')
- d_shrink_bias: float32 [1024], replicated
The draws below stay inside these ranges and needn't reach their ends.
Inputs may be any that keep to these rules, and one draw needn't show every extreme that they name: `offsets`: each row lists, rising, where the 5 crops of one crop set start within its 345 tokens: the first starts at 0, one crop spans 197 tokens, the others 37 each, and the last ends at the set's end.
All inputs are finite; a program needn't handle non-finite values.
Results may differ from the reference program's by a relative error of at most 0.015.
Values may be sent and summed in bfloat16 or wider, within the bound.
No kernel may reach another device: no remote copies, remote signals or barrier semaphores. Data moves between devices by JAX's collectives and lax.ppermute only.
A program may use at most 128 MiB of HBM per device.

```python
import jax
import jax.numpy as jnp
from jax import lax

D = 1024
HEADS = 16
HEAD_DIM = 64
FF = 4096
GLOBAL_TOKENS = 197
LOCAL_TOKENS = 37
LOCALS_SET = 4
SET_TOKENS = 345
SETS = 48
TOKENS = 16560


def draw_offsets(key, part):
    drawn = jax.random.randint(key, (SETS, 1), 0, LOCALS_SET + 1)
    row_index = jnp.arange(SETS, dtype=jnp.int32)[:, None]
    placed = jnp.where(row_index == 0, 0, drawn).astype(jnp.int32)
    slots = jnp.arange(LOCALS_SET + 1, dtype=jnp.int32)[None, :]
    spans = jnp.where(slots == placed, GLOBAL_TOKENS, LOCAL_TOKENS).astype(jnp.int32)
    return (jnp.cumsum(spans, axis=1) - spans).astype(jnp.int32)


def spiked(result, stream_key, source, target, shards_of, factor):
    def block_of(dim):
        return (jnp.arange(result.shape[dim]) // (result.shape[dim] // shards_of)).reshape((-1,) + (1,) * (result.ndim - 1 - dim))

    first = jax.random.permutation(stream_key, shards_of)[block_of(target)]
    second = (block_of(target) + shards_of // 2) % shards_of
    return jnp.where((block_of(source) == first) | (block_of(source) == second), factor * result, result)


def shard_levels(rng, extent, cuts, smallest, top_value):
    loudness = 1.0
    for position, shards_of in cuts:
        heights = jax.random.uniform(jax.random.fold_in(jax.random.fold_in(rng, 6), position), (shards_of,), jnp.float32, smallest / len(cuts), top_value / len(cuts))
        loudness = loudness * jnp.repeat(jnp.exp(heights), extent[position] // shards_of).reshape((-1,) + (1,) * (len(extent) - 1 - position))
    return loudness


def centred(key, dims, scale, bound, cuts=(), kind=jnp.bfloat16):
    result = scale * jax.random.normal(key, dims, jnp.float32)
    if cuts:
        result = result * shard_levels(key, dims, cuts, -0.22, 0.18)
    return jnp.clip(result, -bound, bound).astype(kind)


def heavy_noise(key, shape, width, reach, shards, heavy, held_as=jnp.bfloat16):
    entries = width * jax.random.normal(key, shape, jnp.float32)
    if shards:
        entries = entries * shard_levels(key, shape, shards, -0.22, 0.18)
    return jnp.clip(spiked(entries, jax.random.fold_in(key, 3), *heavy), -reach, reach).astype(held_as)


def setup_inputs(seed: int = 0) -> dict:
    arg_keys = jax.random.split(jax.random.key(seed), 16)
    tokens = heavy_noise(arg_keys[0], (TOKENS, D), 1.0, 6.0, ((0, 8),), (0, 1, 8, 2.0))
    offsets = draw_offsets(jax.random.fold_in(arg_keys[15], 71), 0)
    first_gain = jnp.clip(1.0 + 0.18 * jax.random.normal(arg_keys[2], (D,), jnp.float32), 0.1, 1.9)
    first_shift = centred(arg_keys[3], (D,), 0.3, 1.8, (), jnp.float32)
    qkv_weight = centred(arg_keys[4], (D, 3, D), D ** -0.5, 0.1875, ((0, 8), (2, 4)), jnp.float32)
    qv_bias = centred(arg_keys[5], (2, D), 0.3, 1.8, ((1, 4),), jnp.float32)
    proj_weight = centred(arg_keys[6], (D, D), (D // 8) ** -0.5, 0.5, ((0, 4), (1, 8)), jnp.float32)
    proj_bias = centred(arg_keys[7], (D,), 0.3, 1.8, (), jnp.float32)
    second_gain = jnp.clip(1.0 + 0.18 * jax.random.normal(arg_keys[8], (D,), jnp.float32), 0.1, 1.9)
    second_shift = centred(arg_keys[9], (D,), 0.3, 1.8, (), jnp.float32)
    expand_weight = centred(arg_keys[10], (D, FF), D ** -0.5, 0.1875, ((0, 8), (1, 4)), jnp.float32)
    expand_bias = centred(arg_keys[11], (FF,), 0.3, 1.8, ((0, 4),), jnp.float32)
    shrink_weight = centred(arg_keys[12], (FF, D), FF ** -0.5, 0.09375, ((0, 4), (1, 8)), jnp.float32)
    shrink_bias = centred(arg_keys[13], (D,), 0.3, 1.8, (), jnp.float32)
    cotangent = heavy_noise(arg_keys[14], (TOKENS, D), 1.0, 6.0, ((0, 8),), (0, 1, 8, 2.0))
    return dict(tokens=tokens, offsets=offsets, first_gain=first_gain, first_shift=first_shift, qkv_weight=qkv_weight, qv_bias=qv_bias, proj_weight=proj_weight, proj_bias=proj_bias, second_gain=second_gain, second_shift=second_shift, expand_weight=expand_weight, expand_bias=expand_bias, shrink_weight=shrink_weight, shrink_bias=shrink_bias, cotangent=cotangent)


@jax.custom_vjp
def low(v):
    return lax.optimization_barrier(v.astype(jnp.bfloat16)).astype(jnp.float32)

@jax.custom_vjp
def low_back(v):
    return v

def low_keep(v):
    return (low(v), None)

def low_pass(kept, grad):
    return (grad,)

def back_keep(v):
    return (v, None)

def back_low(kept, grad):
    return (low(grad),)
low.defvjp(low_keep, low_pass)
low_back.defvjp(back_keep, back_low)
highest = lax.Precision.HIGHEST
norm_eps = 1e-06
masked_score = -1e+30
root_half = 0.7071067811865476

def layer_norm(values, gain, shift):
    centre = lax.optimization_barrier(jnp.mean(values, axis=-1, keepdims=True))
    offset_rows = values - centre
    spread = lax.optimization_barrier(jnp.mean(offset_rows * offset_rows, axis=-1, keepdims=True))
    return offset_rows * lax.rsqrt(spread + norm_eps) * gain + shift

def gelu(values):
    return 0.5 * values * (1.0 + lax.erf(values * root_half))

def product(left, right):
    return jnp.dot(left, right, precision=highest, preferred_element_type=jnp.float32)

def attend_set(pieces):
    query_rows, key_rows, value_rows, crop_ids = pieces
    scores = jnp.einsum('qhe,khe->hqk', query_rows, key_rows, precision=highest) * HEAD_DIM ** (-0.5)
    scores = low_back(scores)
    same_crop = crop_ids[:, None] == crop_ids[None, :]
    scores = jnp.where(same_crop[None], scores, masked_score)
    peak_score = lax.optimization_barrier(jnp.max(scores, axis=-1, keepdims=True))
    raised = jnp.exp(scores - peak_score)
    weights = raised / lax.optimization_barrier(jnp.sum(raised, axis=-1, keepdims=True))
    return jnp.einsum('hqk,khe->qhe', low(weights), value_rows, precision=highest)

def reference(tokens, offsets, first_gain, first_shift, qkv_weight, qv_bias, proj_weight, proj_bias, second_gain, second_shift, expand_weight, expand_bias, shrink_weight, shrink_bias, cotangent):
    positions = jnp.arange(SET_TOKENS, dtype=jnp.int32)
    crop_ids = lax.optimization_barrier(jnp.sum((positions[None, :, None] >= offsets[:, None, :]).astype(jnp.int32), axis=-1))

    def forward(inputs, gain_one, shift_one, qkv_full, qv_full, proj_full, proj_shift, gain_two, shift_two, expand_full, expand_shift, shrink_full, shrink_shift):
        normed = low(layer_norm(inputs, gain_one, shift_one))
        projected = jnp.einsum('td,dcf->tcf', normed, low(qkv_full), precision=highest)
        query_rows = low(low_back(projected[:, 0]) + qv_full[0])
        key_rows = low(low_back(projected[:, 1]))
        value_rows = low(low_back(projected[:, 2]) + qv_full[1])
        shaped = (SETS, SET_TOKENS, HEADS, HEAD_DIM)
        attended = lax.map(jax.checkpoint(attend_set), (query_rows.reshape(shaped), key_rows.reshape(shaped), value_rows.reshape(shaped), crop_ids))
        attended = low(low_back(attended.reshape(TOKENS, D)))
        residual = inputs + low_back(product(attended, low(proj_full))) + proj_shift
        second = low(layer_norm(residual, gain_two, shift_two))
        hidden_pre = low_back(product(second, low(expand_full))) + expand_shift
        hidden = low(gelu(hidden_pre))
        return residual + low_back(product(hidden, low(shrink_full))) + shrink_shift
    outputs, pullback = jax.vjp(forward, tokens.astype(jnp.float32), first_gain, first_shift, qkv_weight, qv_bias, proj_weight, proj_bias, second_gain, second_shift, expand_weight, expand_bias, shrink_weight, shrink_bias)
    grads = pullback(cotangent.astype(jnp.float32))
    return (outputs.astype(jnp.bfloat16), grads[0], grads[1], grads[2], grads[3], grads[4], grads[5], grads[6], grads[7], grads[8], grads[9], grads[10], grads[11], grads[12])
```

```python
import functools

import jax
import jax.numpy as jnp
import numpy as np
from jax import lax
from jax.experimental import pallas as pl
from jax.experimental.pallas import tpu as pltpu
from jax.sharding import PartitionSpec as P

HEAD_DIM = 64
SET_TOKENS = 345
SET_ROWS = 352
LANES = 128
CHUNK = 256

norm_eps = 1e-06
masked_score = -1e30
root_half = 0.7071067811865476
density_scale = 0.3989422804014327
f32 = jnp.float32
bf16 = jnp.bfloat16
NN = (((1,), (0,)), ((), ()))
NT = (((1,), (1,)), ((), ()))
TN = (((0,), (0,)), ((), ()))
ANY = pl.BlockSpec(memory_space=pl.ANY)
SMEM = pl.BlockSpec(memory_space=pltpu.SMEM)


def dot(left, right, dims=NN):
    return lax.dot_general(left, right, dims, preferred_element_type=f32)


def call(body, grid, in_specs, out_specs, out_shape, scratch, flops, moved, name):
    return pl.pallas_call(
        body,
        grid_spec=pltpu.PrefetchScalarGridSpec(
            num_scalar_prefetch=1,
            grid=grid,
            in_specs=in_specs,
            out_specs=out_specs,
            scratch_shapes=scratch,
        ),
        out_shape=out_shape,
        compiler_params=pltpu.CompilerParams(
            dimension_semantics=("arbitrary",) * len(grid), vmem_limit_bytes=58 * 2**20
        ),
        cost_estimate=pl.CostEstimate(
            flops=int(flops), bytes_accessed=int(moved), transcendentals=0
        ),
        name=name,
    )


def shape(dims, dtype):
    return jax.ShapeDtypeStruct(tuple(dims), dtype)


def ring_order(count):
    width = 1
    while 2 * (2 * width) ** 2 <= count:
        width *= 2
    length = count // width
    if width == 1:
        return list(range(count))
    path = []
    for z in range(length):
        columns = range(1, width) if z % 2 == 0 else range(width - 1, 0, -1)
        path += [z * width + y for y in columns]
    path += [z * width for z in range(length - 1, -1, -1)]
    return path


class Ring:
    def __init__(self, count):
        self.count = count
        self.order = ring_order(count)
        self.place = {rank: i for i, rank in enumerate(self.order)}
        self.ahead = [(self.order[i], self.order[(i + 1) % count]) for i in range(count)]
        self.behind = [(self.order[i], self.order[(i - 1) % count]) for i in range(count)]

    def rank_at(self, rank, offset):
        return self.order[(self.place[rank] + offset) % self.count]

    def send_ahead(self, value):
        return lax.ppermute(value, "dp", self.ahead)

    def send_behind(self, value):
        return lax.ppermute(value, "dp", self.behind)

    def gather(self, block, axis):
        half = block.shape[axis] // 2
        pieces = [block]
        forward = backward = block
        for step in range(1, self.count // 2 + 1):
            if step == self.count // 2:
                forward = lax.slice_in_dim(forward, 0, half, axis=axis)
                backward = lax.slice_in_dim(backward, half, 2 * half, axis=axis)
            forward = self.send_ahead(forward)
            backward = self.send_behind(backward)
            pieces += [forward, backward]
        return pieces

    def piece_rows(self, rows):
        table = []
        middle = self.count // 2
        for rank in range(self.count):
            starts = [rank * rows]
            for step in range(1, middle + 1):
                ahead = self.rank_at(rank, -step) * rows
                behind = self.rank_at(rank, step) * rows
                if step == middle:
                    behind += rows // 2
                starts += [ahead, behind]
            table.append(starts)
        return np.array(table, np.int32)

    def block_rows(self, rows):
        middle = self.count // 2
        return np.array(
            [
                [self.rank_at(rank, d) * rows for d in range(-middle, middle + 1)]
                for rank in range(self.count)
            ],
            np.int32,
        )

    def scatter(self, whole, axis, starts):
        middle = self.count // 2
        rows = whole.shape[axis] // self.count
        half = rows // 2

        def block(distance, start=0, size=rows):
            return lax.dynamic_slice_in_dim(
                whole, starts[distance + middle] + start, size, axis=axis
            ).astype(f32)

        forward = block(middle, 0, half).astype(bf16)
        backward = block(-middle, half, half).astype(bf16)
        for step in range(1, middle + 1):
            forward = self.send_ahead(forward)
            backward = self.send_behind(backward)
            near = middle - step
            if near == 0:
                break
            got_ahead, got_behind = forward.astype(f32), backward.astype(f32)
            if step == 1:
                forward = jnp.concatenate(
                    [block(near, 0, half) + got_ahead, block(near, half, half)], axis=axis
                )
                backward = jnp.concatenate(
                    [block(-near, 0, half), block(-near, half, half) + got_behind], axis=axis
                )
            else:
                forward = block(near) + got_ahead
                backward = block(-near) + got_behind
            forward, backward = forward.astype(bf16), backward.astype(bf16)
        return block(0) + forward.astype(f32) + backward.astype(f32)


def across(value, step, chips):
    pairs = [
        (x * 2 + core, (x + step) % chips * 2 + core) for x in range(chips) for core in range(2)
    ]
    return lax.ppermute(value, "mp", pairs)


def partner(value, chips):
    return lax.ppermute(value, "mp", [(m, m ^ 1) for m in range(2 * chips)])


def gather_rows(own, chips):
    rows = {(0, 0): own}
    for step in range(1, chips):
        rows[(step, 0)] = across(own, step, chips)
    for step in range(chips):
        rows[(step, 1)] = partner(rows[(step, 0)], chips)
    return rows


def start_all(copies, sems):
    moves = [pltpu.make_async_copy(src, dst, sems.at[i]) for i, (src, dst) in enumerate(copies)]
    for move in moves:
        move.start()
    return moves


def wait_all(moves):
    for move in moves:
        move.wait()


def weight_copies(info, base, pieces, unit, targets):
    copies = []
    for i, piece in enumerate(pieces):
        rows = piece.shape[-2]
        place = pl.ds(pl.multiple_of(info[base + i], unit), rows)
        for source, target in targets:
            copies.append((source(piece), target(place)))
    return copies


def qkv_body(info, x_ref, bias_ref, *rest, base, unit, chips, count):
    pieces, (out_ref, weights, sems) = rest[:count], rest[count:]
    width = weights.shape[2]

    @pl.when(pl.program_id(0) == 0)
    def _():
        targets = [
            (
                lambda piece, b=b: piece.at[b, :, pl.ds(0, width)],
                lambda place, b=b: weights.at[b, place, :],
            )
            for b in range(chips)
        ]
        wait_all(start_all(weight_copies(info, base, pieces, unit, targets), sems))

    x = x_ref[...]
    step = CHUNK if width % CHUNK == 0 else LANES
    for b in range(chips):

        def columns(i, _, b=b):
            at = pl.ds(pl.multiple_of(i * step, step), step)
            to = pl.ds(pl.multiple_of(b * width + i * step, step), step)
            out_ref[:, to] = (dot(x, weights[b, :, at]) + bias_ref[:, to]).astype(bf16)
            return 0

        lax.fori_loop(0, width // step, columns, 0)


def head_mask(head):
    lane = lax.broadcasted_iota(jnp.int32, (1, LANES), 1)
    return (lane < HEAD_DIM) if head == 0 else (lane >= HEAD_DIM)


def keep_head(value, head):
    return jnp.where(head_mask(head), value, jnp.zeros_like(value))


def attend_body(info, qkv_ref, key_ids, query_ids, out_ref, log_ref, block):
    @pl.when(pl.program_id(1) == 0)
    def _():
        block[...] = jnp.where(key_ids[0] == query_ids[0], 0.0, masked_score)

    factor = HEAD_DIM**-0.5
    query = qkv_ref[:, 0:LANES] * jnp.asarray(factor, bf16)
    key = qkv_ref[:, LANES : 2 * LANES]
    value = qkv_ref[:, 2 * LANES : 3 * LANES]
    halves = []
    for head in range(2):
        scores = dot(key, keep_head(query, head), NT) + block[...]
        peak = jnp.max(scores, axis=0, keepdims=True)
        raised = jnp.exp(scores - peak)
        total = jnp.sum(raised, axis=0, keepdims=True)
        mixed = dot(keep_head(value, head), raised.astype(bf16), TN)
        halves.append(mixed * (1.0 / total))
        log_ref[0, 0, head : head + 1, :] = peak + jnp.log(total)
    out_ref[...] = (halves[0] + halves[1]).T.astype(bf16)


def attend_back_body(info, qkv_ref, key_ids, query_ids, log_ref, grad_ref, out_ref, sum_ref, block):
    turn = pl.program_id(1)

    @pl.when(pl.program_id(0) == 0)
    def _():
        block[turn] = jnp.where(key_ids[0] == query_ids[0], 0.0, masked_score)

    factor = HEAD_DIM**-0.5
    query = qkv_ref[:, 0:LANES] * jnp.asarray(factor, bf16)
    key = qkv_ref[:, LANES : 2 * LANES]
    value = qkv_ref[:, 2 * LANES : 3 * LANES]
    grad = grad_ref[...]
    grad_query = grad_key = grad_value = 0.0
    for head in range(2):
        query_one = keep_head(query, head)
        grad_one = keep_head(grad, head)
        scores = dot(key, query_one, NT) + block[turn]
        weights = jnp.exp(scores - log_ref[0, 0, head : head + 1, :])
        grad_value += dot(weights.astype(bf16), grad_one)
        grad_weights = dot(value, grad_one, NT)
        centre = jnp.sum(weights * grad_weights, axis=0, keepdims=True)
        low = (weights * (grad_weights - centre)).astype(bf16)
        grad_key += dot(low, query_one)
        grad_query += dot(keep_head(key, head), low, TN)
    grad_query = (grad_query * factor).T
    out_ref[:, 0:LANES] = grad_query.astype(bf16)
    out_ref[:, LANES : 2 * LANES] = grad_key.astype(bf16)
    out_ref[:, 2 * LANES : 3 * LANES] = grad_value.astype(bf16)

    @pl.when(turn == 0)
    def _():
        sum_ref[...] = jnp.zeros_like(sum_ref)

    sum_ref[0, :, 0:LANES] += jnp.sum(grad_query, axis=0, keepdims=True)
    sum_ref[0, :, 2 * LANES : 3 * LANES] += jnp.sum(grad_value, axis=0, keepdims=True)


def proj_weights(info, base, pieces, unit, chips, weights, sems):
    width = weights.shape[1] // chips
    start = pieces[0].shape[2] - width
    targets = [
        (
            lambda piece, b=b: piece.at[b, :, pl.ds(start, width)],
            lambda place, b=b: weights.at[place, pl.ds(b * width, width)],
        )
        for b in range(chips)
    ]
    return start_all(weight_copies(info, base, pieces, unit, targets), sems)


def proj_body(info, att_ref, *rest, base, unit, chips, count):
    pieces, (out_ref, weights, sems) = rest[:count], rest[count:]
    wait_all(proj_weights(info, base, pieces, unit, chips, weights, sems))
    for i in range(out_ref.shape[1] // CHUNK):
        at = slice(i * CHUNK, (i + 1) * CHUNK)
        out_ref[:, at] = dot(att_ref[...], weights[at, :], NT).astype(bf16)


def row_step(rows):
    return 176 if rows % 176 == 0 else rows


def proj_norm_body(
    info, att_ref, x_ref, got_ref, bias_ref, gain_ref, shift_ref, *rest, base, unit, chips, count
):
    pieces, (residual_ref, low_ref, weights, sems) = rest[:count], rest[count:]
    wait_all(proj_weights(info, base, pieces, unit, chips, weights, sems))
    for i in range(residual_ref.shape[1] // CHUNK):
        at = slice(i * CHUNK, (i + 1) * CHUNK)
        residual_ref[:, at] = (
            dot(att_ref[...], weights[at, :], NT)
            + got_ref[:, at].astype(f32)
            + x_ref[:, at].astype(f32)
            + bias_ref[:, at]
        )
    step = row_step(residual_ref.shape[0])

    def rows(i, _):
        at = pl.ds(pl.multiple_of(i * step, 16), step)
        value = residual_ref[at, :]
        centred = value - jnp.mean(value, axis=-1, keepdims=True)
        spread = jnp.mean(centred * centred, axis=-1, keepdims=True)
        scale = lax.rsqrt(spread + norm_eps)
        low_ref[at, :] = (centred * scale * gain_ref[...] + shift_ref[...]).astype(bf16)
        return 0

    lax.fori_loop(0, residual_ref.shape[0] // step, rows, 0)


def mlp_body(info, cot_ref, bias_ref, *rest, base, unit, count, parts):
    pieces, rest = rest[:count], rest[count:]
    seconds, rest = rest[:parts], rest[parts:]
    hidden_ref, pre_ref, second_ref, out_ref, sum_ref = rest[:5]
    expand, shrink, rows, sems, row_sems = rest[5:]
    width = expand.shape[1]
    turn = pl.program_id(0)

    @pl.when(turn == 0)
    def _():
        targets = [
            (
                lambda piece: piece.at[:, pl.ds(0, width)],
                lambda place: expand.at[place, :],
            ),
            (
                lambda piece: piece.at[:, pl.ds(width, width)],
                lambda place: shrink.at[place, :],
            ),
        ]
        moves = start_all(weight_copies(info, base, pieces, unit, targets), sems)
        start_all([(seconds[i], rows.at[i]) for i in range(parts)], row_sems)
        wait_all(moves)
        sum_ref[...] = jnp.zeros_like(sum_ref)

    pltpu.make_async_copy(seconds[0], rows.at[turn], row_sems.at[turn]).wait()

    def columns(i, _):
        at = pl.ds(pl.multiple_of(i * CHUNK, CHUNK), CHUNK)
        pre = dot(rows[turn], expand[:, at]) + bias_ref[:, at]
        below = 0.5 * (1.0 + lax.erf(pre * root_half))
        density = density_scale * jnp.exp(-0.5 * pre * pre)
        hidden_ref[:, at] = (pre * below).astype(bf16)
        grad = dot(cot_ref[...], shrink[:, at]) * (below + pre * density)
        sum_ref[:, at] += jnp.sum(grad, axis=0, keepdims=True)
        pre_ref[:, at] = grad.astype(bf16)
        return 0

    lax.fori_loop(0, width // CHUNK, columns, 0)

    def back(i, _):
        at = pl.ds(pl.multiple_of(i * CHUNK, CHUNK), CHUNK)
        second_ref[:, at] = dot(pre_ref[...], expand[at, :], NT).astype(bf16)
        out_ref[:, at] = dot(hidden_ref[...], shrink[at, :], NT).astype(bf16)
        return 0

    lax.fori_loop(0, out_ref.shape[1] // CHUNK, back, 0)


def mlp_grad_body(info, cot_ref, *rest, cot_base, parts):
    seconds, rest = rest[:parts], rest[parts:]
    hiddens, pres, out_ref, left, right, sems = rest[:2], rest[2:4], *rest[4:]
    phase = pl.program_id(0)
    rows = left.shape[0] // parts

    def moves(index):
        if index == 0:
            pairs = [(seconds[i], left.at[pl.ds(i * rows, rows)]) for i in range(parts)]
            source = pres
        else:
            pairs = [
                (
                    cot_ref.at[pl.ds(pl.multiple_of(info[cot_base + i] * rows, 16), rows)],
                    left.at[pl.ds(i * rows, rows)],
                )
                for i in range(parts)
            ]
            source = hiddens
        first = source[0].shape[0]
        second = source[1].shape[0]
        pairs.append((source[0], right.at[pl.ds(0, first)]))
        pairs.append((source[1], right.at[pl.ds(first, second)]))
        return pairs

    for index in range(2):

        @pl.when((phase == index) & (pl.program_id(1) == 0))
        def _(index=index):
            wait_all(start_all(moves(index), sems))

    at = pl.ds(pl.multiple_of(pl.program_id(1) * CHUNK, CHUNK), CHUNK)
    out_ref[...] = dot(left[:, at], right[...], TN).astype(bf16)


def norm_back(value, grad, gain):
    centred = value - jnp.mean(value, axis=-1, keepdims=True)
    spread = jnp.mean(centred * centred, axis=-1, keepdims=True)
    scale = lax.rsqrt(spread + norm_eps)
    normal = centred * scale
    weighted = grad * gain
    middle = jnp.mean(weighted, axis=-1, keepdims=True)
    slope = jnp.mean(weighted * normal, axis=-1, keepdims=True)
    return normal, scale * (weighted - middle - normal * slope)


def residual_back_body(info, residual_ref, cot_ref, gain_ref, *rest, parts):
    grads, (grad_ref, low_ref, sum_ref) = rest[:parts], rest[parts:]
    grad = grads[0][...].astype(f32)
    for other in grads[1:]:
        grad += other[...].astype(f32)
    normal, back = norm_back(residual_ref[...], grad, gain_ref[...])
    cotangent = cot_ref[...].astype(f32)
    total = cotangent + back
    grad_ref[...] = total
    low_ref[...] = total.astype(bf16)

    @pl.when(pl.program_id(0) == 0)
    def _():
        sum_ref[...] = jnp.zeros_like(sum_ref)

    sum_ref[0:1, :] += jnp.sum(grad * normal, axis=0, keepdims=True)
    sum_ref[1:2, :] += jnp.sum(grad, axis=0, keepdims=True)
    sum_ref[2:3, :] += jnp.sum(total, axis=0, keepdims=True)
    sum_ref[3:4, :] += jnp.sum(cotangent, axis=0, keepdims=True)


def proj_back_body(info, own_ref, got_ref, att_ref, *rest, base, unit, chips, count):
    pieces, (grad_ref, weight_ref, weights, rows, sems, row_sems) = rest[:count], rest[count:]
    moves = proj_weights(info, base, pieces, unit, chips, weights, sems)
    half = own_ref.shape[0]
    core = info[0]
    wait_all(
        start_all(
            [
                (own_ref, rows.at[pl.ds(pl.multiple_of(core * half, 16), half)]),
                (got_ref, rows.at[pl.ds(pl.multiple_of((1 - core) * half, 16), half)]),
            ],
            row_sems,
        )
    )
    wait_all(moves)
    width = weights.shape[1]
    for i in range(width // CHUNK):
        at = slice(i * CHUNK, (i + 1) * CHUNK)
        grad_ref[:, at] = dot(rows[...], weights[:, at]).astype(bf16)
    part = width // chips
    for i in range(rows.shape[1] // CHUNK):
        at = slice(i * CHUNK, (i + 1) * CHUNK)
        both = dot(rows[:, at], att_ref[...], TN).astype(bf16)
        for b in range(chips):
            weight_ref[b, at, :] = both[:, b * part : (b + 1) * part]


def qkv_grad_body(info, low_ref, grad_ref, proj_ref, out_ref, *, chips):
    width = grad_ref.shape[1] // chips
    out_ref[:, :, width:] = proj_ref[...]
    step = CHUNK if width % CHUNK == 0 else LANES
    for b in range(chips):
        for i in range(width // step):
            at = slice(b * width + i * step, b * width + (i + 1) * step)
            out_ref[b, :, i * step : (i + 1) * step] = dot(
                low_ref[...], grad_ref[:, at], TN
            ).astype(bf16)


def qkv_weights(info, base, pieces, unit, chips, weights, sems):
    width = weights.shape[2]
    targets = [
        (
            lambda piece, b=b: piece.at[b, :, pl.ds(0, width)],
            lambda place, b=b: weights.at[b, place, :],
        )
        for b in range(chips)
    ]
    return start_all(weight_copies(info, base, pieces, unit, targets), sems)


def back_columns(grad_ref, weights, at, chips):
    width = weights.shape[2]
    total = 0.0
    for b in range(chips):
        total += dot(grad_ref[:, b * width : (b + 1) * width], weights[b, at, :], NT)
    return total


def first_body(info, grad_ref, *rest, base, unit, chips, count):
    pieces, (out_ref, weights, sems) = rest[:count], rest[count:]
    wait_all(qkv_weights(info, base, pieces, unit, chips, weights, sems))
    for i in range(out_ref.shape[1] // CHUNK):
        at = slice(i * CHUNK, (i + 1) * CHUNK)
        out_ref[:, at] = back_columns(grad_ref, weights, at, chips).astype(bf16)


def first_norm_body(
    info, grad_ref, got_ref, x_ref, res_ref, gain_ref, *rest, base, unit, chips, count
):
    pieces, (out_ref, low_ref, sum_ref, weights, total, sems) = rest[:count], rest[count:]
    wait_all(qkv_weights(info, base, pieces, unit, chips, weights, sems))
    for i in range(total.shape[1] // CHUNK):
        at = slice(i * CHUNK, (i + 1) * CHUNK)
        total[:, at] = back_columns(grad_ref, weights, at, chips) + got_ref[:, at].astype(f32)
    step = row_step(total.shape[0])
    sum_ref[...] = jnp.zeros_like(sum_ref)

    def rows(i, _):
        at = pl.ds(pl.multiple_of(i * step, 16), step)
        grad = total[at, :]
        normal, back = norm_back(x_ref[at, :].astype(f32), grad, gain_ref[...])
        back = back + res_ref[at, :]
        out_ref[at, :] = back
        low_ref[at, :] = back.astype(bf16)
        sum_ref[0:1, :] += jnp.sum(grad * normal, axis=0, keepdims=True)
        sum_ref[1:2, :] += jnp.sum(grad, axis=0, keepdims=True)
        return 0

    lax.fori_loop(0, total.shape[0] // step, rows, 0)


def layer_norm(values, gain, shift):
    centre = jnp.mean(values, axis=-1, keepdims=True)
    offset_rows = values - centre
    spread = jnp.mean(offset_rows * offset_rows, axis=-1, keepdims=True)
    return offset_rows * lax.rsqrt(spread + norm_eps) * gain + shift


def shards(
    tokens,
    offsets,
    first_gain,
    first_shift,
    qkv_weight,
    qv_bias,
    proj_weight,
    proj_bias,
    second_gain,
    second_shift,
    expand_weight,
    expand_bias,
    shrink_weight,
    shrink_bias,
    cotangent,
):
    dim = tokens.shape[1]
    sets = offsets.shape[0]
    part = qkv_weight.shape[2]
    ff = expand_weight.shape[1]
    chips = lax.axis_size("mp") // 2
    ring = Ring(lax.axis_size("dp"))
    dp_index = lax.axis_index("dp")
    mp_index = lax.axis_index("mp")
    x_index, core = mp_index // 2, mp_index % 2
    sets_x = -(-sets // chips)
    slots = sets_x * chips
    rows_x = sets_x * SET_ROWS
    half = rows_x // 2
    pairs = part // LANES
    groups = chips * pairs
    unit_rows = dim // ring.count
    unit = unit_rows // 2
    keys = [(step, other) for step in range(chips) for other in range(2)]
    near = [key for key in keys if key[0] == 0]
    far = [key for key in keys if key[0] > 0]

    def pad_sets(value):
        value = value.reshape(sets, SET_TOKENS, dim)
        return jnp.pad(value, ((0, slots - sets), (0, SET_ROWS - SET_TOKENS), (0, 0)))

    def mine(value):
        return lax.dynamic_slice_in_dim(value, x_index * sets_x, sets_x, axis=0)

    x_rows = mine(pad_sets(tokens)).reshape(rows_x, dim)
    cot = pad_sets(cotangent).reshape(slots * SET_ROWS, dim)
    starts = mine(jnp.pad(offsets, ((0, slots - sets), (0, 0))))
    positions = jnp.arange(SET_ROWS, dtype=jnp.int32)
    crop_ids = jnp.sum((positions[None, :, None] >= starts[:, None, :]).astype(jnp.int32), axis=-1)
    crop_ids = jnp.where(positions[None, :] < SET_TOKENS, crop_ids, -1)
    key_ids, query_ids = crop_ids[:, :, None], crop_ids[:, None, :]

    row_starts = lax.dynamic_index_in_dim(ring.piece_rows(unit_rows), dp_index, 0, False)
    block_starts = lax.dynamic_index_in_dim(ring.block_rows(unit_rows), dp_index, 0, False)
    cot_places = [(x_index - step) % chips * 2 + (core ^ other) for step, other in near + far]
    info = jnp.concatenate(
        [jnp.stack([core, *cot_places]).astype(jnp.int32), row_starts.astype(jnp.int32)]
    )
    cot_base = 1
    base = 1 + len(keys)

    qkv_shard = qkv_weight.astype(bf16).reshape(unit_rows, 3, pairs, LANES)
    qkv_shard = qkv_shard.transpose(0, 2, 1, 3).reshape(unit_rows, 3 * part)
    shard = jnp.concatenate([qkv_shard, proj_weight.astype(bf16).T], axis=1)
    bias_shard = jnp.zeros((pairs, 3, LANES), f32)
    bias_shard = bias_shard.at[:, 0].set(qv_bias[0].reshape(pairs, LANES))
    bias_shard = bias_shard.at[:, 2].set(qv_bias[1].reshape(pairs, LANES)).reshape(1, 3 * part)
    shards_x, bias_x = [shard], [bias_shard]
    for step in range(1, chips):
        shards_x.append(across(shard, step, chips))
        bias_x.append(across(bias_shard, step, chips))
    attn_pieces = ring.gather(jnp.stack(shards_x), 1)
    qkv_bias = jnp.concatenate(bias_x, axis=1)
    mlp_shard = jnp.concatenate(
        [expand_weight.astype(bf16), shrink_weight.astype(bf16).T], axis=1
    )
    mlp_pieces = ring.gather(mlp_shard, 0)
    count = len(attn_pieces)
    settings = dict(base=base, unit=unit, chips=chips, count=count)
    copies = count * chips
    sem = pltpu.SemaphoreType.DMA
    row = lambda value: value.reshape(1, -1)
    whole = lambda *dims: pl.BlockSpec(dims, lambda *_: (0,) * len(dims))

    first_low = layer_norm(x_rows.astype(f32), first_gain, first_shift).astype(bf16)
    width = 3 * part
    qkv = call(
        functools.partial(qkv_body, **settings),
        (2,),
        [pl.BlockSpec((half, dim), lambda i, _: (i, 0)), whole(1, chips * width)] + [ANY] * count,
        pl.BlockSpec((half, chips * width), lambda i, _: (i, 0)),
        shape((rows_x, chips * width), bf16),
        [pltpu.VMEM((chips, dim, width), bf16), sem((copies,))],
        2 * rows_x * dim * chips * width,
        2 * (rows_x + width * chips) * dim,
        "qkv",
    )(info, first_low, qkv_bias, *attn_pieces)

    score_flops = 2 * sets_x * groups * 2 * SET_ROWS * SET_ROWS * LANES
    attended, logs = call(
        attend_body,
        (sets_x, groups),
        [
            pl.BlockSpec((SET_ROWS, 3 * LANES), lambda s, i, _: (s, i)),
            pl.BlockSpec((1, SET_ROWS, 1), lambda s, i, _: (s, 0, 0)),
            pl.BlockSpec((1, 1, SET_ROWS), lambda s, i, _: (s, 0, 0)),
        ],
        [
            pl.BlockSpec((SET_ROWS, LANES), lambda s, i, _: (s, i)),
            pl.BlockSpec((1, 1, 2, SET_ROWS), lambda s, i, _: (s, i, 0, 0)),
        ],
        [
            shape((rows_x, groups * LANES), bf16),
            shape((sets_x, groups, 2, SET_ROWS), f32),
        ],
        [pltpu.VMEM((SET_ROWS, SET_ROWS), f32)],
        4 * score_flops,
        2 * rows_x * chips * width,
        "attend",
    )(info, qkv, key_ids, query_ids)

    att_width = groups * LANES
    proj_flops = 2 * half * att_width * dim
    proj_scratch = [pltpu.VMEM((dim, att_width), bf16), sem((copies,))]
    other_half = lambda *dims: pl.BlockSpec(dims, lambda i, info: (1 - info[0], 0))
    own_half = lambda *dims: pl.BlockSpec(dims, lambda i, info: (info[0], 0))
    sent = call(
        functools.partial(proj_body, **settings),
        (1,),
        [other_half(half, att_width)] + [ANY] * count,
        whole(half, dim),
        shape((half, dim), bf16),
        proj_scratch,
        proj_flops,
        2 * dim * (att_width + half),
        "proj_send",
    )(info, attended, *attn_pieces)
    got = partner(sent, chips)
    residual, second_low = call(
        functools.partial(proj_norm_body, **settings),
        (1,),
        [own_half(half, att_width), own_half(half, dim), whole(half, dim)]
        + [whole(1, dim)] * 3
        + [ANY] * count,
        [whole(half, dim), whole(half, dim)],
        [shape((half, dim), f32), shape((half, dim), bf16)],
        proj_scratch,
        proj_flops,
        2 * dim * (att_width + 5 * half),
        "proj_norm",
    )(
        info,
        attended,
        x_rows,
        got,
        row(proj_bias),
        row(second_gain),
        row(second_shift),
        *attn_pieces,
    )
    seconds = gather_rows(second_low, chips)

    def feed(group, first):
        parts = len(group)
        outs = call(
            functools.partial(mlp_body, base=base, unit=unit, count=count, parts=parts),
            (parts,),
            [
                pl.BlockSpec((half, dim), lambda i, info: (info[cot_base + first + i], 0)),
                whole(1, ff),
            ]
            + [ANY] * (count + parts),
            [pl.BlockSpec((half, ff), lambda i, _: (i, 0))] * 2
            + [pl.BlockSpec((half, dim), lambda i, _: (i, 0))] * 2
            + [whole(1, ff)],
            [shape((parts * half, ff), bf16)] * 2
            + [shape((parts * half, dim), bf16)] * 2
            + [shape((1, ff), f32)],
            [
                pltpu.VMEM((dim, ff), bf16),
                pltpu.VMEM((dim, ff), bf16),
                pltpu.VMEM((parts, half, dim), bf16),
                sem((2 * count,)),
                sem((parts,)),
            ],
            8 * parts * half * dim * ff,
            4 * dim * ff + parts * half * (4 * ff + 8 * dim),
            "mlp",
        )(info, cot, row(expand_bias), *mlp_pieces, *[seconds[key] for key in group])
        cut = lambda value: {
            key: lax.slice_in_dim(value, i * half, (i + 1) * half) for i, key in enumerate(group)
        }
        return outs[0], outs[1], cut(outs[2]), cut(outs[3]), outs[4]

    hidden_far, pre_far, back_far, out_far, sum_far = feed(far, len(near))
    hidden_near, pre_near, back_near, out_near, sum_near = feed(near, 0)
    back_parts, out_parts = {**back_far, **back_near}, {**out_far, **out_near}
    expand_bias_grad = (sum_far + sum_near).reshape(ff)

    def spread_sum(parts):
        terms = [parts[(0, 0)], partner(parts[(0, 1)], chips)]
        for step in range(1, chips):
            both = parts[(step, 0)].astype(f32) + partner(parts[(step, 1)], chips).astype(f32)
            terms.append(across(both.astype(bf16), chips - step, chips))
        return terms

    back_terms = spread_sum(back_parts)
    mlp_grad = call(
        functools.partial(mlp_grad_body, cot_base=cot_base, parts=len(keys)),
        (2, dim // CHUNK),
        [ANY] * (5 + len(keys)),
        pl.BlockSpec((CHUNK, ff), lambda p, i, _: (i, p)),
        shape((dim, 2 * ff), bf16),
        [
            pltpu.VMEM((len(keys) * half, dim), bf16),
            pltpu.VMEM((len(keys) * half, ff), bf16),
            sem((len(keys) + 2,)),
        ],
        4 * len(keys) * half * dim * ff,
        4 * len(keys) * half * (dim + ff),
        "mlp_grad",
    )(
        info,
        cot,
        *[seconds[key] for key in near + far],
        hidden_near,
        hidden_far,
        pre_near,
        pre_far,
    )
    mlp_grad = ring.scatter(mlp_grad, 0, block_starts)
    out_terms = spread_sum(out_parts)

    step_rows = row_step(half)
    own_rows = pl.BlockSpec(
        (step_rows, dim), lambda i, info: (info[0] * (half // step_rows) + i, 0)
    )
    cot_rows = pl.BlockSpec(
        (step_rows, dim), lambda i, info: (info[cot_base] * (half // step_rows) + i, 0)
    )
    plain_rows = pl.BlockSpec((step_rows, dim), lambda i, _: (i, 0))
    grad_residual, residual_low, sums_two = call(
        functools.partial(residual_back_body, parts=len(back_terms)),
        (half // step_rows,),
        [plain_rows, cot_rows, whole(1, dim)] + [plain_rows] * len(back_terms),
        [plain_rows, plain_rows, whole(8, dim)],
        [shape((half, dim), f32), shape((half, dim), bf16), shape((8, dim), f32)],
        [],
        30 * half * dim,
        half * dim * 18,
        "residual_back",
    )(info, residual, cot, row(second_gain), *back_terms)
    low_other = partner(residual_low, chips)

    grad_attended, proj_grad = call(
        functools.partial(proj_back_body, **settings),
        (1,),
        [ANY, ANY, whole(rows_x, att_width)] + [ANY] * count,
        [whole(rows_x, att_width), whole(chips, dim, part)],
        [shape((rows_x, att_width), bf16), shape((chips, dim, part), bf16)],
        [
            pltpu.VMEM((dim, att_width), bf16),
            pltpu.VMEM((rows_x, dim), bf16),
            sem((copies,)),
            sem((2,)),
        ],
        4 * rows_x * att_width * dim,
        2 * rows_x * (dim + 2 * att_width) + 4 * dim * att_width,
        "proj_back",
    )(info, residual_low, low_other, attended, *attn_pieces)
    grad_qkv, qkv_sums = call(
        attend_back_body,
        (groups, sets_x),
        [
            pl.BlockSpec((SET_ROWS, 3 * LANES), lambda i, s, _: (s, i)),
            pl.BlockSpec((1, SET_ROWS, 1), lambda i, s, _: (s, 0, 0)),
            pl.BlockSpec((1, 1, SET_ROWS), lambda i, s, _: (s, 0, 0)),
            pl.BlockSpec((1, 1, 2, SET_ROWS), lambda i, s, _: (s, i, 0, 0)),
            pl.BlockSpec((SET_ROWS, LANES), lambda i, s, _: (s, i)),
        ],
        [
            pl.BlockSpec((SET_ROWS, 3 * LANES), lambda i, s, _: (s, i)),
            pl.BlockSpec((1, 1, 3 * LANES), lambda i, s, _: (i, 0, 0)),
        ],
        [
            shape((rows_x, chips * width), bf16),
            shape((groups, 1, 3 * LANES), f32),
        ],
        [pltpu.VMEM((sets_x, SET_ROWS, SET_ROWS), f32)],
        10 * score_flops,
        6 * rows_x * chips * width,
        "attend_back",
    )(info, qkv, key_ids, query_ids, logs, grad_attended)

    first_scratch = [pltpu.VMEM((chips, dim, width), bf16)]
    first_flops = 2 * half * chips * width * dim
    sent_first = call(
        functools.partial(first_body, **settings),
        (1,),
        [other_half(half, chips * width)] + [ANY] * count,
        whole(half, dim),
        shape((half, dim), bf16),
        first_scratch + [sem((copies,))],
        first_flops,
        2 * chips * width * (half + dim),
        "first_send",
    )(info, grad_qkv, *attn_pieces)
    got_first = partner(sent_first, chips)
    attn_grad = call(
        functools.partial(qkv_grad_body, chips=chips),
        (dim // CHUNK,),
        [
            pl.BlockSpec((rows_x, CHUNK), lambda i, _: (0, i)),
            whole(rows_x, chips * width),
            pl.BlockSpec((chips, CHUNK, part), lambda i, _: (0, i, 0)),
        ],
        pl.BlockSpec((chips, CHUNK, width + part), lambda i, _: (0, i, 0)),
        shape((chips, dim, width + part), bf16),
        [],
        2 * rows_x * dim * chips * width,
        2 * rows_x * (dim + chips * width) + 2 * chips * dim * width,
        "qkv_grad",
    )(info, first_low, grad_qkv, proj_grad)
    grad_tokens, tokens_low, sums_one = call(
        functools.partial(first_norm_body, **settings),
        (1,),
        [
            own_half(half, chips * width),
            whole(half, dim),
            own_half(half, dim),
            whole(half, dim),
            whole(1, dim),
        ]
        + [ANY] * count,
        [whole(half, dim), whole(half, dim), whole(8, dim)],
        [shape((half, dim), f32), shape((half, dim), bf16), shape((8, dim), f32)],
        first_scratch + [pltpu.VMEM((half, dim), f32), sem((copies,))],
        first_flops,
        2 * chips * width * (half + dim) + 14 * half * dim,
        "first_norm",
    )(info, grad_qkv, got_first, x_rows, grad_residual, row(first_gain), *attn_pieces)
    attn_grad = ring.scatter(attn_grad, 1, block_starts)
    attn_low = attn_grad.astype(bf16)
    attn_part = attn_grad[0]
    for step in range(1, chips):
        attn_part = attn_part + across(attn_low[step], chips - step, chips).astype(f32)

    def assemble(own, rows):
        rows = {**rows, (0, 0): own}
        total = jnp.zeros((slots * SET_ROWS, dim), own.dtype)
        for (step, other), value in rows.items():
            place = ((x_index - step) % chips * 2 + (core ^ other)) * half
            total = lax.dynamic_update_slice_in_dim(total, value.astype(own.dtype), place, 0)
        total = total.reshape(slots, SET_ROWS, dim)[:sets, :SET_TOKENS]
        return total.reshape(sets * SET_TOKENS, dim)

    out_own = residual + shrink_bias
    for term in out_terms:
        out_own = out_own + term.astype(f32)
    out_own = out_own.astype(bf16)
    outputs = assemble(out_own, gather_rows(out_own, chips))
    grad_tokens = assemble(grad_tokens, gather_rows(tokens_low, chips))

    shared = jnp.concatenate(
        [sums_one[0], sums_one[1], sums_two[2], sums_two[0], sums_two[1], sums_two[3]]
    )
    bias_sums = qkv_sums.reshape(chips, pairs, 3, LANES)
    bias_sums = jnp.stack([bias_sums[:, :, 0], bias_sums[:, :, 2]], axis=1).reshape(chips, 2 * part)
    bias_own = bias_sums[0]
    if chips == 2:
        got = across(jnp.concatenate([shared, bias_sums[1]]), 1, chips)
        shared = shared + got[: 6 * dim]
        bias_own = bias_own + got[6 * dim :]
    else:
        bit = 1
        while bit < chips:
            shared = shared + lax.ppermute(
                shared, "mp", [(m, m ^ (2 * bit)) for m in range(2 * chips)]
            )
            bit *= 2
        for step in range(1, chips):
            bias_own = bias_own + across(bias_sums[step], chips - step, chips)
    shared = shared + partner(shared, chips)
    small = jnp.concatenate([shared, bias_own, expand_bias_grad]).reshape(-1, LANES)
    bit = 1
    while bit < ring.count:
        small = small + lax.ppermute(small, "dp", [(r, r ^ bit) for r in range(ring.count)])
        bit *= 2
    small = small.reshape(-1)
    shared = small[: 6 * dim].reshape(6, dim)
    bias_own = small[6 * dim : 6 * dim + 2 * part].reshape(2, part)
    expand_bias_grad = small[6 * dim + 2 * part :]

    qkv_part = attn_part[:, :width].reshape(unit_rows, pairs, 3, LANES)
    qkv_part = qkv_part.transpose(0, 2, 1, 3).reshape(unit_rows, 3, part)
    return (
        outputs,
        grad_tokens,
        shared[0],
        shared[1],
        qkv_part,
        bias_own,
        attn_part[:, width:].T,
        shared[2],
        shared[3],
        shared[4],
        mlp_grad[:, :ff],
        expand_bias_grad,
        mlp_grad[:, ff:].T,
        shared[5],
    )


def solution(mesh):
    placed = (
        P("dp", None),
        P("dp", None),
        P(),
        P(),
        P("dp", None, "mp"),
        P(None, "mp"),
        P("mp", "dp"),
        P(),
        P(),
        P(),
        P("dp", "mp"),
        P("mp"),
        P("mp", "dp"),
        P(),
        P("dp", None),
    )
    return jax.shard_map(
        shards,
        mesh=mesh,
        in_specs=placed,
        out_specs=(
            P("dp", None),
            P("dp", None),
            P(),
            P(),
            P("dp", None, "mp"),
            P(None, "mp"),
            P("mp", "dp"),
            P(),
            P(),
            P(),
            P("dp", "mp"),
            P("mp"),
            P("mp", "dp"),
            P(),
        ),
        check_vma=False,
    )
```

```python
import functools

import jax
import jax.numpy as jnp
import numpy as np
from jax import lax
from jax.experimental import pallas as pl
from jax.experimental.pallas import tpu as pltpu
from jax.sharding import PartitionSpec as P

HEAD_DIM = 64
SET_TOKENS = 345
SET_ROWS = 352
LANES = 128
CHUNK = 256

norm_eps = 1e-06
masked_score = -1e30
root_half = 0.7071067811865476
density_scale = 0.3989422804014327
f32 = jnp.float32
bf16 = jnp.bfloat16
NN = (((1,), (0,)), ((), ()))
NT = (((1,), (1,)), ((), ()))
TN = (((0,), (0,)), ((), ()))
ANY = pl.BlockSpec(memory_space=pl.ANY)
SMEM = pl.BlockSpec(memory_space=pltpu.SMEM)


def dot(left, right, dims=NN):
    return lax.dot_general(left, right, dims, preferred_element_type=f32)


def call(body, grid, in_specs, out_specs, out_shape, scratch, name, aliases=None):
    return pl.pallas_call(
        body,
        grid_spec=pltpu.PrefetchScalarGridSpec(
            num_scalar_prefetch=1,
            grid=grid,
            in_specs=in_specs,
            out_specs=out_specs,
            scratch_shapes=scratch,
        ),
        out_shape=out_shape,
        compiler_params=pltpu.CompilerParams(
            dimension_semantics=("arbitrary",) * len(grid), vmem_limit_bytes=58 * 2**20
        ),
        cost_estimate=pl.CostEstimate(flops=1, bytes_accessed=1, transcendentals=0),
        name=name,
        input_output_aliases=aliases or {},
    )


def tie(value, *earlier):
    return lax.optimization_barrier((value, earlier))[0]


class Order:
    def __init__(self, info):
        self.info = info
        self.now = info

    def after(self, value):
        return tie(value, self.now)

    def run(self, kernel, *values, wait=()):
        out = kernel(tie(self.info, self.now, wait), *values)
        self.now = out[0] if isinstance(out, (list, tuple)) else out
        return out


def shape(dims, dtype):
    return jax.ShapeDtypeStruct(tuple(dims), dtype)


def ring_order(count):
    width = 1
    while 2 * (2 * width) ** 2 <= count:
        width *= 2
    length = count // width
    if width == 1:
        return list(range(count))
    path = []
    for z in range(length):
        columns = range(1, width) if z % 2 == 0 else range(width - 1, 0, -1)
        path += [z * width + y for y in columns]
    path += [z * width for z in range(length - 1, -1, -1)]
    return path


class Ring:
    def __init__(self, count):
        self.count = count
        self.order = ring_order(count)
        self.place = {rank: i for i, rank in enumerate(self.order)}
        self.ahead = [(self.order[i], self.order[(i + 1) % count]) for i in range(count)]
        self.behind = [(self.order[i], self.order[(i - 1) % count]) for i in range(count)]

    def rank_at(self, rank, offset):
        return self.order[(self.place[rank] + offset) % self.count]

    def send_ahead(self, value):
        return lax.ppermute(value, "dp", self.ahead)

    def send_behind(self, value):
        return lax.ppermute(value, "dp", self.behind)

    def gather_steps(self, block, axis, order):
        half = block.shape[axis] // 2
        forward = backward = block
        for step in range(1, self.count // 2 + 1):
            if step == self.count // 2:
                forward = lax.slice_in_dim(forward, 0, half, axis=axis)
                backward = lax.slice_in_dim(backward, half, 2 * half, axis=axis)
            forward, backward = order.after((forward, backward))
            forward = self.send_ahead(forward)
            backward = self.send_behind(backward)
            yield forward, backward

    def piece_rows(self, rows):
        table = []
        middle = self.count // 2
        for rank in range(self.count):
            starts = [rank * rows]
            for step in range(1, middle + 1):
                ahead = self.rank_at(rank, -step) * rows
                behind = self.rank_at(rank, step) * rows
                if step == middle:
                    behind += rows // 2
                starts += [ahead, behind]
            table.append(starts)
        return np.array(table, np.int32)

    def block_rows(self, rows):
        middle = self.count // 2
        return np.array(
            [
                [self.rank_at(rank, d) * rows for d in range(-middle, middle + 1)]
                for rank in range(self.count)
            ],
            np.int32,
        )

    def scatter_steps(self, whole, axis, starts, order):
        middle = self.count // 2
        rows = whole.shape[axis] // self.count
        half = rows // 2

        def block(distance, start=0, size=rows):
            return lax.dynamic_slice_in_dim(
                whole, starts[distance + middle] + start, size, axis=axis
            ).astype(f32)

        forward = block(middle, 0, half).astype(bf16)
        backward = block(-middle, half, half).astype(bf16)
        for step in range(1, middle + 1):
            forward, backward = order.after((forward, backward))
            forward = self.send_ahead(forward)
            backward = self.send_behind(backward)
            yield forward, backward
            near = middle - step
            if near == 0:
                break
            forward, backward = order.after((forward, backward))
            got_ahead, got_behind = forward.astype(f32), backward.astype(f32)
            if step == 1:
                forward = jnp.concatenate(
                    [block(near, 0, half) + got_ahead, block(near, half, half)], axis=axis
                )
                backward = jnp.concatenate(
                    [block(-near, 0, half), block(-near, half, half) + got_behind], axis=axis
                )
            else:
                forward = block(near) + got_ahead
                backward = block(-near) + got_behind
            forward, backward = forward.astype(bf16), backward.astype(bf16)
        yield block(0) + forward.astype(f32) + backward.astype(f32)


def across(value, step, chips):
    pairs = [
        (x * 2 + core, (x + step) % chips * 2 + core) for x in range(chips) for core in range(2)
    ]
    return lax.ppermute(value, "mp", pairs)


def partner(value, chips):
    return lax.ppermute(value, "mp", [(m, m ^ 1) for m in range(2 * chips)])


def layer_norm(values, gain, shift):
    centre = jnp.mean(values, axis=-1, keepdims=True)
    offset_rows = values - centre
    spread = jnp.mean(offset_rows * offset_rows, axis=-1, keepdims=True)
    return offset_rows * lax.rsqrt(spread + norm_eps) * gain + shift


def start_all(copies, sems):
    moves = [pltpu.make_async_copy(src, dst, sems.at[i]) for i, (src, dst) in enumerate(copies)]
    for move in moves:
        move.start()
    return moves


def wait_all(moves):
    for move in moves:
        move.wait()


def weight_copies(info, base, pieces, unit, targets):
    copies = []
    for i, piece in enumerate(pieces):
        rows = piece.shape[-2]
        place = pl.ds(pl.multiple_of(info[base + i], unit), rows)
        for source, target in targets:
            copies.append((source(piece), target(place)))
    return copies


def pad_body(info, in_ref, out_ref, rows, *, sets):
    total = in_ref.shape[0]
    rows[0:total, :] = in_ref[...].astype(f32)
    inside = lax.broadcasted_iota(jnp.int32, (SET_ROWS, 1), 0) < SET_TOKENS
    for g in range(out_ref.shape[0] // SET_ROWS):
        to = slice(g * SET_ROWS, (g + 1) * SET_ROWS)
        if g < sets:
            value = rows[g * SET_TOKENS : g * SET_TOKENS + SET_ROWS, :]
            out_ref[to, :] = jnp.where(inside, value, 0.0).astype(bf16)
        else:
            out_ref[to, :] = jnp.zeros((SET_ROWS, out_ref.shape[1]), bf16)


def assemble_body(info, *refs, base, sets):
    pieces, (out_ref, padded, packed) = refs[:-3], refs[-3:]
    half = pieces[0].shape[0]
    for i, piece in enumerate(pieces):
        place = pl.ds(pl.multiple_of(info[base + i] * half, 16), half)
        padded[place, :] = piece[...].astype(f32)
    target = out_ref if out_ref.dtype == f32 else packed
    for g in range(sets):
        target[g * SET_TOKENS : (g + 1) * SET_TOKENS, :] = padded[
            g * SET_ROWS : g * SET_ROWS + SET_TOKENS, :
        ]
    if out_ref.dtype != f32:
        out_ref[...] = packed[0 : out_ref.shape[0], :].astype(out_ref.dtype)


def first_low_body(info, x_ref, gain_ref, shift_ref, out_ref):
    out_ref[...] = layer_norm(x_ref[...].astype(f32), gain_ref[...], shift_ref[...]).astype(bf16)


def qkv_weights(info, base, pieces, unit, chips, weights, sems):
    width = weights.shape[1] // chips
    targets = [
        (
            lambda piece, b=b: piece.at[b, :, pl.ds(0, width)],
            lambda place, b=b: weights.at[place, pl.ds(b * width, width)],
        )
        for b in range(chips)
    ]
    return start_all(weight_copies(info, base, pieces, unit, targets), sems)


def qkv_body(info, x_ref, bias_ref, *rest, base, unit, chips, count):
    pieces, (out_ref, weights, sems) = rest[:count], rest[count:]

    @pl.when(pl.program_id(0) == 0)
    def _():
        wait_all(qkv_weights(info, base, pieces, unit, chips, weights, sems))

    out_ref[...] = (dot(x_ref[...], weights[...]) + bias_ref[...]).astype(bf16)


def head_mask(head):
    lane = lax.broadcasted_iota(jnp.int32, (1, LANES), 1)
    return (lane < HEAD_DIM) if head == 0 else (lane >= HEAD_DIM)


def keep_head(value, head):
    return jnp.where(head_mask(head), value, jnp.zeros_like(value))


def attend_body(info, qkv_ref, key_ids, query_ids, *rest):
    out_ref, log_ref, block = rest[-3:]

    @pl.when(pl.program_id(1) == 0)
    def _():
        block[...] = jnp.where(key_ids[0] == query_ids[0], 0.0, masked_score)

    factor = HEAD_DIM**-0.5
    query = qkv_ref[:, 0:LANES] * jnp.asarray(factor, bf16)
    key = qkv_ref[:, LANES : 2 * LANES]
    value = qkv_ref[:, 2 * LANES : 3 * LANES]
    halves = []
    for head in range(2):
        scores = dot(key, keep_head(query, head), NT) + block[...]
        peak = jnp.max(scores, axis=0, keepdims=True)
        raised = jnp.exp(scores - peak)
        total = jnp.sum(raised, axis=0, keepdims=True)
        mixed = dot(keep_head(value, head), raised.astype(bf16), TN)
        halves.append(mixed * (1.0 / total))
        log_ref[0, 0, head : head + 1, :] = peak + jnp.log(total)
    out_ref[...] = (halves[0] + halves[1]).T.astype(bf16)


def attend_back_body(info, qkv_ref, key_ids, query_ids, log_ref, grad_ref, *rest):
    out_ref, sum_ref, block = rest[-3:]
    turn = pl.program_id(1)

    @pl.when(pl.program_id(0) == 0)
    def _():
        block[turn] = jnp.where(key_ids[0] == query_ids[0], 0.0, masked_score)

    factor = HEAD_DIM**-0.5
    query = qkv_ref[:, 0:LANES] * jnp.asarray(factor, bf16)
    key = qkv_ref[:, LANES : 2 * LANES]
    value = qkv_ref[:, 2 * LANES : 3 * LANES]
    grad = grad_ref[...]
    grad_query = grad_key = grad_value = 0.0
    for head in range(2):
        query_one = keep_head(query, head)
        grad_one = keep_head(grad, head)
        scores = dot(key, query_one, NT) + block[turn]
        weights = jnp.exp(scores - log_ref[0, 0, head : head + 1, :])
        grad_value += dot(weights.astype(bf16), grad_one)
        grad_weights = dot(value, grad_one, NT)
        centre = jnp.sum(weights * grad_weights, axis=0, keepdims=True)
        low = (weights * (grad_weights - centre)).astype(bf16)
        grad_key += dot(low, query_one)
        grad_query += dot(keep_head(key, head), low, TN)
    grad_query = (grad_query * factor).T
    out_ref[:, 0:LANES] = grad_query.astype(bf16)
    out_ref[:, LANES : 2 * LANES] = grad_key.astype(bf16)
    out_ref[:, 2 * LANES : 3 * LANES] = grad_value.astype(bf16)

    @pl.when(turn == 0)
    def _():
        sum_ref[...] = jnp.zeros_like(sum_ref)

    sum_ref[0, :, 0:LANES] += jnp.sum(grad_query, axis=0, keepdims=True)
    sum_ref[0, :, 2 * LANES : 3 * LANES] += jnp.sum(grad_value, axis=0, keepdims=True)


def proj_weights(info, base, pieces, unit, chips, weights, sems):
    width = weights.shape[1] // chips
    start = pieces[0].shape[2] - width
    targets = [
        (
            lambda piece, b=b: piece.at[b, :, pl.ds(start, width)],
            lambda place, b=b: weights.at[place, pl.ds(b * width, width)],
        )
        for b in range(chips)
    ]
    return start_all(weight_copies(info, base, pieces, unit, targets), sems)


def proj_body(info, att_ref, *rest, base, unit, chips, count):
    pieces, (out_ref, weights, sems) = rest[:count], rest[count:]
    wait_all(proj_weights(info, base, pieces, unit, chips, weights, sems))
    out_ref[...] = dot(att_ref[...], weights[...], NT).astype(bf16)


def row_step(rows):
    return 176 if rows % 176 == 0 else rows


def proj_norm_body(
    info, att_ref, x_ref, got_ref, bias_ref, gain_ref, shift_ref, *rest, base, unit, chips, count
):
    pieces, (residual_ref, low_ref, weights, sems) = rest[:count], rest[count:]
    wait_all(proj_weights(info, base, pieces, unit, chips, weights, sems))
    residual_ref[...] = dot(att_ref[...], weights[...], NT)
    step = row_step(residual_ref.shape[0])

    def rows(i, _):
        at = pl.ds(pl.multiple_of(i * step, 16), step)
        value = residual_ref[at, :] + got_ref[at, :].astype(f32)
        value = value + x_ref[at, :].astype(f32) + bias_ref[...]
        residual_ref[at, :] = value
        centred = value - jnp.mean(value, axis=-1, keepdims=True)
        spread = jnp.mean(centred * centred, axis=-1, keepdims=True)
        scale = lax.rsqrt(spread + norm_eps)
        low_ref[at, :] = (centred * scale * gain_ref[...] + shift_ref[...]).astype(bf16)
        return 0

    lax.fori_loop(0, residual_ref.shape[0] // step, rows, 0)


def mlp_body(info, cot_ref, bias_ref, *rest, base, unit, count, parts):
    pieces, rest = rest[:count], rest[count:]
    seconds, rest = rest[:parts], rest[parts:]
    hidden_ref, pre_ref, second_ref, out_ref, sum_ref = rest[:5]
    expand, shrink, rows, sems, row_sems = rest[5:]
    width = expand.shape[1]
    turn = pl.program_id(0)

    @pl.when(turn == 0)
    def _():
        targets = [
            (
                lambda piece: piece.at[:, pl.ds(0, width)],
                lambda place: expand.at[place, :],
            ),
            (
                lambda piece: piece.at[:, pl.ds(width, width)],
                lambda place: shrink.at[place, :],
            ),
        ]
        moves = start_all(weight_copies(info, base, pieces, unit, targets), sems)
        start_all([(seconds[i], rows.at[i]) for i in range(parts)], row_sems)
        wait_all(moves)
        sum_ref[...] = jnp.zeros_like(sum_ref)

    pltpu.make_async_copy(seconds[0], rows.at[turn], row_sems.at[turn]).wait()

    span = 2 * CHUNK if width % (2 * CHUNK) == 0 else LANES

    def columns(i, _):
        at = pl.ds(pl.multiple_of(i * span, span), span)
        pre = dot(rows[turn], expand[:, at]) + bias_ref[:, at]
        below = 0.5 * (1.0 + lax.erf(pre * root_half))
        density = density_scale * jnp.exp(-0.5 * pre * pre)
        hidden_ref[:, at] = (pre * below).astype(bf16)
        grad = dot(cot_ref[...], shrink[:, at]) * (below + pre * density)
        sum_ref[:, at] += jnp.sum(grad, axis=0, keepdims=True)
        pre_ref[:, at] = grad.astype(bf16)
        return 0

    lax.fori_loop(0, width // span, columns, 0)
    second_ref[...] = dot(pre_ref[...], expand[...], NT).astype(bf16)
    out_ref[...] = dot(hidden_ref[...], shrink[...], NT).astype(bf16)


def mlp_grad_body(info, cot_ref, *rest, cot_base, parts):
    seconds, rest = rest[:parts], rest[parts:]
    hiddens, pres, out_ref, left, right, sems = rest[:2], rest[2:4], *rest[4:]
    phase = pl.program_id(0)
    rows = left.shape[1] // parts
    span = out_ref.shape[0]

    def moves(index):
        pairs = []
        for i in range(parts):
            source = seconds[i]
            if index == 1:
                place = pl.multiple_of(info[cot_base + i] * rows, 16)
                source = cot_ref.at[pl.ds(place, rows)]
            pairs.append((source, left.at[index, pl.ds(i * rows, rows)]))
        start = 0
        for source in (pres, hiddens)[index]:
            pairs.append((source, right.at[index, pl.ds(start, source.shape[0])]))
            start += source.shape[0]
        return [
            pltpu.make_async_copy(src, dst, sems.at[index, i]) for i, (src, dst) in enumerate(pairs)
        ]

    @pl.when((phase == 0) & (pl.program_id(1) == 0))
    def _():
        for index in range(2):
            for move in moves(index):
                move.start()

    for index in range(2):

        @pl.when((phase == index) & (pl.program_id(1) == 0))
        def _(index=index):
            wait_all(moves(index))

    at = pl.ds(pl.multiple_of(pl.program_id(1) * span, span), span)
    out_ref[...] = dot(left[phase, :, at], right[phase], TN).astype(bf16)


def norm_back(value, grad, gain):
    centred = value - jnp.mean(value, axis=-1, keepdims=True)
    spread = jnp.mean(centred * centred, axis=-1, keepdims=True)
    scale = lax.rsqrt(spread + norm_eps)
    normal = centred * scale
    weighted = grad * gain
    middle = jnp.mean(weighted, axis=-1, keepdims=True)
    slope = jnp.mean(weighted * normal, axis=-1, keepdims=True)
    return normal, scale * (weighted - middle - normal * slope)


def residual_back_body(info, residual_ref, cot_ref, gain_ref, *rest, parts):
    grads, (grad_ref, low_ref, sum_ref) = rest[:parts], rest[parts:]
    grad = grads[0][...].astype(f32)
    for other in grads[1:]:
        grad += other[...].astype(f32)
    normal, back = norm_back(residual_ref[...], grad, gain_ref[...])
    cotangent = cot_ref[...].astype(f32)
    total = cotangent + back
    grad_ref[...] = total
    low_ref[...] = total.astype(bf16)

    @pl.when(pl.program_id(0) == 0)
    def _():
        sum_ref[...] = jnp.zeros_like(sum_ref)

    sum_ref[0:1, :] += jnp.sum(grad * normal, axis=0, keepdims=True)
    sum_ref[1:2, :] += jnp.sum(grad, axis=0, keepdims=True)
    sum_ref[2:3, :] += jnp.sum(total, axis=0, keepdims=True)
    sum_ref[3:4, :] += jnp.sum(cotangent, axis=0, keepdims=True)


def proj_back_body(info, own_ref, got_ref, att_ref, *rest, base, unit, chips, count):
    pieces, (grad_ref, weight_ref, weights, rows, sems, row_sems) = rest[:count], rest[count:]
    moves = proj_weights(info, base, pieces, unit, chips, weights, sems)
    half = own_ref.shape[0]
    core = info[0]
    wait_all(
        start_all(
            [
                (own_ref, rows.at[pl.ds(pl.multiple_of(core * half, 16), half)]),
                (got_ref, rows.at[pl.ds(pl.multiple_of((1 - core) * half, 16), half)]),
            ],
            row_sems,
        )
    )
    wait_all(moves)
    width = weights.shape[1]
    grad_ref[...] = dot(rows[...], weights[...]).astype(bf16)
    part = width // chips
    both = dot(rows[...], att_ref[...], TN).astype(bf16)
    for b in range(chips):
        weight_ref[b] = both[:, b * part : (b + 1) * part]


def qkv_grad_body(info, low_ref, grad_ref, proj_ref, out_ref, *, chips):
    width = grad_ref.shape[1] // chips
    out_ref[:, :, width:] = proj_ref[...]
    both = dot(low_ref[...], grad_ref[...], TN).astype(bf16)
    for b in range(chips):
        out_ref[b, :, :width] = both[:, b * width : (b + 1) * width]


def first_body(info, grad_ref, *rest, base, unit, chips, count):
    pieces, (out_ref, weights, sems) = rest[:count], rest[count:]
    wait_all(qkv_weights(info, base, pieces, unit, chips, weights, sems))
    out_ref[...] = dot(grad_ref[...], weights[...], NT).astype(bf16)


def first_norm_body(
    info, grad_ref, got_ref, x_ref, res_ref, gain_ref, *rest, base, unit, chips, count
):
    pieces, (low_ref, sum_ref, weights, total, sems) = rest[:count], rest[count:]
    wait_all(qkv_weights(info, base, pieces, unit, chips, weights, sems))
    total[...] = dot(grad_ref[...], weights[...], NT)
    step = row_step(total.shape[0])
    sum_ref[...] = jnp.zeros_like(sum_ref)

    def rows(i, _):
        at = pl.ds(pl.multiple_of(i * step, 16), step)
        grad = total[at, :] + got_ref[at, :].astype(f32)
        normal, back = norm_back(x_ref[at, :].astype(f32), grad, gain_ref[...])
        back = back + res_ref[at, :]
        low_ref[at, :] = back.astype(bf16)
        sum_ref[0:1, :] += jnp.sum(grad * normal, axis=0, keepdims=True)
        sum_ref[1:2, :] += jnp.sum(grad, axis=0, keepdims=True)
        return 0

    lax.fori_loop(0, total.shape[0] // step, rows, 0)


def shards(
    tokens,
    offsets,
    first_gain,
    first_shift,
    qkv_weight,
    qv_bias,
    proj_weight,
    proj_bias,
    second_gain,
    second_shift,
    expand_weight,
    expand_bias,
    shrink_weight,
    shrink_bias,
    cotangent,
):
    token_rows, dim = tokens.shape
    sets = offsets.shape[0]
    part = qkv_weight.shape[2]
    ff = expand_weight.shape[1]
    chips = lax.axis_size("mp") // 2
    ring = Ring(lax.axis_size("dp"))
    dp_index = lax.axis_index("dp")
    mp_index = lax.axis_index("mp")
    x_index, core = mp_index // 2, mp_index % 2
    sets_x = -(-sets // chips)
    slots = sets_x * chips
    rows_x = sets_x * SET_ROWS
    half = rows_x // 2
    pairs = part // LANES
    groups = chips * pairs
    unit_rows = dim // ring.count
    unit = unit_rows // 2
    width = 3 * part
    att_width = groups * LANES
    near = [(0, 0), (0, 1)]
    far = [(step, other) for step in range(1, chips) for other in range(2)]
    keys = near + far
    sem = pltpu.SemaphoreType.DMA
    row = lambda value: value.reshape(1, -1)
    whole = lambda *dims: pl.BlockSpec(dims, lambda *_: (0,) * len(dims))

    row_starts = lax.dynamic_index_in_dim(ring.piece_rows(unit_rows), dp_index, 0, False)
    block_starts = lax.dynamic_index_in_dim(ring.block_rows(unit_rows), dp_index, 0, False)
    places = [(x_index - step) % chips * 2 + (core ^ other) for step, other in keys]
    info = jnp.concatenate(
        [jnp.stack([core, x_index, *places]).astype(jnp.int32), row_starts.astype(jnp.int32)]
    )
    place_base = 2
    base = place_base + len(keys)

    order = Order(info)

    qkv_shard = qkv_weight.astype(bf16).reshape(unit_rows, 3, pairs, LANES)
    qkv_shard = qkv_shard.transpose(0, 2, 1, 3).reshape(unit_rows, width)
    shard = jnp.concatenate([qkv_shard, proj_weight.astype(bf16).T], axis=1)
    bias_shard = jnp.zeros((pairs, 3, LANES), f32)
    bias_shard = bias_shard.at[:, 0].set(qv_bias[0].reshape(pairs, LANES))
    bias_shard = bias_shard.at[:, 2].set(qv_bias[1].reshape(pairs, LANES)).reshape(1, width)
    shards_x, bias_x = [shard], [bias_shard]
    for step in range(1, chips):
        shards_x.append(across(shard, step, chips))
        bias_x.append(across(bias_shard, step, chips))
    both_shards = jnp.stack(shards_x)
    mlp_shard = jnp.concatenate(
        [expand_weight.astype(bf16), shrink_weight.astype(bf16).T], axis=1
    )
    attn_steps = ring.gather_steps(both_shards, 1, order)
    attn_pieces, mlp_pieces = [both_shards], [mlp_shard]

    def next_step(steps, pieces):
        got = next(steps, None)
        if got is not None:
            pieces += got
        return got

    def pad_sets(value, wait):
        columns = pl.BlockSpec((token_rows, CHUNK), lambda i, _: (0, i))
        kernel = call(
            functools.partial(pad_body, sets=sets),
            (dim // CHUNK,),
            [columns],
            pl.BlockSpec((slots * SET_ROWS, CHUNK), lambda i, _: (0, i)),
            shape((slots * SET_ROWS, dim), bf16),
            [pltpu.VMEM((token_rows + 16, CHUNK), f32)],
            "pad",
        )
        return order.run(kernel, value, wait=wait)

    next_step(attn_steps, attn_pieces)
    x_rows = pad_sets(tokens, shards_x)
    next_step(attn_steps, attn_pieces)
    kernel = call(
        first_low_body,
        (sets_x,),
        [
            pl.BlockSpec((SET_ROWS, dim), lambda i, info: (info[1] * sets_x + i, 0)),
            whole(1, dim),
            whole(1, dim),
        ],
        pl.BlockSpec((SET_ROWS, dim), lambda i, _: (i, 0)),
        shape((rows_x, dim), bf16),
        [],
        "first_low",
    )
    first_low = order.run(kernel, x_rows, row(first_gain), row(first_shift), wait=attn_pieces[1:3])
    next_step(attn_steps, attn_pieces)
    starts = order.after(jnp.pad(offsets, ((0, slots - sets), (0, 0))))
    starts = lax.dynamic_slice_in_dim(starts, x_index * sets_x, sets_x, axis=0)
    positions = jnp.arange(SET_ROWS, dtype=jnp.int32)
    ids = jnp.sum((positions[None, :, None] >= starts[:, None, :]).astype(jnp.int32), axis=-1)
    ids = jnp.where(positions[None, :] < SET_TOKENS, ids, -1)
    key_ids, query_ids = ids[:, :, None], ids[:, None, :]
    cot = pad_sets(cotangent, (attn_pieces[3:5], key_ids, query_ids, mlp_shard))
    while next_step(attn_steps, attn_pieces):
        pass
    mlp_steps_first = tie(mlp_shard, attn_pieces[5:7])
    mlp_steps = ring.gather_steps(mlp_steps_first, 0, order)
    next_step(mlp_steps, mlp_pieces)
    count = len(attn_pieces)
    settings = dict(base=base, unit=unit, chips=chips, count=count)
    copies = count * chips

    kernel = call(
        functools.partial(qkv_body, **settings),
        (2,),
        [pl.BlockSpec((half, dim), lambda i, _: (i, 0)), whole(1, chips * width)] + [ANY] * count,
        pl.BlockSpec((half, chips * width), lambda i, _: (i, 0)),
        shape((rows_x, chips * width), bf16),
        [pltpu.VMEM((dim, chips * width), bf16), sem((copies,))],
        "qkv",
    )
    qkv = order.run(kernel, first_low, jnp.concatenate(bias_x, axis=1), *attn_pieces)

    def attend(first, number, before):
        kernel = call(
            attend_body,
            (number, groups),
            [
                pl.BlockSpec((SET_ROWS, 3 * LANES), lambda s, i, _: (first + s, i)),
                pl.BlockSpec((1, SET_ROWS, 1), lambda s, i, _: (first + s, 0, 0)),
                pl.BlockSpec((1, 1, SET_ROWS), lambda s, i, _: (first + s, 0, 0)),
            ]
            + [ANY] * len(before),
            [
                pl.BlockSpec((SET_ROWS, LANES), lambda s, i, _: (first + s, i)),
                pl.BlockSpec((1, 1, 2, SET_ROWS), lambda s, i, _: (first + s, i, 0, 0)),
            ],
            [
                shape((rows_x, att_width), bf16),
                shape((sets_x, groups, 2, SET_ROWS), f32),
            ],
            [pltpu.VMEM((SET_ROWS, SET_ROWS), f32)],
            "attend",
            {4 + i: i for i in range(len(before))},
        )
        return order.run(kernel, qkv, key_ids, query_ids, *before)

    begun = attend(0, 1, ())
    got = next_step(mlp_steps, mlp_pieces)
    attended, logs = attend(1, sets_x - 1, begun)

    proj_scratch = [pltpu.VMEM((dim, att_width), bf16), sem((copies,))]
    other_half = lambda *dims: pl.BlockSpec(dims, lambda i, info: (1 - info[0], 0))
    own_half = lambda *dims: pl.BlockSpec(dims, lambda i, info: (info[0], 0))
    own_place = lambda *dims: pl.BlockSpec(dims, lambda i, info: (info[place_base], 0))
    kernel = call(
        functools.partial(proj_body, **settings),
        (1,),
        [other_half(half, att_width)] + [ANY] * count,
        whole(half, dim),
        shape((half, dim), bf16),
        proj_scratch,
        "proj_send",
    )
    sent = order.run(kernel, attended, *attn_pieces, wait=got)
    got = partner(order.after(sent), chips)
    next_step(mlp_steps, mlp_pieces)
    kernel = call(
        functools.partial(proj_norm_body, **settings),
        (1,),
        [own_half(half, att_width), own_place(half, dim), whole(half, dim)]
        + [whole(1, dim)] * 3
        + [ANY] * count,
        [whole(half, dim), whole(half, dim)],
        [shape((half, dim), f32), shape((half, dim), bf16)],
        proj_scratch,
        "proj_norm",
    )
    residual, second_low = order.run(
        kernel,
        attended,
        x_rows,
        got,
        row(proj_bias),
        row(second_gain),
        row(second_shift),
        *attn_pieces,
    )
    seconds = {(0, 0): second_low, (0, 1): partner(second_low, chips)}
    for step in range(1, chips):
        seconds[(step, 0)] = across(second_low, step, chips)
    while next_step(mlp_steps, mlp_pieces):
        pass

    def feed(group, wait=()):
        parts = len(group)
        first = keys.index(group[0])
        kernel = call(
            functools.partial(mlp_body, base=base, unit=unit, count=count, parts=parts),
            (parts,),
            [
                pl.BlockSpec((half, dim), lambda i, info: (info[place_base + first + i], 0)),
                whole(1, ff),
            ]
            + [ANY] * (count + parts),
            [pl.BlockSpec((half, ff), lambda i, _: (i, 0))] * 2
            + [pl.BlockSpec((half, dim), lambda i, _: (i, 0))] * 2
            + [whole(1, ff)],
            [shape((parts * half, ff), bf16)] * 2
            + [shape((parts * half, dim), bf16)] * 2
            + [shape((1, ff), f32)],
            [
                pltpu.VMEM((dim, ff), bf16),
                pltpu.VMEM((dim, ff), bf16),
                pltpu.VMEM((parts, half, dim), bf16),
                sem((2 * count,)),
                sem((parts,)),
            ],
            "mlp",
        )
        outs = order.run(
            kernel,
            cot,
            row(expand_bias),
            *mlp_pieces,
            *[seconds[key] for key in group],
            wait=wait,
        )
        cut = lambda value: {
            key: lax.slice_in_dim(value, i * half, (i + 1) * half) for i, key in enumerate(group)
        }
        return outs[0], outs[1], cut(outs[2]), cut(outs[3]), outs[4]

    def meet_far(parts):
        both = {}
        for step in range(1, chips):
            got = partner(parts[(step, 1)], chips).astype(f32)
            both[step] = (parts[(step, 0)].astype(f32) + got).astype(bf16)
        return both

    def spread(both, near_parts):
        terms = [near_parts[(0, 0)], partner(near_parts[(0, 1)], chips)]
        return terms + [across(both[step], chips - step, chips) for step in range(1, chips)]

    hidden_near, pre_near, back_near, out_near, sum_near = feed(near)
    for step in range(1, chips):
        seconds[(step, 0)] = order.after(seconds[(step, 0)])
        seconds[(step, 1)] = partner(seconds[(step, 0)], chips)
    hidden_far, pre_far, back_far, out_far, sum_far = feed(far)
    back_both = meet_far(back_far)
    back_terms = spread(back_both, back_near)
    expand_bias_grad = (sum_far + sum_near).reshape(ff)
    span = 2 * CHUNK
    total_rows = len(keys) * half
    kernel = call(
        functools.partial(mlp_grad_body, cot_base=place_base, parts=len(keys)),
        (2, dim // span),
        [ANY] * (5 + len(keys)),
        pl.BlockSpec((span, ff), lambda p, i, _: (i, p)),
        shape((dim, 2 * ff), bf16),
        [
            pltpu.VMEM((2, total_rows, dim), bf16),
            pltpu.VMEM((2, total_rows, ff), bf16),
            sem((2, len(keys) + 2)),
        ],
        "mlp_grad",
    )
    mlp_grad = order.run(
        kernel,
        cot,
        *[seconds[key] for key in keys],
        hidden_near,
        hidden_far,
        pre_near,
        pre_far,
        wait=back_both,
    )
    mlp_ring = ring.scatter_steps(mlp_grad, 0, block_starts, order)
    next(mlp_ring)

    step_rows = row_step(half)
    cot_rows = pl.BlockSpec(
        (step_rows, dim), lambda i, info: (info[place_base] * (half // step_rows) + i, 0)
    )
    plain_rows = pl.BlockSpec((step_rows, dim), lambda i, _: (i, 0))
    kernel = call(
        functools.partial(residual_back_body, parts=len(back_terms)),
        (half // step_rows,),
        [plain_rows, cot_rows, whole(1, dim)] + [plain_rows] * len(back_terms),
        [plain_rows, plain_rows, whole(8, dim)],
        [shape((half, dim), f32), shape((half, dim), bf16), shape((8, dim), f32)],
        [],
        "residual_back",
    )
    grad_residual, residual_low, sums_two = order.run(
        kernel, residual, cot, row(second_gain), *back_terms
    )
    low_other = partner(residual_low, chips)
    out_both = meet_far(order.after(out_far))
    out_terms = spread(out_both, out_near)
    next(mlp_ring)

    kernel = call(
        functools.partial(proj_back_body, **settings),
        (1,),
        [ANY, ANY, whole(rows_x, att_width)] + [ANY] * count,
        [whole(rows_x, att_width), whole(chips, dim, part)],
        [shape((rows_x, att_width), bf16), shape((chips, dim, part), bf16)],
        [
            pltpu.VMEM((dim, att_width), bf16),
            pltpu.VMEM((rows_x, dim), bf16),
            sem((copies,)),
            sem((2,)),
        ],
        "proj_back",
    )
    grad_attended, proj_grad = order.run(
        kernel, residual_low, low_other, attended, *attn_pieces, wait=out_both
    )

    def attend_back(first, number, before):
        kernel = call(
            attend_back_body,
            (number, sets_x),
            [
                pl.BlockSpec((SET_ROWS, 3 * LANES), lambda i, s, _: (s, first + i)),
                pl.BlockSpec((1, SET_ROWS, 1), lambda i, s, _: (s, 0, 0)),
                pl.BlockSpec((1, 1, SET_ROWS), lambda i, s, _: (s, 0, 0)),
                pl.BlockSpec((1, 1, 2, SET_ROWS), lambda i, s, _: (s, first + i, 0, 0)),
                pl.BlockSpec((SET_ROWS, LANES), lambda i, s, _: (s, first + i)),
            ]
            + [ANY] * len(before),
            [
                pl.BlockSpec((SET_ROWS, 3 * LANES), lambda i, s, _: (s, first + i)),
                pl.BlockSpec((1, 1, 3 * LANES), lambda i, s, _: (first + i, 0, 0)),
            ],
            [
                shape((rows_x, chips * width), bf16),
                shape((groups, 1, 3 * LANES), f32),
            ],
            [pltpu.VMEM((sets_x, SET_ROWS, SET_ROWS), f32)],
            "attend_back",
            {6 + i: i for i in range(len(before))},
        )
        return order.run(kernel, qkv, key_ids, query_ids, logs, grad_attended, *before)

    next(mlp_ring)
    begun = attend_back(pairs, groups - pairs, ())
    out_own = order.after(residual) + shrink_bias
    for term in order.after(out_terms):
        out_own = out_own + term.astype(f32)
    out_own = out_own.astype(bf16)
    outs = {(0, 0): out_own}
    for step in range(1, chips):
        outs[(step, 0)] = across(out_own, step, chips)
    mlp_grad = next(mlp_ring)
    grad_qkv, qkv_sums = attend_back(0, pairs, begun)
    while isinstance(mlp_grad, tuple):
        mlp_grad = next(mlp_ring)

    kernel = call(
        functools.partial(qkv_grad_body, chips=chips),
        (dim // span,),
        [
            pl.BlockSpec((rows_x, span), lambda i, _: (0, i)),
            whole(rows_x, chips * width),
            pl.BlockSpec((chips, span, part), lambda i, _: (0, i, 0)),
        ],
        pl.BlockSpec((chips, span, width + part), lambda i, _: (0, i, 0)),
        shape((chips, dim, width + part), bf16),
        [],
        "qkv_grad",
    )
    attn_grad = order.run(kernel, first_low, grad_qkv, proj_grad, wait=mlp_grad)
    attn_ring = ring.scatter_steps(attn_grad, 1, block_starts, order)
    next(attn_ring)
    first_scratch = [pltpu.VMEM((dim, chips * width), bf16)]
    kernel = call(
        functools.partial(first_body, **settings),
        (1,),
        [other_half(half, chips * width)] + [ANY] * count,
        whole(half, dim),
        shape((half, dim), bf16),
        first_scratch + [sem((copies,))],
        "first_send",
    )
    sent_first = order.run(kernel, grad_qkv, *attn_pieces)
    got_first = partner(order.after(sent_first), chips)
    next(attn_ring)
    kernel = call(
        functools.partial(first_norm_body, **settings),
        (1,),
        [
            own_half(half, chips * width),
            whole(half, dim),
            own_place(half, dim),
            whole(half, dim),
            whole(1, dim),
        ]
        + [ANY] * count,
        [whole(half, dim), whole(8, dim)],
        [shape((half, dim), bf16), shape((8, dim), f32)],
        first_scratch + [pltpu.VMEM((half, dim), f32), sem((copies,))],
        "first_norm",
    )
    tokens_low, sums_one = order.run(
        kernel, grad_qkv, got_first, x_rows, grad_residual, row(first_gain), *attn_pieces
    )

    def assemble(rows, dtype, wait=()):
        block = lambda count: pl.BlockSpec((count, CHUNK), lambda i, _: (0, i))
        kernel = call(
            functools.partial(assemble_body, base=place_base, sets=sets),
            (dim // CHUNK,),
            [block(half)] * len(keys),
            block(token_rows),
            shape((token_rows, dim), dtype),
            [
                pltpu.VMEM((slots * SET_ROWS, CHUNK), f32),
                pltpu.VMEM((token_rows + 16, CHUNK), f32),
            ],
            "assemble",
        )
        return order.run(kernel, *[rows[key] for key in keys], wait=wait)

    grads = {(0, 0): tokens_low}
    for step in range(1, chips):
        grads[(step, 0)] = across(tokens_low, step, chips)
    grads[(0, 1)] = partner(tokens_low, chips)
    for step in range(chips):
        outs[(step, 1)] = partner(order.after(outs[(step, 0)]), chips)
    next(attn_ring)
    outputs = assemble(outs, bf16)
    attn_grad = next(attn_ring)
    for step in range(1, chips):
        grads[(step, 1)] = partner(order.after(grads[(step, 0)]), chips)
    grad_tokens = assemble(grads, f32)
    while isinstance(attn_grad, tuple):
        attn_grad = next(attn_ring)
    attn_low = attn_grad.astype(bf16)
    attn_part = attn_grad[0]
    for step in range(1, chips):
        attn_part = attn_part + across(attn_low[step], chips - step, chips).astype(f32)

    shared = jnp.concatenate(
        [sums_one[0], sums_one[1], sums_two[2], sums_two[0], sums_two[1], sums_two[3]]
    )
    bias_sums = qkv_sums.reshape(chips, pairs, 3, LANES)
    bias_sums = jnp.stack([bias_sums[:, :, 0], bias_sums[:, :, 2]], axis=1).reshape(chips, 2 * part)
    bias_own = bias_sums[0]
    if chips == 2:
        got = across(jnp.concatenate([shared, bias_sums[1]]), 1, chips)
        shared = shared + got[: 6 * dim]
        bias_own = bias_own + got[6 * dim :]
    else:
        bit = 1
        while bit < chips:
            shared = shared + lax.ppermute(
                shared, "mp", [(m, m ^ (2 * bit)) for m in range(2 * chips)]
            )
            bit *= 2
        for step in range(1, chips):
            bias_own = bias_own + across(bias_sums[step], chips - step, chips)
    shared = shared + partner(shared, chips)
    small = jnp.concatenate([shared, bias_own, expand_bias_grad]).reshape(-1, LANES)
    bit = 1
    while bit < ring.count:
        small = small + lax.ppermute(small, "dp", [(r, r ^ bit) for r in range(ring.count)])
        bit *= 2
    small = small.reshape(-1)
    shared = small[: 6 * dim].reshape(6, dim)
    bias_own = small[6 * dim : 6 * dim + 2 * part].reshape(2, part)
    expand_bias_grad = small[6 * dim + 2 * part :]

    qkv_part = attn_part[:, :width].reshape(unit_rows, pairs, 3, LANES)
    qkv_part = qkv_part.transpose(0, 2, 1, 3).reshape(unit_rows, 3, part)
    return (
        outputs,
        grad_tokens,
        shared[0],
        shared[1],
        qkv_part,
        bias_own,
        attn_part[:, width:].T,
        shared[2],
        shared[3],
        shared[4],
        mlp_grad[:, :ff],
        expand_bias_grad,
        mlp_grad[:, ff:].T,
        shared[5],
    )


def solution(mesh):
    placed = (
        P("dp", None),
        P("dp", None),
        P(),
        P(),
        P("dp", None, "mp"),
        P(None, "mp"),
        P("mp", "dp"),
        P(),
        P(),
        P(),
        P("dp", "mp"),
        P("mp"),
        P("mp", "dp"),
        P(),
        P("dp", None),
    )
    return jax.shard_map(
        shards,
        mesh=mesh,
        in_specs=placed,
        out_specs=(
            P("dp", None),
            P("dp", None),
            P(),
            P(),
            P("dp", None, "mp"),
            P(None, "mp"),
            P("mp", "dp"),
            P(),
            P(),
            P(),
            P("dp", "mp"),
            P("mp"),
            P("mp", "dp"),
            P(),
        ),
        check_vma=False,
    )
```

```python
import functools

import jax
import jax.numpy as jnp
import numpy as np
from jax import lax
from jax.experimental import pallas as pl
from jax.experimental.pallas import tpu as pltpu
from jax.sharding import PartitionSpec as P

HEAD_DIM = 64
SET_TOKENS = 345
SET_ROWS = 352
LANES = 128
CHUNK = 256

norm_eps = 1e-06
masked_score = -1e30
root_half = 0.7071067811865476
density_scale = 0.3989422804014327
f32 = jnp.float32
bf16 = jnp.bfloat16
NN = (((1,), (0,)), ((), ()))
NT = (((1,), (1,)), ((), ()))
TN = (((0,), (0,)), ((), ()))
ANY = pl.BlockSpec(memory_space=pl.ANY)
HBM = pl.BlockSpec(memory_space=pltpu.HBM)


def dot(left, right, dims=NN):
    return lax.dot_general(left, right, dims, preferred_element_type=f32)


ROOM = {
    "ring_first": 4,
    "ring_add": 10,
    "ring_last": 8,
    "qkv": 20,
    "pad": 20,
    "assemble": 20,
    "first_low": 10,
    "attend": 10,
    "attend_back": 12,
    "proj_norm": 20,
    "mlp": 58,
    "mlp_grad": 58,
    "residual_back": 16,
    "qkv_grad": 20,
    "first_norm": 58,
}


def call(body, grid, in_specs, out_specs, out_shape, scratch, name, aliases=None):
    return pl.pallas_call(
        body,
        grid_spec=pltpu.PrefetchScalarGridSpec(
            num_scalar_prefetch=1,
            grid=grid,
            in_specs=in_specs,
            out_specs=out_specs,
            scratch_shapes=scratch,
        ),
        out_shape=out_shape,
        compiler_params=pltpu.CompilerParams(
            dimension_semantics=("arbitrary",) * len(grid), vmem_limit_bytes=ROOM[name] * 2**20
        ),
        cost_estimate=pl.CostEstimate(flops=1, bytes_accessed=1, transcendentals=0),
        name=name,
        input_output_aliases=aliases or {},
    )


def tie(value, *earlier):
    return lax.optimization_barrier((value, earlier))[0]


class Order:
    def __init__(self, info):
        self.info = info
        self.now = info
        self.due = ()
        self.hold = ()

    def after(self, value):
        return tie(value, self.now, self.due)

    def run(self, kernel, *values, wait=()):
        out = kernel(tie(self.info, self.now, wait, self.hold), *values)
        self.hold = ()
        self.now = out[0] if isinstance(out, (list, tuple)) else out
        return out


def shape(dims, dtype):
    return jax.ShapeDtypeStruct(tuple(dims), dtype)


def ring_order(count):
    width = 1
    while 2 * (2 * width) ** 2 <= count:
        width *= 2
    length = count // width
    if width == 1:
        return list(range(count))
    path = []
    for z in range(length):
        columns = range(1, width) if z % 2 == 0 else range(width - 1, 0, -1)
        path += [z * width + y for y in columns]
    path += [z * width for z in range(length - 1, -1, -1)]
    return path


class Ring:
    def __init__(self, count):
        self.count = count
        self.order = ring_order(count)
        self.place = {rank: i for i, rank in enumerate(self.order)}
        self.ahead = [(self.order[i], self.order[(i + 1) % count]) for i in range(count)]
        self.behind = [(self.order[i], self.order[(i - 1) % count]) for i in range(count)]

    def rank_at(self, rank, offset):
        return self.order[(self.place[rank] + offset) % self.count]

    def send_ahead(self, value):
        return lax.ppermute(value, "dp", self.ahead)

    def send_behind(self, value):
        return lax.ppermute(value, "dp", self.behind)

    def gather_steps(self, block, axis, order):
        half = block.shape[axis] // 2
        forward = backward = block
        for step in range(1, self.count // 2 + 1):
            if step == self.count // 2:
                forward = lax.slice_in_dim(forward, 0, half, axis=axis)
                backward = lax.slice_in_dim(backward, half, 2 * half, axis=axis)
            forward, backward = order.after((forward, backward))
            forward = self.send_ahead(forward)
            backward = self.send_behind(backward)
            yield forward, backward

    def piece_rows(self, rows):
        table = []
        middle = self.count // 2
        for rank in range(self.count):
            starts = [rank * rows]
            for step in range(1, middle + 1):
                ahead = self.rank_at(rank, -step) * rows
                behind = self.rank_at(rank, step) * rows
                if step == middle:
                    behind += rows // 2
                starts += [ahead, behind]
            table.append(starts)
        return np.array(table, np.int32)

    def block_ranks(self):
        middle = self.count // 2
        return np.array(
            [
                [self.rank_at(rank, d) for d in range(-middle, middle + 1)]
                for rank in range(self.count)
            ],
            np.int32,
        )

    def scatter_steps(self, whole, ranks, order):
        middle = self.count // 2
        dim, columns = whole.shape
        rows = dim // self.count
        half = rows // 2
        wide = columns
        grid = (columns // wide,)
        block = lambda d: pl.BlockSpec((rows, wide), lambda j, info: (info[ranks + middle + d], j))
        plain = lambda count: pl.BlockSpec((count, wide), lambda j, _: (0, j))
        kernel = call(
            ring_first_body,
            grid,
            [
                pl.BlockSpec((half, wide), lambda j, info: (2 * info[ranks + 2 * middle], j)),
                pl.BlockSpec((half, wide), lambda j, info: (2 * info[ranks] + 1, j)),
            ],
            [plain(half)] * 2,
            [shape((half, columns), bf16)] * 2,
            [],
            "ring_first",
        )
        forward, backward = order.run(kernel, whole, whole)
        for step in range(1, middle + 1):
            forward = self.send_ahead(order.after(forward))
            backward = self.send_behind(order.after(backward))
            yield forward, backward
            near = middle - step
            if near == 0:
                break
            kernel = call(
                ring_add_body,
                grid,
                [block(near), block(-near)] + [plain(forward.shape[0])] * 2,
                [plain(rows)] * 2,
                [shape((rows, columns), bf16)] * 2,
                [],
                "ring_add",
            )
            forward, backward = order.run(kernel, whole, whole, forward, backward)
        kernel = call(
            ring_last_body,
            grid,
            [block(0)] + [plain(rows)] * 2,
            plain(rows),
            shape((rows, columns), f32),
            [],
            "ring_last",
        )
        yield order.run(kernel, whole, forward, backward)


def across(value, step, chips):
    pairs = [
        (x * 2 + core, (x + step) % chips * 2 + core) for x in range(chips) for core in range(2)
    ]
    return lax.ppermute(value, "mp", pairs)


def partner(value, chips):
    return lax.ppermute(value, "mp", [(m, m ^ 1) for m in range(2 * chips)])


def layer_norm(values, gain, shift):
    centre = jnp.mean(values, axis=-1, keepdims=True)
    offset_rows = values - centre
    spread = jnp.mean(offset_rows * offset_rows, axis=-1, keepdims=True)
    return offset_rows * lax.rsqrt(spread + norm_eps) * gain + shift


def start_all(copies, sems):
    moves = [pltpu.make_async_copy(src, dst, sems.at[i]) for i, (src, dst) in enumerate(copies)]
    for move in moves:
        move.start()
    return moves


def wait_all(moves):
    for move in moves:
        move.wait()


def weight_copies(info, base, pieces, unit, targets):
    copies = []
    for i, piece in enumerate(pieces):
        rows = piece.shape[-2]
        place = pl.ds(pl.multiple_of(info[base + i], unit), rows)
        for source, target in targets:
            copies.append((source(piece), target(place)))
    return copies


def ring_first_body(info, ahead_ref, behind_ref, ahead_out, behind_out):
    ahead_out[...] = ahead_ref[...]
    behind_out[...] = behind_ref[...]


def ring_add_body(info, ahead_ref, behind_ref, got_ahead, got_behind, ahead_out, behind_out):
    rows, part = ahead_out.shape[0], got_ahead.shape[0]
    first, last = slice(0, part), slice(rows - part, rows)
    total = ahead_ref[first, :].astype(f32) + got_ahead[...].astype(f32)
    ahead_out[first, :] = total.astype(bf16)
    total = behind_ref[last, :].astype(f32) + got_behind[...].astype(f32)
    behind_out[last, :] = total.astype(bf16)
    if part < rows:
        ahead_out[part:, :] = ahead_ref[part:, :]
        behind_out[: rows - part, :] = behind_ref[: rows - part, :]


def ring_last_body(info, own_ref, got_ahead, got_behind, out_ref):
    both = got_ahead[...].astype(f32) + got_behind[...].astype(f32)
    out_ref[...] = own_ref[...].astype(f32) + both


def qkv_body(info, x_ref, bias_ref, *rest, base, unit, chips, count):
    pieces, (out_ref, whole_ref, weights, sems, out_sem) = rest[:count], rest[count:]
    part = weights.shape[1] // chips
    width = out_ref.shape[1] // chips
    keep = pltpu.make_async_copy(weights, whole_ref, out_sem)

    @pl.when(pl.program_id(0) == 0)
    def _():
        targets = [
            (
                lambda piece, b=b: piece.at[b],
                lambda place, b=b: weights.at[place, pl.ds(b * part, part)],
            )
            for b in range(chips)
        ]
        wait_all(start_all(weight_copies(info, base, pieces, unit, targets), sems))
        keep.start()

    def columns(b, _):
        to = pl.ds(pl.multiple_of(b * width, LANES), width)
        product = dot(x_ref[...], weights[:, pl.ds(pl.multiple_of(b * part, LANES), width)])
        out_ref[:, to] = (product + bias_ref[:, to]).astype(bf16)
        return 0

    lax.fori_loop(0, chips, columns, 0)

    @pl.when(pl.program_id(0) == pl.num_programs(0) - 1)
    def _():
        keep.wait()


def pad_body(info, in_ref, out_ref, rows, *, sets):
    total = in_ref.shape[0]
    rows[0:total, :] = in_ref[...].astype(f32)
    inside = lax.broadcasted_iota(jnp.int32, (SET_ROWS, 1), 0) < SET_TOKENS
    for g in range(out_ref.shape[0] // SET_ROWS):
        to = slice(g * SET_ROWS, (g + 1) * SET_ROWS)
        if g < sets:
            value = rows[g * SET_TOKENS : g * SET_TOKENS + SET_ROWS, :]
            out_ref[to, :] = jnp.where(inside, value, 0.0).astype(bf16)
        else:
            out_ref[to, :] = jnp.zeros((SET_ROWS, out_ref.shape[1]), bf16)


def assemble_body(info, *refs, base, sets):
    pieces, (out_ref, padded, packed) = refs[:-3], refs[-3:]
    half = pieces[0].shape[0]
    for i, piece in enumerate(pieces):
        place = pl.ds(pl.multiple_of(info[base + i] * half, 16), half)
        padded[place, :] = piece[...].astype(f32)
    target = out_ref if out_ref.dtype == f32 else packed
    for g in range(sets):
        target[g * SET_TOKENS : (g + 1) * SET_TOKENS, :] = padded[
            g * SET_ROWS : g * SET_ROWS + SET_TOKENS, :
        ]
    if out_ref.dtype != f32:
        out_ref[...] = packed[0 : out_ref.shape[0], :].astype(out_ref.dtype)


def first_low_body(info, x_ref, gain_ref, shift_ref, out_ref):
    out_ref[...] = layer_norm(x_ref[...].astype(f32), gain_ref[...], shift_ref[...]).astype(bf16)


def head_mask(head):
    lane = lax.broadcasted_iota(jnp.int32, (1, LANES), 1)
    return (lane < HEAD_DIM) if head == 0 else (lane >= HEAD_DIM)


def keep_head(value, head):
    return jnp.where(head_mask(head), value, jnp.zeros_like(value))


def attend_body(info, qkv_ref, key_ids, query_ids, out_ref, log_ref, block):
    @pl.when(pl.program_id(1) == 0)
    def _():
        block[...] = jnp.where(key_ids[0] == query_ids[0], 0.0, masked_score)

    factor = HEAD_DIM**-0.5
    query = qkv_ref[:, 0:LANES] * jnp.asarray(factor, bf16)
    key = qkv_ref[:, LANES : 2 * LANES]
    value = qkv_ref[:, 2 * LANES : 3 * LANES]
    halves = []
    for head in range(2):
        scores = dot(key, keep_head(query, head), NT) + block[...]
        peak = jnp.max(scores, axis=0, keepdims=True)
        raised = jnp.exp(scores - peak)
        total = jnp.sum(raised, axis=0, keepdims=True)
        mixed = dot(keep_head(value, head), raised.astype(bf16), TN)
        halves.append(mixed * (1.0 / total))
        log_ref[0, 0, head : head + 1, :] = peak + jnp.log(total)
    out_ref[...] = (halves[0] + halves[1]).T.astype(bf16)


def attend_back_body(info, qkv_ref, key_ids, query_ids, log_ref, *rest, first_half):
    grads = rest[:4]
    out_ref, sum_ref, block = rest[-3:]
    turn = pl.program_id(1)

    @pl.when(pl.program_id(0) == 0)
    def _():
        block[turn] = jnp.where(key_ids[0] == query_ids[0], 0.0, masked_score)

    factor = HEAD_DIM**-0.5
    query = qkv_ref[:, 0:LANES] * jnp.asarray(factor, bf16)
    key = qkv_ref[:, LANES : 2 * LANES]
    value = qkv_ref[:, 2 * LANES : 3 * LANES]
    parts = []
    for j in range(2):
        core = ((2 * turn + j) >= first_half).astype(jnp.int32)
        parts.append(jnp.where(core == info[0], grads[2 * j][...], grads[2 * j + 1][...]))
    grad = jnp.concatenate(parts, axis=0)
    grad_query = grad_key = grad_value = 0.0
    for head in range(2):
        query_one = keep_head(query, head)
        grad_one = keep_head(grad, head)
        scores = dot(key, query_one, NT) + block[turn]
        weights = jnp.exp(scores - log_ref[0, 0, head : head + 1, :])
        grad_value += dot(weights.astype(bf16), grad_one)
        grad_weights = dot(value, grad_one, NT)
        centre = jnp.sum(weights * grad_weights, axis=0, keepdims=True)
        low = (weights * (grad_weights - centre)).astype(bf16)
        grad_key += dot(low, query_one)
        grad_query += dot(keep_head(key, head), low, TN)
    grad_query = (grad_query * factor).T
    out_ref[:, 0:LANES] = grad_query.astype(bf16)
    out_ref[:, LANES : 2 * LANES] = grad_key.astype(bf16)
    out_ref[:, 2 * LANES : 3 * LANES] = grad_value.astype(bf16)

    @pl.when(turn == 0)
    def _():
        sum_ref[...] = jnp.zeros_like(sum_ref)

    sum_ref[0, :, 0:LANES] += jnp.sum(grad_query, axis=0, keepdims=True)
    sum_ref[0, :, 2 * LANES : 3 * LANES] += jnp.sum(grad_value, axis=0, keepdims=True)


def proj_moves(wholes, weights, chips, sems):
    width = weights.shape[1] // (2 * chips)
    part = wholes[0].shape[1] // chips
    copies = []
    for j, source in enumerate(wholes):
        for b in range(chips):
            columns = pl.ds((b + 1) * part - width, width)
            target = pl.ds((j * chips + b) * width, width)
            copies.append((source.at[:, columns], weights.at[:, target]))
    return [pltpu.make_async_copy(src, dst, sems.at[i]) for i, (src, dst) in enumerate(copies)]


def proj_norm_body(
    info, own_ref, got_ref, x_ref, bias_ref, gain_ref, shift_ref, *rest, chips
):
    wholes, (residual_ref, low_ref, weights, sems) = rest[:2], rest[2:]
    moves = proj_moves(wholes, weights, chips, sems)
    for move in moves:
        move.start()
    wait_all(moves)
    width = own_ref.shape[1]
    span = 2 * CHUNK

    def columns(i, _):
        at = pl.ds(pl.multiple_of(i * span, span), span)
        own_part = dot(own_ref[...], weights[at, :width], NT)
        residual_ref[:, at] = own_part + dot(got_ref[...], weights[at, width:], NT)
        return 0

    lax.fori_loop(0, residual_ref.shape[1] // span, columns, 0)
    step = row_step(residual_ref.shape[0])

    def rows(i, _):
        at = pl.ds(pl.multiple_of(i * step, 16), step)
        value = residual_ref[at, :] + x_ref[at, :].astype(f32) + bias_ref[...]
        residual_ref[at, :] = value
        low_ref[at, :] = layer_norm(value, gain_ref[...], shift_ref[...]).astype(bf16)
        return 0

    lax.fori_loop(0, residual_ref.shape[0] // step, rows, 0)


def row_step(rows):
    return 176 if rows % 176 == 0 else rows


def mlp_body(info, cot_ref, bias_ref, *rest, base, unit, count, parts, adds):
    pieces, rest = rest[:count], rest[count:]
    seconds, rest = rest[:parts], rest[parts:]
    gots, rest = rest[: 2 * adds], rest[2 * adds :]
    hidden_ref, pre_ref, rest = rest[0], rest[1], rest[2:]
    backs, outs, rest = rest[:parts], rest[parts : 2 * parts], rest[2 * parts :]
    sum_ref, expand, shrink, rows, sems, row_sems = rest
    width = expand.shape[1]
    turn = pl.program_id(0)

    @pl.when(turn == 0)
    def _():
        targets = [
            (
                lambda piece: piece.at[:, pl.ds(0, width)],
                lambda place: expand.at[place, :],
            ),
            (
                lambda piece: piece.at[:, pl.ds(width, width)],
                lambda place: shrink.at[place, :],
            ),
        ]
        moves = start_all(weight_copies(info, base, pieces, unit, targets), sems)
        start_all([(seconds[i], rows.at[i]) for i in range(parts)], row_sems)
        wait_all(moves)
        sum_ref[...] = jnp.zeros_like(sum_ref)

    pltpu.make_async_copy(seconds[0], rows.at[turn], row_sems.at[turn]).wait()
    span = 2 * CHUNK if width % (2 * CHUNK) == 0 else LANES

    def columns(i, _):
        at = pl.ds(pl.multiple_of(i * span, span), span)
        pre = dot(rows[turn], expand[:, at]) + bias_ref[:, at]
        below = 0.5 * (1.0 + lax.erf(pre * root_half))
        density = density_scale * jnp.exp(-0.5 * pre * pre)
        hidden_ref[:, at] = (pre * below).astype(bf16)
        grad = dot(cot_ref[...], shrink[:, at]) * (below + pre * density)
        sum_ref[:, at] += jnp.sum(grad, axis=0, keepdims=True)
        pre_ref[:, at] = grad.astype(bf16)
        return 0

    lax.fori_loop(0, width // span, columns, 0)

    def back(i, _):
        at = pl.ds(pl.multiple_of(i * span, span), span)
        for targets, left, right, kind in (
            (backs, pre_ref, expand, 0),
            (outs, hidden_ref, shrink, 1),
        ):
            product = dot(left[...], right[at, :], NT)
            for i in range(parts):

                @pl.when(turn == i)
                def _(i=i, targets=targets, product=product, kind=kind):
                    total = product
                    if adds:
                        total = total + gots[2 * i + kind][:, at].astype(f32)
                    targets[i][:, at] = total.astype(bf16)

        return 0

    lax.fori_loop(0, backs[0].shape[1] // span, back, 0)


def mlp_grad_body(info, cot_ref, *rest, cot_base, parts, groups):
    seconds, rest = rest[:parts], rest[parts:]
    hiddens, pres, rest = rest[:groups], rest[groups : 2 * groups], rest[2 * groups :]
    out_ref, left, right, sems = rest
    phase = pl.program_id(0)
    rows = left.shape[1] // parts
    span = out_ref.shape[0]

    def moves(index):
        pairs = []
        for i in range(parts):
            source = seconds[i]
            if index == 1:
                place = pl.multiple_of(info[cot_base + i] * rows, 16)
                source = cot_ref.at[pl.ds(place, rows)]
            pairs.append((source, left.at[index, pl.ds(i * rows, rows)]))
        start = 0
        for source in (pres, hiddens)[index]:
            pairs.append((source, right.at[index, pl.ds(start, source.shape[0])]))
            start += source.shape[0]
        return [
            pltpu.make_async_copy(src, dst, sems.at[index, i]) for i, (src, dst) in enumerate(pairs)
        ]

    @pl.when((phase == 0) & (pl.program_id(1) == 0))
    def _():
        for index in range(2):
            for move in moves(index):
                move.start()

    for index in range(2):

        @pl.when((phase == index) & (pl.program_id(1) == 0))
        def _(index=index):
            wait_all(moves(index))

    at = pl.ds(pl.multiple_of(pl.program_id(1) * span, span), span)
    out_ref[...] = dot(left[phase, :, at], right[phase], TN).astype(bf16)


def norm_back(value, grad, gain):
    centred = value - jnp.mean(value, axis=-1, keepdims=True)
    spread = jnp.mean(centred * centred, axis=-1, keepdims=True)
    scale = lax.rsqrt(spread + norm_eps)
    normal = centred * scale
    weighted = grad * gain
    middle = jnp.mean(weighted, axis=-1, keepdims=True)
    slope = jnp.mean(weighted * normal, axis=-1, keepdims=True)
    return normal, scale * (weighted - middle - normal * slope)


def residual_back_body(info, residual_ref, cot_ref, gain_ref, *rest, parts, chips):
    grads, rest = rest[:parts], rest[parts:]
    wholes, (grad_ref, low_ref, own_ref, send_ref, sum_ref, weights, sems) = rest[:2], rest[2:]
    moves = proj_moves(wholes, weights, chips, sems)

    @pl.when(pl.program_id(0) == 0)
    def _():
        for move in moves:
            move.start()
        sum_ref[...] = jnp.zeros_like(sum_ref)

    grad = grads[0][...].astype(f32)
    for other in grads[1:]:
        grad += other[...].astype(f32)
    normal, back = norm_back(residual_ref[...], grad, gain_ref[...])
    cotangent = cot_ref[...].astype(f32)
    total = cotangent + back
    grad_ref[...] = total
    low_ref[...] = total.astype(bf16)
    sum_ref[0:1, :] += jnp.sum(grad * normal, axis=0, keepdims=True)
    sum_ref[1:2, :] += jnp.sum(grad, axis=0, keepdims=True)
    sum_ref[2:3, :] += jnp.sum(total, axis=0, keepdims=True)
    sum_ref[3:4, :] += jnp.sum(cotangent, axis=0, keepdims=True)

    @pl.when(pl.program_id(0) == 0)
    def _():
        wait_all(moves)

    both = dot(low_ref[...], weights[...]).astype(bf16)
    width = own_ref.shape[1]
    own_ref[...] = both[:, :width]
    send_ref[...] = both[:, width:]


def qkv_grad_body(info, first_ref, grad_ref, own_ref, got_ref, att_own, att_got, *rest):
    out_ref = rest[-1]
    width = grad_ref.shape[1]
    out_ref[:, :width] = dot(first_ref[...], grad_ref[...], TN).astype(bf16)
    out_ref[:, width:] = (
        dot(own_ref[...], att_own[...], TN) + dot(got_ref[...], att_got[...], TN)
    ).astype(bf16)


def first_norm_body(info, *refs, chips):
    grads, (x_ref, res_ref, gain_ref, *rest) = refs[: 2 * chips], refs[2 * chips :]
    wholes, (low_ref, sum_ref, weights, lefts, total, sems) = rest[:2], rest[2:]
    half, width = lefts.shape[1:]
    part = wholes[0].shape[1] // chips

    def move(i):
        return pltpu.make_async_copy(
            wholes[i // chips].at[:, pl.ds(i % chips * part, width)], weights.at[i], sems.at[i]
        )

    for i in range(2 * chips):
        move(i).start()
    for i in range(2 * chips):
        lefts[i] = grads[i][...]
    total[...] = jnp.zeros_like(total)

    def term(i, _):
        pltpu.make_async_copy(
            wholes[0].at[:, pl.ds(0, width)], weights.at[i], sems.at[i]
        ).wait()
        total[...] += dot(lefts[i], weights[i], NT)
        return 0

    lax.fori_loop(0, 2 * chips, term, 0)
    step = row_step(total.shape[0])
    sum_ref[...] = jnp.zeros_like(sum_ref)

    def rows(i, _):
        at = pl.ds(pl.multiple_of(i * step, 16), step)
        grad = total[at, :]
        normal, back = norm_back(x_ref[at, :].astype(f32), grad, gain_ref[...])
        low_ref[at, :] = (back + res_ref[at, :]).astype(bf16)
        sum_ref[0:1, :] += jnp.sum(grad * normal, axis=0, keepdims=True)
        sum_ref[1:2, :] += jnp.sum(grad, axis=0, keepdims=True)
        return 0

    lax.fori_loop(0, total.shape[0] // step, rows, 0)


def shards(
    tokens,
    offsets,
    first_gain,
    first_shift,
    qkv_weight,
    qv_bias,
    proj_weight,
    proj_bias,
    second_gain,
    second_shift,
    expand_weight,
    expand_bias,
    shrink_weight,
    shrink_bias,
    cotangent,
):
    token_rows, dim = tokens.shape
    sets = offsets.shape[0]
    part = qkv_weight.shape[2]
    ff = expand_weight.shape[1]
    chips = lax.axis_size("mp") // 2
    ring = Ring(lax.axis_size("dp"))
    dp_index = lax.axis_index("dp")
    mp_index = lax.axis_index("mp")
    x_index, core = mp_index // 2, mp_index % 2
    sets_x = -(-sets // chips)
    slots = sets_x * chips
    rows_x = sets_x * SET_ROWS
    half = rows_x // 2
    pairs = part // LANES
    groups = chips * pairs
    unit_rows = dim // ring.count
    unit = unit_rows // 2
    width = 3 * part
    att_width = groups * LANES
    near = [(0, 0), (0, 1)]
    far_other = [(step, 1) for step in range(1, chips)]
    far_own = [(step, 0) for step in range(1, chips)]
    keys = near + far_other + far_own
    sem = pltpu.SemaphoreType.DMA
    row = lambda value: value.reshape(1, -1)
    whole = lambda *dims: pl.BlockSpec(dims, lambda *_: (0,) * len(dims))

    row_starts = lax.dynamic_index_in_dim(ring.piece_rows(unit_rows), dp_index, 0, False)
    block_ranks = lax.dynamic_index_in_dim(ring.block_ranks(), dp_index, 0, False)
    places = [(x_index - step) % chips * 2 + (core ^ other) for step, other in keys]
    info = jnp.concatenate(
        [jnp.stack([core, x_index, *places]).astype(jnp.int32), row_starts, block_ranks]
    )
    place_base = 2
    base = place_base + len(keys)
    ranks = base + ring.count + 1

    order = Order(info)

    qkv_shard = qkv_weight.astype(bf16).reshape(unit_rows, 3, pairs, LANES)
    qkv_shard = qkv_shard.transpose(0, 2, 1, 3).reshape(unit_rows, width)
    shard = jnp.concatenate([qkv_shard, proj_weight.astype(bf16).T], axis=1)
    bias_shard = jnp.zeros((pairs, 3, LANES), f32)
    bias_shard = bias_shard.at[:, 0].set(qv_bias[0].reshape(pairs, LANES))
    bias_shard = bias_shard.at[:, 2].set(qv_bias[1].reshape(pairs, LANES)).reshape(1, width)
    shards_x, bias_x = [shard], [bias_shard]
    for step in range(1, chips):
        shards_x.append(across(shard, step, chips))
        bias_x.append(across(bias_shard, step, chips))
    both_shards = jnp.stack(shards_x)
    mlp_shard = jnp.concatenate(
        [expand_weight.astype(bf16), shrink_weight.astype(bf16).T], axis=1
    )
    attn_steps = ring.gather_steps(both_shards, 1, order)
    mlp_steps = ring.gather_steps(mlp_shard, 0, order)
    attn_pieces, mlp_pieces = [both_shards], [mlp_shard]

    def next_step(steps, pieces):
        got = next(steps, None)
        if got is not None:
            pieces += got
        return got

    def pad_sets(value, wait):
        columns = pl.BlockSpec((token_rows, CHUNK), lambda i, _: (0, i))
        kernel = call(
            functools.partial(pad_body, sets=sets),
            (dim // CHUNK,),
            [columns],
            pl.BlockSpec((slots * SET_ROWS, CHUNK), lambda i, _: (0, i)),
            shape((slots * SET_ROWS, dim), bf16),
            [pltpu.VMEM((token_rows + 16, CHUNK), f32)],
            "pad",
        )
        return order.run(kernel, value, wait=wait)

    next_step(attn_steps, attn_pieces)
    x_rows = pad_sets(tokens, shards_x)
    next_step(attn_steps, attn_pieces)
    kernel = call(
        first_low_body,
        (sets_x,),
        [
            pl.BlockSpec((SET_ROWS, dim), lambda i, info: (info[1] * sets_x + i, 0)),
            whole(1, dim),
            whole(1, dim),
        ],
        pl.BlockSpec((SET_ROWS, dim), lambda i, _: (i, 0)),
        shape((rows_x, dim), bf16),
        [],
        "first_low",
    )
    first_low = order.run(kernel, x_rows, row(first_gain), row(first_shift), wait=attn_pieces[1:3])
    next_step(attn_steps, attn_pieces)
    starts = order.after(jnp.pad(offsets, ((0, slots - sets), (0, 0))))
    starts = lax.dynamic_slice_in_dim(starts, x_index * sets_x, sets_x, axis=0)
    positions = jnp.arange(SET_ROWS, dtype=jnp.int32)
    ids = jnp.sum((positions[None, :, None] >= starts[:, None, :]).astype(jnp.int32), axis=-1)
    ids = jnp.where(positions[None, :] < SET_TOKENS, ids, -1)
    key_ids, query_ids = ids[:, :, None], ids[:, None, :]
    cot = pad_sets(cotangent, (attn_pieces[3:5], key_ids, query_ids, mlp_shard))
    while next_step(attn_steps, attn_pieces):
        pass
    mlp_steps = ring.gather_steps(tie(mlp_shard, attn_pieces[-2:]), 0, order)
    next_step(mlp_steps, mlp_pieces)
    count = len(attn_pieces)
    copies = count * chips

    joint = chips * (width + part)
    kernel = call(
        functools.partial(qkv_body, base=base, unit=unit, chips=chips, count=count),
        (2,),
        [pl.BlockSpec((half, dim), lambda i, _: (i, 0)), whole(1, chips * width)] + [ANY] * count,
        [pl.BlockSpec((half, chips * width), lambda i, _: (i, 0)), HBM],
        [shape((rows_x, chips * width), bf16), shape((dim, joint), bf16)],
        [pltpu.VMEM((dim, joint), bf16), sem((copies,)), sem],
        "qkv",
    )
    qkv, weights = order.run(kernel, first_low, jnp.concatenate(bias_x, axis=1), *attn_pieces)
    order.due = mlp_pieces[-2:]
    both_weights = [weights, partner(order.after(weights), chips)]

    order.due = ()
    next_step(mlp_steps, mlp_pieces)
    kernel = call(
        attend_body,
        (sets_x, groups),
        [
            pl.BlockSpec((SET_ROWS, 3 * LANES), lambda s, i, _: (s, i)),
            pl.BlockSpec((1, SET_ROWS, 1), lambda s, i, _: (s, 0, 0)),
            pl.BlockSpec((1, 1, SET_ROWS), lambda s, i, _: (s, 0, 0)),
        ],
        [
            pl.BlockSpec((SET_ROWS, LANES), lambda s, i, _: (s, i)),
            pl.BlockSpec((1, 1, 2, SET_ROWS), lambda s, i, _: (s, i, 0, 0)),
        ],
        [
            shape((rows_x, att_width), bf16),
            shape((sets_x, groups, 2, SET_ROWS), f32),
        ],
        [pltpu.VMEM((SET_ROWS, SET_ROWS), f32)],
        "attend",
    )
    attended, logs = order.run(kernel, qkv, key_ids, query_ids)
    order.due = [*mlp_pieces[-2:], both_weights[1]]
    attended_other = partner(order.after(attended), chips)
    order.due = ()
    next_step(mlp_steps, mlp_pieces)

    own_half = lambda *dims: pl.BlockSpec(dims, lambda i, info: (info[0], 0))
    own_place = lambda *dims: pl.BlockSpec(dims, lambda i, info: (info[place_base], 0))
    proj_scratch = [pltpu.VMEM((dim, 2 * att_width), bf16), sem((2 * chips,))]
    kernel = call(
        functools.partial(proj_norm_body, chips=chips),
        (1,),
        [own_half(half, att_width)] * 2 + [own_place(half, dim)] + [whole(1, dim)] * 3 + [HBM] * 2,
        [whole(half, dim), whole(half, dim)],
        [shape((half, dim), f32), shape((half, dim), bf16)],
        proj_scratch,
        "proj_norm",
    )
    residual, second_low = order.run(
        kernel,
        attended,
        attended_other,
        x_rows,
        row(proj_bias),
        row(second_gain),
        row(second_shift),
        *both_weights,
    )
    order.due = mlp_pieces[-2:]
    second_low = order.after(second_low)
    order.due = ()
    seconds = {(0, 0): second_low, (0, 1): partner(second_low, chips)}
    for step in range(1, chips):
        seconds[(step, 0)] = across(second_low, step, chips)
    while next_step(mlp_steps, mlp_pieces):
        pass

    def feed(group, gots=()):
        parts = len(group)
        first = keys.index(group[0])
        kernel = call(
            functools.partial(
                mlp_body, base=base, unit=unit, count=count, parts=parts, adds=len(gots) // 2
            ),
            (parts,),
            [
                pl.BlockSpec((half, dim), lambda i, info: (info[place_base + first + i], 0)),
                whole(1, ff),
            ]
            + [HBM] * (count + parts)
            + [whole(half, dim)] * len(gots),
            [pl.BlockSpec((half, ff), lambda i, _: (i, 0))] * 2
            + [whole(half, dim)] * (2 * parts)
            + [whole(1, ff)],
            [shape((parts * half, ff), bf16)] * 2
            + [shape((half, dim), bf16)] * (2 * parts)
            + [shape((1, ff), f32)],
            [
                pltpu.VMEM((dim, ff), bf16),
                pltpu.VMEM((dim, ff), bf16),
                pltpu.VMEM((parts, half, dim), bf16),
                sem((2 * count,)),
                sem((parts,)),
            ],
            "mlp",
        )
        outs = order.run(
            kernel,
            cot,
            row(expand_bias),
            *mlp_pieces,
            *[seconds[key] for key in group],
            *gots,
        )
        backs, rows = outs[2 : 2 + parts], outs[2 + parts : 2 + 2 * parts]
        return outs[0], outs[1], list(backs), list(rows), outs[-1]

    first = feed(near)
    for step in range(1, chips):
        seconds[(step, 1)] = partner(order.after(seconds[(step, 0)]), chips)
    other = feed(far_other)
    gots = []
    for back, out in zip(other[2], other[3]):
        gots += [partner(back, chips), partner(out, chips)]
    own = feed(far_own, gots)
    feeds = [first, other, own]

    def along_x(own, sums):
        terms = [own[0], partner(own[1], chips)]
        return terms + [across(value, chips - 1 - i, chips) for i, value in enumerate(sums)]

    back_terms = along_x(first[2], own[2])
    expand_bias_grad = (first[4] + other[4] + own[4]).reshape(ff)
    span = 2 * CHUNK
    total_rows = len(keys) * half
    kernel = call(
        functools.partial(mlp_grad_body, cot_base=place_base, parts=len(keys), groups=3),
        (2, dim // span),
        [HBM] * (7 + len(keys)),
        pl.BlockSpec((span, ff), lambda p, i, _: (i, p)),
        shape((dim, 2 * ff), bf16),
        [
            pltpu.VMEM((2, total_rows, dim), bf16),
            pltpu.VMEM((2, total_rows, ff), bf16),
            sem((2, len(keys) + 3)),
        ],
        "mlp_grad",
    )
    mlp_grad = order.run(
        kernel,
        cot,
        *[seconds[key] for key in keys],
        *[outs[0] for outs in feeds],
        *[outs[1] for outs in feeds],
    )
    mlp_ring = ring.scatter_steps(mlp_grad, ranks, order)
    mlp_due = next(mlp_ring)

    step_rows = row_step(half)
    cot_rows = pl.BlockSpec(
        (step_rows, dim), lambda i, info: (info[place_base] * (half // step_rows) + i, 0)
    )
    plain_rows = lambda count: pl.BlockSpec((step_rows, count), lambda i, _: (i, 0))
    kernel = call(
        functools.partial(residual_back_body, parts=len(back_terms), chips=chips),
        (half // step_rows,),
        [plain_rows(dim), cot_rows, whole(1, dim)]
        + [plain_rows(dim)] * len(back_terms)
        + [HBM] * 2,
        [plain_rows(dim)] * 2 + [plain_rows(att_width)] * 2 + [whole(8, dim)],
        [
            shape((half, dim), f32),
            shape((half, dim), bf16),
            shape((half, att_width), bf16),
            shape((half, att_width), bf16),
            shape((8, dim), f32),
        ],
        proj_scratch,
        "residual_back",
    )
    grad_residual, residual_low, grad_own, grad_send, sums_two = order.run(
        kernel, residual, cot, row(second_gain), *back_terms, *both_weights
    )
    order.due = mlp_due
    grad_got = partner(order.after(grad_send), chips)
    residual_other = partner(order.after(residual_low), chips)
    order.due = ()
    mlp_due = next(mlp_ring)
    if chips == 2:
        out_near = order.after(residual) + shrink_bias + first[3][0].astype(f32)
        out_near = (out_near + partner(order.after(first[3][1]), chips).astype(f32)).astype(bf16)
        out_far = own[3][0]
        cut = half // 2
        out_sends = iter([out_far[:cut], out_far[cut:], out_near[:cut], out_near[cut:]])
        out_gots = [across(order.after(next(out_sends)), 1, chips)]
    else:
        out_terms = along_x(order.after(first[3]), order.after(own[3]))

    def attend_back(b):
        half_block = lambda j: pl.BlockSpec(
            (row_step(half), LANES), lambda i, s, _: (lax.rem(2 * s + j, sets_x), b * pairs + i)
        )
        kernel = call(
            functools.partial(attend_back_body, first_half=sets_x),
            (pairs, sets_x),
            [
                pl.BlockSpec((SET_ROWS, 3 * LANES), lambda i, s, _: (s, b * pairs + i)),
                pl.BlockSpec((1, SET_ROWS, 1), lambda i, s, _: (s, 0, 0)),
                pl.BlockSpec((1, 1, SET_ROWS), lambda i, s, _: (s, 0, 0)),
                pl.BlockSpec((1, 1, 2, SET_ROWS), lambda i, s, _: (s, b * pairs + i, 0, 0)),
                half_block(0),
                half_block(0),
                half_block(1),
                half_block(1),
            ],
            [
                pl.BlockSpec((SET_ROWS, 3 * LANES), lambda i, s, _: (s, i)),
                pl.BlockSpec((1, 1, 3 * LANES), lambda i, s, _: (i, 0, 0)),
            ],
            [shape((rows_x, width), bf16), shape((pairs, 1, 3 * LANES), f32)],
            [pltpu.VMEM((sets_x, SET_ROWS, SET_ROWS), f32)],
            "attend_back",
        )
        ids = key_ids, query_ids
        return order.run(kernel, qkv, *ids, logs, grad_own, grad_got, grad_own, grad_got)

    def qkv_grad(b, before):
        columns = lambda count: pl.BlockSpec((count, span), lambda i, _: (0, i))
        kernel = call(
            qkv_grad_body,
            (dim // span,),
            [
                columns(rows_x),
                whole(rows_x, width),
                columns(half),
                columns(half),
                pl.BlockSpec((half, part), lambda i, info: (info[0], b)),
                pl.BlockSpec((half, part), lambda i, info: (1 - info[0], b)),
            ]
            + [ANY] * len(before),
            pl.BlockSpec((span, width + part), lambda i, _: (i, b)),
            shape((dim, joint), bf16),
            [],
            "qkv_grad",
            {7 + i: i for i in range(len(before))},
        )
        return order.run(
            kernel,
            first_low,
            grads_qkv[b],
            residual_low,
            residual_other,
            attended,
            attended,
            *before,
        )

    def out_due(i):
        if chips != 2 or i > 3:
            return ()
        if i < 3:
            out_gots.append(across(order.after(next(out_sends)), 1, chips))
        return out_gots[i]

    grads_qkv, grads_other, qkv_sums, begun = {}, {}, {}, ()
    for b in range(1, chips):
        grads_qkv[b], qkv_sums[b] = attend_back(b)
        order.due = mlp_due, residual_other, out_due(b - 1)
        grads_other[b] = partner(order.after(grads_qkv[b]), chips)
        order.due = ()
        mlp_due = next(mlp_ring, ())
        begun = (qkv_grad(b, begun),)
    grads_qkv[0], qkv_sums[0] = attend_back(0)
    order.due = mlp_due, [grads_other[b] for b in range(1, chips)], out_due(1)
    grads_other[0] = partner(order.after(grads_qkv[0]), chips)
    order.due = ()
    mlp_due = next(mlp_ring, ())
    attn_ring = ring.scatter_steps(qkv_grad(0, begun), ranks, order)
    order.due = [grads_other[b] for b in range(chips)]
    next(attn_ring)
    order.due = ()
    for mlp_grad in mlp_ring:
        pass
    expand_part, shrink_part = mlp_grad[:, :ff], mlp_grad[:, ff:].T
    order.due = out_due(2)
    attn_due = next(attn_ring)
    order.due = ()

    kernel = call(
        functools.partial(first_norm_body, chips=chips),
        (1,),
        [own_half(half, width)] * (2 * chips)
        + [own_place(half, dim), whole(half, dim), whole(1, dim)]
        + [HBM] * 2,
        [whole(half, dim), whole(8, dim)],
        [shape((half, dim), bf16), shape((8, dim), f32)],
        [
            pltpu.VMEM((2 * chips, dim, width), bf16),
            pltpu.VMEM((2 * chips, half, width), bf16),
            pltpu.VMEM((half, dim), f32),
            sem((2 * chips,)),
        ],
        "first_norm",
    )
    tokens_low, sums_one = order.run(
        kernel,
        *[grads_qkv[b] for b in range(chips)],
        *[grads_other[b] for b in range(chips)],
        x_rows,
        grad_residual,
        row(first_gain),
        *both_weights,
    )

    def assemble(rows, dtype):
        block = lambda count, at: pl.BlockSpec((count, CHUNK), lambda i, _: (at, i))
        kernel = call(
            functools.partial(assemble_body, base=place_base, sets=sets),
            (dim // CHUNK,),
            [block(half, rows[key][1]) for key in keys],
            block(token_rows, 0),
            shape((token_rows, dim), dtype),
            [
                pltpu.VMEM((slots * SET_ROWS, CHUNK), f32),
                pltpu.VMEM((token_rows + 16, CHUNK), f32),
            ],
            "assemble",
        )
        return order.run(kernel, *[rows[key][0] for key in keys])

    order.due = attn_due, out_due(3)
    tokens_low = order.after(tokens_low)
    order.due = ()
    grads, outs = {(0, 0): (tokens_low, 0)}, {}
    for step in range(1, chips):
        grads[(step, 0)] = across(tokens_low, step, chips), 0
    next(attn_ring)
    if chips == 2:
        out_rows = jnp.concatenate([out_near, out_far]).astype(f32)
        out_rows = out_rows + jnp.concatenate(order.after(out_gots)).astype(f32)
    else:
        out_rows = order.after(residual) + shrink_bias
        for term in out_terms:
            out_rows = out_rows + term.astype(f32)
        low = out_rows.astype(bf16)
        out_rows = jnp.concatenate([low] + [across(low, step, chips) for step in range(1, chips)])
    out_rows = out_rows.astype(bf16)
    out_other = partner(out_rows, chips)
    for step in range(chips):
        outs[(step, 0)], outs[(step, 1)] = (out_rows, step), (out_other, step)

    bias_sums = jnp.stack([qkv_sums[b] for b in range(chips)]).reshape(chips, pairs, 3, LANES)
    bias_sums = jnp.stack([bias_sums[:, :, 0], bias_sums[:, :, 2]], axis=1)
    hidden_sums = jnp.pad(expand_bias_grad, (0, -ff % dim)).reshape(-1, dim)
    shared = jnp.concatenate([sums_one[0:2], sums_two[2:3], sums_two[0:2], sums_two[3:4]])
    shared = shared + partner(shared, chips)
    small = jnp.concatenate([shared, bias_sums.reshape(-1, dim), hidden_sums])
    bits = [1 << i for i in range(ring.count.bit_length() - 1)]

    def add_ranks(small, bit):
        pairs = [(r, r ^ bit) for r in range(ring.count)]
        return small + lax.ppermute(order.after(small), "dp", pairs)

    def add_chips(small):
        shared = small[:6]
        own, *others = small[6:7].reshape(chips, 2 * part)
        if chips == 2:
            sent = jnp.concatenate([shared.reshape(-1), others[0]])
            got = across(order.after(sent), 1, chips)
            shared = shared + got[: 6 * dim].reshape(6, dim)
            own = own + got[6 * dim :]
        else:
            bit = 1
            while bit < chips:
                flips = [(m, m ^ (2 * bit)) for m in range(2 * chips)]
                shared = shared + lax.ppermute(shared, "mp", flips)
                bit *= 2
            for step in range(1, chips):
                own = own + across(others[step - 1], chips - step, chips)
        own = jnp.pad(own, (0, dim - 2 * part)).reshape(1, dim)
        return jnp.concatenate([shared, own, small[7:]])

    outputs = assemble(outs, bf16)
    small = add_ranks(small, bits[0])
    order.hold = (small, expand_part, shrink_part)
    next(attn_ring)
    grads[(0, 1)] = partner(order.after(tokens_low), chips), 0
    for step in range(1, chips):
        grads[(step, 1)] = partner(order.after(grads[(step, 0)][0]), chips), 0
    small = add_chips(small)
    grad_tokens = assemble(grads, f32)
    for attn_sum in attn_ring:
        pass
    for bit in bits[1:]:
        small = add_ranks(small, bit)
    shared = small[:6]
    bias_own = small[6, : 2 * part].reshape(2, part)
    expand_bias_grad = small[7:].reshape(-1)[:ff]
    attn_part = attn_sum[:, : width + part]
    for step in range(1, chips):
        sent = attn_sum[:, step * (width + part) : (step + 1) * (width + part)].astype(bf16)
        attn_part = attn_part + across(sent, chips - step, chips).astype(f32)

    qkv_part = attn_part[:, :width].reshape(unit_rows, pairs, 3, LANES)
    qkv_part = qkv_part.transpose(0, 2, 1, 3).reshape(unit_rows, 3, part)
    return (
        outputs,
        grad_tokens,
        shared[0],
        shared[1],
        qkv_part,
        bias_own,
        attn_part[:, width:].T,
        shared[2],
        shared[3],
        shared[4],
        expand_part,
        expand_bias_grad,
        shrink_part,
        shared[5],
    )


def solution(mesh):
    placed = (
        P("dp", None),
        P("dp", None),
        P(),
        P(),
        P("dp", None, "mp"),
        P(None, "mp"),
        P("mp", "dp"),
        P(),
        P(),
        P(),
        P("dp", "mp"),
        P("mp"),
        P("mp", "dp"),
        P(),
        P("dp", None),
    )
    return jax.shard_map(
        shards,
        mesh=mesh,
        in_specs=placed,
        out_specs=(
            P("dp", None),
            P("dp", None),
            P(),
            P(),
            P("dp", None, "mp"),
            P(None, "mp"),
            P("mp", "dp"),
            P(),
            P(),
            P(),
            P("dp", "mp"),
            P("mp"),
            P("mp", "dp"),
            P(),
        ),
        check_vma=False,
    )
```

```python
import functools

import jax
import jax.numpy as jnp
import numpy as np
from jax import lax
from jax.experimental import pallas as pl
from jax.experimental.pallas import tpu as pltpu
from jax.sharding import PartitionSpec as P

HEAD_DIM = 64
SET_TOKENS = 345
SET_ROWS = 352
LANES = 128
CHUNK = 256

norm_eps = 1e-06
masked_score = -1e30
root_half = 0.7071067811865476
density_scale = 0.3989422804014327
f32 = jnp.float32
bf16 = jnp.bfloat16
NN = (((1,), (0,)), ((), ()))
NT = (((1,), (1,)), ((), ()))
TN = (((0,), (0,)), ((), ()))
ANY = pl.BlockSpec(memory_space=pl.ANY)
HBM = pl.BlockSpec(memory_space=pltpu.HBM)


def dot(left, right, dims=NN):
    return lax.dot_general(left, right, dims, preferred_element_type=f32)


ROOM = {
    "ring_first": 4,
    "ring_add": 10,
    "ring_last": 8,
    "qkv": 20,
    "pad": 20,
    "assemble": 20,
    "first_low": 10,
    "attend": 10,
    "attend_back": 12,
    "proj_norm": 20,
    "mlp": 58,
    "mlp_grad": 58,
    "residual_back": 16,
    "qkv_grad": 20,
    "first_norm": 58,
}


def call(body, grid, in_specs, out_specs, out_shape, scratch, name, aliases=None):
    return pl.pallas_call(
        body,
        grid_spec=pltpu.PrefetchScalarGridSpec(
            num_scalar_prefetch=1,
            grid=grid,
            in_specs=in_specs,
            out_specs=out_specs,
            scratch_shapes=scratch,
        ),
        out_shape=out_shape,
        compiler_params=pltpu.CompilerParams(
            dimension_semantics=("arbitrary",) * len(grid), vmem_limit_bytes=ROOM[name] * 2**20
        ),
        cost_estimate=pl.CostEstimate(flops=1, bytes_accessed=1, transcendentals=0),
        name=name,
        input_output_aliases=aliases or {},
    )


def tie(value, *earlier):
    return lax.optimization_barrier((value, earlier))[0]


class Order:
    def __init__(self, info):
        self.info = info
        self.now = info
        self.due = ()
        self.hold = ()

    def after(self, value):
        return tie(value, self.now, self.due)

    def run(self, kernel, *values, wait=()):
        out = kernel(tie(self.info, self.now, wait, self.hold), *values)
        self.hold = ()
        self.now = out[0] if isinstance(out, (list, tuple)) else out
        return out


def shape(dims, dtype):
    return jax.ShapeDtypeStruct(tuple(dims), dtype)


def ring_order(count):
    width = 1
    while 2 * (2 * width) ** 2 <= count:
        width *= 2
    length = count // width
    if width == 1:
        return list(range(count))
    path = []
    for z in range(length):
        columns = range(1, width) if z % 2 == 0 else range(width - 1, 0, -1)
        path += [z * width + y for y in columns]
    path += [z * width for z in range(length - 1, -1, -1)]
    return path


class Ring:
    def __init__(self, count):
        self.count = count
        self.order = ring_order(count)
        self.place = {rank: i for i, rank in enumerate(self.order)}
        self.ahead = [(self.order[i], self.order[(i + 1) % count]) for i in range(count)]
        self.behind = [(self.order[i], self.order[(i - 1) % count]) for i in range(count)]

    def rank_at(self, rank, offset):
        return self.order[(self.place[rank] + offset) % self.count]

    def send_ahead(self, value):
        return lax.ppermute(value, "dp", self.ahead)

    def send_behind(self, value):
        return lax.ppermute(value, "dp", self.behind)

    def gather_steps(self, block, axis, order):
        half = block.shape[axis] // 2
        forward = backward = block
        for step in range(1, self.count // 2 + 1):
            if step == self.count // 2:
                forward = lax.slice_in_dim(forward, 0, half, axis=axis)
                backward = lax.slice_in_dim(backward, half, 2 * half, axis=axis)
            forward, backward = order.after((forward, backward))
            forward = self.send_ahead(forward)
            backward = self.send_behind(backward)
            yield forward, backward

    def piece_rows(self, rows):
        table = []
        middle = self.count // 2
        for rank in range(self.count):
            starts = [rank * rows]
            for step in range(1, middle + 1):
                ahead = self.rank_at(rank, -step) * rows
                behind = self.rank_at(rank, step) * rows
                if step == middle:
                    behind += rows // 2
                starts += [ahead, behind]
            table.append(starts)
        return np.array(table, np.int32)

    def block_ranks(self):
        middle = self.count // 2
        return np.array(
            [
                [self.rank_at(rank, d) for d in range(-middle, middle + 1)]
                for rank in range(self.count)
            ],
            np.int32,
        )

    def scatter_steps(self, whole, ranks, order):
        middle = self.count // 2
        dim, columns = whole.shape
        rows = dim // self.count
        half = rows // 2
        wide = columns
        grid = (columns // wide,)
        block = lambda d: pl.BlockSpec((rows, wide), lambda j, info: (info[ranks + middle + d], j))
        plain = lambda count: pl.BlockSpec((count, wide), lambda j, _: (0, j))
        kernel = call(
            ring_first_body,
            grid,
            [
                pl.BlockSpec((half, wide), lambda j, info: (2 * info[ranks + 2 * middle], j)),
                pl.BlockSpec((half, wide), lambda j, info: (2 * info[ranks] + 1, j)),
            ],
            [plain(half)] * 2,
            [shape((half, columns), bf16)] * 2,
            [],
            "ring_first",
        )
        forward, backward = order.run(kernel, whole, whole)
        for step in range(1, middle + 1):
            forward = self.send_ahead(order.after(forward))
            backward = self.send_behind(order.after(backward))
            yield forward, backward
            near = middle - step
            if near == 0:
                break
            kernel = call(
                ring_add_body,
                grid,
                [block(near), block(-near)] + [plain(forward.shape[0])] * 2,
                [plain(rows)] * 2,
                [shape((rows, columns), bf16)] * 2,
                [],
                "ring_add",
            )
            forward, backward = order.run(kernel, whole, whole, forward, backward)
        kernel = call(
            ring_last_body,
            grid,
            [block(0)] + [plain(rows)] * 2,
            plain(rows),
            shape((rows, columns), f32),
            [],
            "ring_last",
        )
        yield order.run(kernel, whole, forward, backward)


def across(value, step, chips):
    pairs = [
        (x * 2 + core, (x + step) % chips * 2 + core) for x in range(chips) for core in range(2)
    ]
    return lax.ppermute(value, "mp", pairs)


def partner(value, chips):
    return lax.ppermute(value, "mp", [(m, m ^ 1) for m in range(2 * chips)])


def layer_norm(values, gain, shift):
    centre = jnp.mean(values, axis=-1, keepdims=True)
    offset_rows = values - centre
    spread = jnp.mean(offset_rows * offset_rows, axis=-1, keepdims=True)
    return offset_rows * lax.rsqrt(spread + norm_eps) * gain + shift


def start_all(copies, sems):
    moves = [pltpu.make_async_copy(src, dst, sems.at[i]) for i, (src, dst) in enumerate(copies)]
    for move in moves:
        move.start()
    return moves


def wait_all(moves):
    for move in moves:
        move.wait()


def weight_copies(info, base, pieces, unit, targets):
    copies = []
    for i, piece in enumerate(pieces):
        rows = piece.shape[-2]
        place = pl.ds(pl.multiple_of(info[base + i], unit), rows)
        for source, target in targets:
            copies.append((source(piece), target(place)))
    return copies


def ring_first_body(info, ahead_ref, behind_ref, ahead_out, behind_out):
    ahead_out[...] = ahead_ref[...]
    behind_out[...] = behind_ref[...]


def ring_add_body(info, ahead_ref, behind_ref, got_ahead, got_behind, ahead_out, behind_out):
    rows, part = ahead_out.shape[0], got_ahead.shape[0]
    first, last = slice(0, part), slice(rows - part, rows)
    total = ahead_ref[first, :].astype(f32) + got_ahead[...].astype(f32)
    ahead_out[first, :] = total.astype(bf16)
    total = behind_ref[last, :].astype(f32) + got_behind[...].astype(f32)
    behind_out[last, :] = total.astype(bf16)
    if part < rows:
        ahead_out[part:, :] = ahead_ref[part:, :]
        behind_out[: rows - part, :] = behind_ref[: rows - part, :]


def ring_last_body(info, own_ref, got_ahead, got_behind, out_ref):
    both = got_ahead[...].astype(f32) + got_behind[...].astype(f32)
    out_ref[...] = own_ref[...].astype(f32) + both


def qkv_body(info, x_ref, bias_ref, *rest, base, unit, chips, count):
    steps = count // 2 + 1
    own, rest = rest[:count], rest[count:]
    far, (out_ref, whole_ref, weights, sems, out_sem) = (
        rest[: steps * (chips - 1)],
        rest[steps * (chips - 1) :],
    )
    part = weights.shape[1] // chips
    width = out_ref.shape[1] // chips
    keep = pltpu.make_async_copy(weights, whole_ref, out_sem)

    @pl.when(pl.program_id(0) == 0)
    def _():
        copies = []
        for b in range(chips):
            for i, piece in enumerate(own):
                rows = piece.shape[0]
                source = piece
                if b:
                    joined = far[(b - 1) * steps + (i + 1) // 2]
                    source = joined.at[pl.ds(rows if i and i % 2 == 0 else 0, rows)]
                place = pl.ds(pl.multiple_of(info[base + i], unit), rows)
                copies.append((source, weights.at[place, pl.ds(b * part, part)]))
        wait_all(start_all(copies, sems))
        keep.start()

    def columns(b, _):
        to = pl.ds(pl.multiple_of(b * width, LANES), width)
        product = dot(x_ref[...], weights[:, pl.ds(pl.multiple_of(b * part, LANES), width)])
        out_ref[:, to] = (product + bias_ref[:, to]).astype(bf16)
        return 0

    lax.fori_loop(0, chips, columns, 0)

    @pl.when(pl.program_id(0) == pl.num_programs(0) - 1)
    def _():
        keep.wait()


def pad_body(info, in_ref, out_ref, rows, *, sets):
    total = in_ref.shape[0]
    rows[0:total, :] = in_ref[...].astype(f32)
    inside = lax.broadcasted_iota(jnp.int32, (SET_ROWS, 1), 0) < SET_TOKENS
    for g in range(out_ref.shape[0] // SET_ROWS):
        to = slice(g * SET_ROWS, (g + 1) * SET_ROWS)
        if g < sets:
            value = rows[g * SET_TOKENS : g * SET_TOKENS + SET_ROWS, :]
            out_ref[to, :] = jnp.where(inside, value, 0.0).astype(bf16)
        else:
            out_ref[to, :] = jnp.zeros((SET_ROWS, out_ref.shape[1]), bf16)


def assemble_body(info, *refs, base, sets):
    pieces, (out_ref, padded, packed) = refs[:-3], refs[-3:]
    half = pieces[0].shape[0]
    for i, piece in enumerate(pieces):
        place = pl.ds(pl.multiple_of(info[base + i] * half, 16), half)
        padded[place, :] = piece[...].astype(f32)
    target = out_ref if out_ref.dtype == f32 else packed
    for g in range(sets):
        target[g * SET_TOKENS : (g + 1) * SET_TOKENS, :] = padded[
            g * SET_ROWS : g * SET_ROWS + SET_TOKENS, :
        ]
    if out_ref.dtype != f32:
        out_ref[...] = packed[0 : out_ref.shape[0], :].astype(out_ref.dtype)


def first_low_body(info, x_ref, gain_ref, shift_ref, out_ref):
    out_ref[...] = layer_norm(x_ref[...].astype(f32), gain_ref[...], shift_ref[...]).astype(bf16)


def head_mask(head):
    lane = lax.broadcasted_iota(jnp.int32, (1, LANES), 1)
    return (lane < HEAD_DIM) if head == 0 else (lane >= HEAD_DIM)


def keep_head(value, head):
    return jnp.where(head_mask(head), value, jnp.zeros_like(value))


def attend_body(info, qkv_ref, key_ids, query_ids, out_ref, log_ref, block):
    @pl.when(pl.program_id(1) == 0)
    def _():
        block[...] = jnp.where(key_ids[0] == query_ids[0], 0.0, masked_score)

    factor = HEAD_DIM**-0.5
    query = qkv_ref[:, 0:LANES] * jnp.asarray(factor, bf16)
    key = qkv_ref[:, LANES : 2 * LANES]
    value = qkv_ref[:, 2 * LANES : 3 * LANES]
    halves = []
    for head in range(2):
        scores = dot(key, keep_head(query, head), NT) + block[...]
        peak = jnp.max(scores, axis=0, keepdims=True)
        raised = jnp.exp(scores - peak)
        total = jnp.sum(raised, axis=0, keepdims=True)
        mixed = dot(keep_head(value, head), raised.astype(bf16), TN)
        halves.append(mixed * (1.0 / total))
        log_ref[0, 0, head : head + 1, :] = peak + jnp.log(total)
    out_ref[...] = (halves[0] + halves[1]).T.astype(bf16)


def attend_back_body(info, qkv_ref, key_ids, query_ids, log_ref, *rest, first_half):
    grads = rest[:4]
    out_ref, sum_ref, block = rest[-3:]
    turn = pl.program_id(1)

    @pl.when(pl.program_id(0) == 0)
    def _():
        block[turn] = jnp.where(key_ids[0] == query_ids[0], 0.0, masked_score)

    factor = HEAD_DIM**-0.5
    query = qkv_ref[:, 0:LANES] * jnp.asarray(factor, bf16)
    key = qkv_ref[:, LANES : 2 * LANES]
    value = qkv_ref[:, 2 * LANES : 3 * LANES]
    parts = []
    for j in range(2):
        core = ((2 * turn + j) >= first_half).astype(jnp.int32)
        parts.append(jnp.where(core == info[0], grads[2 * j][...], grads[2 * j + 1][...]))
    grad = jnp.concatenate(parts, axis=0)
    grad_query = grad_key = grad_value = 0.0
    for head in range(2):
        query_one = keep_head(query, head)
        grad_one = keep_head(grad, head)
        scores = dot(key, query_one, NT) + block[turn]
        weights = jnp.exp(scores - log_ref[0, 0, head : head + 1, :])
        grad_value += dot(weights.astype(bf16), grad_one)
        grad_weights = dot(value, grad_one, NT)
        centre = jnp.sum(weights * grad_weights, axis=0, keepdims=True)
        low = (weights * (grad_weights - centre)).astype(bf16)
        grad_key += dot(low, query_one)
        grad_query += dot(keep_head(key, head), low, TN)
    grad_query = (grad_query * factor).T
    out_ref[:, 0:LANES] = grad_query.astype(bf16)
    out_ref[:, LANES : 2 * LANES] = grad_key.astype(bf16)
    out_ref[:, 2 * LANES : 3 * LANES] = grad_value.astype(bf16)

    @pl.when(turn == 0)
    def _():
        sum_ref[...] = jnp.zeros_like(sum_ref)

    sum_ref[0, :, 0:LANES] += jnp.sum(grad_query, axis=0, keepdims=True)
    sum_ref[0, :, 2 * LANES : 3 * LANES] += jnp.sum(grad_value, axis=0, keepdims=True)


def proj_moves(wholes, weights, chips, sems):
    width = weights.shape[1] // (2 * chips)
    part = wholes[0].shape[1] // chips
    copies = []
    for j, source in enumerate(wholes):
        for b in range(chips):
            columns = pl.ds((b + 1) * part - width, width)
            target = pl.ds((j * chips + b) * width, width)
            copies.append((source.at[:, columns], weights.at[:, target]))
    return [pltpu.make_async_copy(src, dst, sems.at[i]) for i, (src, dst) in enumerate(copies)]


def proj_norm_body(
    info, own_ref, got_ref, x_ref, bias_ref, gain_ref, shift_ref, *rest, chips
):
    wholes, (residual_ref, low_ref, weights, sems) = rest[:2], rest[2:]
    moves = proj_moves(wholes, weights, chips, sems)
    for move in moves:
        move.start()
    wait_all(moves)
    width = own_ref.shape[1]
    span = 2 * CHUNK

    def columns(i, _):
        at = pl.ds(pl.multiple_of(i * span, span), span)
        own_part = dot(own_ref[...], weights[at, :width], NT)
        residual_ref[:, at] = own_part + dot(got_ref[...], weights[at, width:], NT)
        return 0

    lax.fori_loop(0, residual_ref.shape[1] // span, columns, 0)
    step = row_step(residual_ref.shape[0])

    def rows(i, _):
        at = pl.ds(pl.multiple_of(i * step, 16), step)
        value = residual_ref[at, :] + x_ref[at, :].astype(f32) + bias_ref[...]
        residual_ref[at, :] = value
        low_ref[at, :] = layer_norm(value, gain_ref[...], shift_ref[...]).astype(bf16)
        return 0

    lax.fori_loop(0, residual_ref.shape[0] // step, rows, 0)


def row_step(rows):
    return 176 if rows % 176 == 0 else rows


def mlp_body(info, cot_ref, bias_ref, *rest, base, unit, count, parts, adds):
    pieces, rest = rest[:count], rest[count:]
    seconds, rest = rest[:parts], rest[parts:]
    gots, rest = rest[:adds], rest[adds:]
    hidden_ref, pre_ref, rest = rest[0], rest[1], rest[2:]
    backs, outs, rest = rest[:parts], rest[parts : 2 * parts], rest[2 * parts :]
    sum_ref, expand, shrink, rows, sems, row_sems = rest
    width = expand.shape[1]
    turn = pl.program_id(0)

    @pl.when(turn == 0)
    def _():
        targets = [
            (
                lambda piece: piece.at[:, pl.ds(0, width)],
                lambda place: expand.at[place, :],
            ),
            (
                lambda piece: piece.at[:, pl.ds(width, width)],
                lambda place: shrink.at[place, :],
            ),
        ]
        moves = start_all(weight_copies(info, base, pieces, unit, targets), sems)
        start_all([(seconds[i], rows.at[i]) for i in range(parts)], row_sems)
        wait_all(moves)
        sum_ref[...] = jnp.zeros_like(sum_ref)

    pltpu.make_async_copy(seconds[0], rows.at[turn], row_sems.at[turn]).wait()
    span = 2 * CHUNK if width % (2 * CHUNK) == 0 else LANES

    def columns(i, _):
        at = pl.ds(pl.multiple_of(i * span, span), span)
        pre = dot(rows[turn], expand[:, at]) + bias_ref[:, at]
        below = 0.5 * (1.0 + lax.erf(pre * root_half))
        density = density_scale * jnp.exp(-0.5 * pre * pre)
        hidden_ref[:, at] = (pre * below).astype(bf16)
        grad = dot(cot_ref[...], shrink[:, at]) * (below + pre * density)
        sum_ref[:, at] += jnp.sum(grad, axis=0, keepdims=True)
        pre_ref[:, at] = grad.astype(bf16)
        return 0

    lax.fori_loop(0, width // span, columns, 0)

    def back(i, _):
        at = pl.ds(pl.multiple_of(i * span, span), span)
        for targets, left, right, kind in (
            (backs, pre_ref, expand, 0),
            (outs, hidden_ref, shrink, 1),
        ):
            product = dot(left[...], right[at, :], NT)
            for i in range(parts):

                @pl.when(turn == i)
                def _(i=i, targets=targets, product=product, kind=kind):
                    total = product
                    if adds and kind == 0:
                        total = total + gots[i][:, at].astype(f32)
                    targets[i][:, at] = total.astype(bf16)

        return 0

    lax.fori_loop(0, backs[0].shape[1] // span, back, 0)


def mlp_grad_body(info, cot_ref, *rest, cot_base, parts, groups):
    seconds, rest = rest[:parts], rest[parts:]
    hiddens, pres, rest = rest[:groups], rest[groups : 2 * groups], rest[2 * groups :]
    out_ref, left, right, sems = rest
    phase = pl.program_id(0)
    rows = left.shape[1] // parts
    span = out_ref.shape[0]

    def moves(index):
        pairs = []
        for i in range(parts):
            source = seconds[i]
            if index == 1:
                place = pl.multiple_of(info[cot_base + i] * rows, 16)
                source = cot_ref.at[pl.ds(place, rows)]
            pairs.append((source, left.at[index, pl.ds(i * rows, rows)]))
        start = 0
        for source in (pres, hiddens)[index]:
            pairs.append((source, right.at[index, pl.ds(start, source.shape[0])]))
            start += source.shape[0]
        return [
            pltpu.make_async_copy(src, dst, sems.at[index, i]) for i, (src, dst) in enumerate(pairs)
        ]

    @pl.when((phase == 0) & (pl.program_id(1) == 0))
    def _():
        for index in range(2):
            for move in moves(index):
                move.start()

    for index in range(2):

        @pl.when((phase == index) & (pl.program_id(1) == 0))
        def _(index=index):
            wait_all(moves(index))

    at = pl.ds(pl.multiple_of(pl.program_id(1) * span, span), span)
    out_ref[...] = dot(left[phase, :, at], right[phase], TN).astype(bf16)


def norm_back(value, grad, gain):
    centred = value - jnp.mean(value, axis=-1, keepdims=True)
    spread = jnp.mean(centred * centred, axis=-1, keepdims=True)
    scale = lax.rsqrt(spread + norm_eps)
    normal = centred * scale
    weighted = grad * gain
    middle = jnp.mean(weighted, axis=-1, keepdims=True)
    slope = jnp.mean(weighted * normal, axis=-1, keepdims=True)
    return normal, scale * (weighted - middle - normal * slope)


def residual_back_body(info, residual_ref, cot_ref, gain_ref, *rest, parts, chips):
    grads, rest = rest[:parts], rest[parts:]
    wholes, (grad_ref, low_ref, own_ref, send_ref, sum_ref, weights, sems) = rest[:2], rest[2:]
    moves = proj_moves(wholes, weights, chips, sems)

    @pl.when(pl.program_id(0) == 0)
    def _():
        for move in moves:
            move.start()
        sum_ref[...] = jnp.zeros_like(sum_ref)

    grad = grads[0][...].astype(f32)
    for other in grads[1:]:
        grad += other[...].astype(f32)
    normal, back = norm_back(residual_ref[...], grad, gain_ref[...])
    cotangent = cot_ref[...].astype(f32)
    total = cotangent + back
    grad_ref[...] = total
    low_ref[...] = total.astype(bf16)
    sum_ref[0:1, :] += jnp.sum(grad * normal, axis=0, keepdims=True)
    sum_ref[1:2, :] += jnp.sum(grad, axis=0, keepdims=True)
    sum_ref[2:3, :] += jnp.sum(total, axis=0, keepdims=True)
    sum_ref[3:4, :] += jnp.sum(cotangent, axis=0, keepdims=True)

    @pl.when(pl.program_id(0) == 0)
    def _():
        wait_all(moves)

    both = dot(low_ref[...], weights[...]).astype(bf16)
    width = own_ref.shape[1]
    own_ref[...] = both[:, :width]
    send_ref[...] = both[:, width:]


def qkv_grad_body(info, first_ref, grad_ref, own_ref, got_ref, att_own, att_got, *rest):
    out_ref = rest[-1]
    width = grad_ref.shape[1]
    out_ref[:, :width] = dot(first_ref[...], grad_ref[...], TN).astype(bf16)
    out_ref[:, width:] = (
        dot(own_ref[...], att_own[...], TN) + dot(got_ref[...], att_got[...], TN)
    ).astype(bf16)


def first_norm_body(info, *refs, chips):
    grads, (x_ref, res_ref, gain_ref, *rest) = refs[: 2 * chips], refs[2 * chips :]
    wholes, (low_ref, sum_ref, weights, lefts, total, sems) = rest[:2], rest[2:]
    half, width = lefts.shape[1:]
    part = wholes[0].shape[1] // chips

    def move(i):
        return pltpu.make_async_copy(
            wholes[i // chips].at[:, pl.ds(i % chips * part, width)], weights.at[i], sems.at[i]
        )

    for i in range(2 * chips):
        move(i).start()
    for i in range(2 * chips):
        lefts[i] = grads[i][...]
    total[...] = jnp.zeros_like(total)

    def term(i, _):
        pltpu.make_async_copy(
            wholes[0].at[:, pl.ds(0, width)], weights.at[i], sems.at[i]
        ).wait()
        total[...] += dot(lefts[i], weights[i], NT)
        return 0

    lax.fori_loop(0, 2 * chips, term, 0)
    step = row_step(total.shape[0])
    sum_ref[...] = jnp.zeros_like(sum_ref)

    def rows(i, _):
        at = pl.ds(pl.multiple_of(i * step, 16), step)
        grad = total[at, :]
        normal, back = norm_back(x_ref[at, :].astype(f32), grad, gain_ref[...])
        low_ref[at, :] = (back + res_ref[at, :]).astype(bf16)
        sum_ref[0:1, :] += jnp.sum(grad * normal, axis=0, keepdims=True)
        sum_ref[1:2, :] += jnp.sum(grad, axis=0, keepdims=True)
        return 0

    lax.fori_loop(0, total.shape[0] // step, rows, 0)


def shards(
    tokens,
    offsets,
    first_gain,
    first_shift,
    qkv_weight,
    qv_bias,
    proj_weight,
    proj_bias,
    second_gain,
    second_shift,
    expand_weight,
    expand_bias,
    shrink_weight,
    shrink_bias,
    cotangent,
):
    token_rows, dim = tokens.shape
    sets = offsets.shape[0]
    part = qkv_weight.shape[2]
    ff = expand_weight.shape[1]
    chips = lax.axis_size("mp") // 2
    ring = Ring(lax.axis_size("dp"))
    dp_index = lax.axis_index("dp")
    mp_index = lax.axis_index("mp")
    x_index, core = mp_index // 2, mp_index % 2
    sets_x = -(-sets // chips)
    slots = sets_x * chips
    rows_x = sets_x * SET_ROWS
    half = rows_x // 2
    pairs = part // LANES
    groups = chips * pairs
    unit_rows = dim // ring.count
    unit = unit_rows // 2
    width = 3 * part
    att_width = groups * LANES
    near = [(0, 0), (0, 1)]
    far_other = [(step, 1) for step in range(1, chips)]
    far_own = [(step, 0) for step in range(1, chips)]
    keys = near + far_other + far_own
    sem = pltpu.SemaphoreType.DMA
    row = lambda value: value.reshape(1, -1)
    whole = lambda *dims: pl.BlockSpec(dims, lambda *_: (0,) * len(dims))

    row_starts = lax.dynamic_index_in_dim(ring.piece_rows(unit_rows), dp_index, 0, False)
    block_ranks = lax.dynamic_index_in_dim(ring.block_ranks(), dp_index, 0, False)
    places = [(x_index - step) % chips * 2 + (core ^ other) for step, other in keys]
    info = jnp.concatenate(
        [jnp.stack([core, x_index, *places]).astype(jnp.int32), row_starts, block_ranks]
    )
    place_base = 2
    base = place_base + len(keys)
    ranks = base + ring.count + 1

    order = Order(info)

    qkv_shard = qkv_weight.astype(bf16).reshape(unit_rows, 3, pairs, LANES)
    qkv_shard = qkv_shard.transpose(0, 2, 1, 3).reshape(unit_rows, width)
    shard = jnp.concatenate([qkv_shard, proj_weight.astype(bf16).T], axis=1)
    bias_shard = jnp.zeros((pairs, 3, LANES), f32)
    bias_shard = bias_shard.at[:, 0].set(qv_bias[0].reshape(pairs, LANES))
    bias_shard = bias_shard.at[:, 2].set(qv_bias[1].reshape(pairs, LANES)).reshape(1, width)
    high = bias_shard.astype(bf16)
    both = jnp.concatenate([high, (bias_shard - high.astype(f32)).astype(bf16)])
    below = jnp.pad(both, ((0, 14), (0, part)))
    joined = jnp.concatenate([shard, below])
    attn_steps = ring.gather_steps(shard, 0, order)
    attn_pieces = [shard]
    far_pieces = {step: [across(joined, step, chips)] for step in range(1, chips)}
    bias_x = [bias_shard]
    for step in range(1, chips):
        got = far_pieces[step][0][unit_rows : unit_rows + 2, :width].astype(f32)
        bias_x.append(got[0:1] + got[1:2])

    def next_step(steps, pieces):
        got = next(steps, None)
        if got is not None:
            pieces += got
        return got

    def send_far(got):
        joined = jnp.concatenate(order.after(got))
        for step in range(1, chips):
            far_pieces[step].append(across(joined, step, chips))

    def last_far(i=-1):
        return [far_pieces[step][i] for step in range(1, chips)]

    def pad_sets(value, wait):
        columns = pl.BlockSpec((token_rows, CHUNK), lambda i, _: (0, i))
        kernel = call(
            functools.partial(pad_body, sets=sets),
            (dim // CHUNK,),
            [columns],
            pl.BlockSpec((slots * SET_ROWS, CHUNK), lambda i, _: (0, i)),
            shape((slots * SET_ROWS, dim), bf16),
            [pltpu.VMEM((token_rows + 16, CHUNK), f32)],
            "pad",
        )
        return order.run(kernel, value, wait=wait)

    got = next_step(attn_steps, attn_pieces)
    order.due = last_far()
    after = next_step(attn_steps, attn_pieces)
    order.due = ()
    send_far(got)
    x_rows = pad_sets(tokens, ())
    order.due = last_far()
    got = next_step(attn_steps, attn_pieces)
    order.due = ()
    send_far(after)
    kernel = call(
        first_low_body,
        (sets_x,),
        [
            pl.BlockSpec((SET_ROWS, dim), lambda i, info: (info[1] * sets_x + i, 0)),
            whole(1, dim),
            whole(1, dim),
        ],
        pl.BlockSpec((SET_ROWS, dim), lambda i, _: (i, 0)),
        shape((rows_x, dim), bf16),
        [],
        "first_low",
    )
    first_low = order.run(kernel, x_rows, row(first_gain), row(first_shift))
    while got:
        order.due = last_far(-2)
        after = next_step(attn_steps, attn_pieces)
        if after is None:
            shrink_shard = tie(shrink_weight, far_pieces[1][0]).astype(bf16).T
            mlp_shard = jnp.concatenate([expand_weight.astype(bf16), shrink_shard], axis=1)
            mlp_pieces = [mlp_shard]
            mlp_steps = ring.gather_steps(tie(mlp_shard, got), 0, order)
            next_step(mlp_steps, mlp_pieces)
        order.due = ()
        send_far(got)
        got = after
    order.due = last_far(-2) + last_far()
    starts = tie(jnp.pad(offsets, ((0, slots - sets), (0, 0))), order.now)
    starts = lax.dynamic_slice_in_dim(starts, x_index * sets_x, sets_x, axis=0)
    positions = jnp.arange(SET_ROWS, dtype=jnp.int32)
    ids = jnp.sum((positions[None, :, None] >= starts[:, None, :]).astype(jnp.int32), axis=-1)
    ids = jnp.where(positions[None, :] < SET_TOKENS, ids, -1)
    key_ids, query_ids = ids[:, :, None], ids[:, None, :]
    cot = pad_sets(cotangent, (key_ids, query_ids))
    next_step(mlp_steps, mlp_pieces)
    order.due = ()
    count = len(attn_pieces)
    copies = count * chips
    far_list = [piece for step in range(1, chips) for piece in far_pieces[step]]

    joint = chips * (width + part)
    kernel = call(
        functools.partial(qkv_body, base=base, unit=unit, chips=chips, count=count),
        (2,),
        [pl.BlockSpec((half, dim), lambda i, _: (i, 0)), whole(1, chips * width)]
        + [ANY] * (count + len(far_list)),
        [pl.BlockSpec((half, chips * width), lambda i, _: (i, 0)), HBM],
        [shape((rows_x, chips * width), bf16), shape((dim, joint), bf16)],
        [pltpu.VMEM((dim, joint), bf16), sem((copies,)), sem],
        "qkv",
    )
    qkv, weights = order.run(kernel, first_low, jnp.concatenate(bias_x, axis=1), *attn_pieces, *far_list)
    order.due = mlp_pieces[-2:]
    both_weights = [weights, partner(order.after(weights), chips)]

    order.due = ()
    next_step(mlp_steps, mlp_pieces)
    kernel = call(
        attend_body,
        (sets_x, groups),
        [
            pl.BlockSpec((SET_ROWS, 3 * LANES), lambda s, i, _: (s, i)),
            pl.BlockSpec((1, SET_ROWS, 1), lambda s, i, _: (s, 0, 0)),
            pl.BlockSpec((1, 1, SET_ROWS), lambda s, i, _: (s, 0, 0)),
        ],
        [
            pl.BlockSpec((SET_ROWS, LANES), lambda s, i, _: (s, i)),
            pl.BlockSpec((1, 1, 2, SET_ROWS), lambda s, i, _: (s, i, 0, 0)),
        ],
        [
            shape((rows_x, att_width), bf16),
            shape((sets_x, groups, 2, SET_ROWS), f32),
        ],
        [pltpu.VMEM((SET_ROWS, SET_ROWS), f32)],
        "attend",
    )
    attended, logs = order.run(kernel, qkv, key_ids, query_ids)
    order.due = [*mlp_pieces[-2:], both_weights[1]]
    attended_other = partner(order.after(attended), chips)
    order.due = ()
    next_step(mlp_steps, mlp_pieces)

    own_half = lambda *dims: pl.BlockSpec(dims, lambda i, info: (info[0], 0))
    own_place = lambda *dims: pl.BlockSpec(dims, lambda i, info: (info[place_base], 0))
    proj_scratch = [pltpu.VMEM((dim, 2 * att_width), bf16), sem((2 * chips,))]
    kernel = call(
        functools.partial(proj_norm_body, chips=chips),
        (1,),
        [own_half(half, att_width)] * 2 + [own_place(half, dim)] + [whole(1, dim)] * 3 + [HBM] * 2,
        [whole(half, dim), whole(half, dim)],
        [shape((half, dim), f32), shape((half, dim), bf16)],
        proj_scratch,
        "proj_norm",
    )
    residual, second_low = order.run(
        kernel,
        attended,
        attended_other,
        x_rows,
        row(proj_bias),
        row(second_gain),
        row(second_shift),
        *both_weights,
    )
    seconds = {(0, 0): second_low}
    for step in range(1, chips):
        seconds[(step, 0)] = across(second_low, step, chips)
    order.due = mlp_pieces[-2:]
    seconds[(0, 1)] = partner(order.after(second_low), chips)
    order.due = ()
    while next_step(mlp_steps, mlp_pieces):
        pass

    def feed(group, gots=()):
        parts = len(group)
        first = keys.index(group[0])
        kernel = call(
            functools.partial(
                mlp_body, base=base, unit=unit, count=count, parts=parts, adds=len(gots)
            ),
            (parts,),
            [
                pl.BlockSpec((half, dim), lambda i, info: (info[place_base + first + i], 0)),
                whole(1, ff),
            ]
            + [HBM] * (count + parts)
            + [whole(half, dim)] * len(gots),
            [pl.BlockSpec((half, ff), lambda i, _: (i, 0))] * 2
            + [whole(half, dim)] * (2 * parts)
            + [whole(1, ff)],
            [shape((parts * half, ff), bf16)] * 2
            + [shape((half, dim), bf16)] * (2 * parts)
            + [shape((1, ff), f32)],
            [
                pltpu.VMEM((dim, ff), bf16),
                pltpu.VMEM((dim, ff), bf16),
                pltpu.VMEM((parts, half, dim), bf16),
                sem((2 * count,)),
                sem((parts,)),
            ],
            "mlp",
        )
        outs = order.run(
            kernel,
            cot,
            row(expand_bias),
            *mlp_pieces,
            *[seconds[key] for key in group],
            *gots,
        )
        backs, rows = outs[2 : 2 + parts], outs[2 + parts : 2 + 2 * parts]
        return outs[0], outs[1], list(backs), list(rows), outs[-1]

    first = feed(near)
    for step in range(1, chips):
        seconds[(step, 1)] = partner(order.after(seconds[(step, 0)]), chips)
    other = feed(far_other)
    own = feed(far_own, [partner(back, chips) for back in other[2]])
    feeds = [first, other, own]

    def along_x(own, sums):
        terms = [own[0], partner(own[1], chips)]
        return terms + [across(value, chips - 1 - i, chips) for i, value in enumerate(sums)]

    back_terms = along_x(first[2], own[2])
    expand_bias_grad = (first[4] + other[4] + own[4]).reshape(ff)
    span = 2 * CHUNK
    total_rows = len(keys) * half
    kernel = call(
        functools.partial(mlp_grad_body, cot_base=place_base, parts=len(keys), groups=3),
        (2, dim // span),
        [HBM] * (7 + len(keys)),
        pl.BlockSpec((span, ff), lambda p, i, _: (i, p)),
        shape((dim, 2 * ff), bf16),
        [
            pltpu.VMEM((2, total_rows, dim), bf16),
            pltpu.VMEM((2, total_rows, ff), bf16),
            sem((2, len(keys) + 3)),
        ],
        "mlp_grad",
    )
    mlp_grad = order.run(
        kernel,
        cot,
        *[seconds[key] for key in keys],
        *[outs[0] for outs in feeds],
        *[outs[1] for outs in feeds],
    )
    mlp_ring = ring.scatter_steps(mlp_grad, ranks, order)
    mlp_due = next(mlp_ring)

    step_rows = row_step(half)
    cot_rows = pl.BlockSpec(
        (step_rows, dim), lambda i, info: (info[place_base] * (half // step_rows) + i, 0)
    )
    plain_rows = lambda count: pl.BlockSpec((step_rows, count), lambda i, _: (i, 0))
    kernel = call(
        functools.partial(residual_back_body, parts=len(back_terms), chips=chips),
        (half // step_rows,),
        [plain_rows(dim), cot_rows, whole(1, dim)]
        + [plain_rows(dim)] * len(back_terms)
        + [HBM] * 2,
        [plain_rows(dim)] * 2 + [plain_rows(att_width)] * 2 + [whole(8, dim)],
        [
            shape((half, dim), f32),
            shape((half, dim), bf16),
            shape((half, att_width), bf16),
            shape((half, att_width), bf16),
            shape((8, dim), f32),
        ],
        proj_scratch,
        "residual_back",
    )
    grad_residual, residual_low, grad_own, grad_send, sums_two = order.run(
        kernel, residual, cot, row(second_gain), *back_terms, *both_weights
    )
    order.due = mlp_due
    grad_got = partner(order.after(grad_send), chips)
    residual_other = partner(order.after(residual_low), chips)
    order.due = ()
    mlp_due = next(mlp_ring)
    if chips == 2:
        out_near = order.after(residual) + shrink_bias + first[3][0].astype(f32)
        out_near = (out_near + partner(order.after(first[3][1]), chips).astype(f32)).astype(bf16)
        out_far = own[3][0].astype(f32)
        out_far = (out_far + partner(other[3][0], chips).astype(f32)).astype(bf16)
        cut = half // 2
        out_sends = iter([out_far[:cut], out_far[cut:], out_near[:cut], out_near[cut:]])
        out_gots = [across(order.after(next(out_sends)), 1, chips)]
    else:
        out_own = [
            (mine.astype(f32) + partner(order.after(got), chips).astype(f32)).astype(bf16)
            for mine, got in zip(own[3], other[3])
        ]
        out_terms = along_x(order.after(first[3]), out_own)

    def attend_back(b):
        half_block = lambda j: pl.BlockSpec(
            (row_step(half), LANES), lambda i, s, _: (lax.rem(2 * s + j, sets_x), b * pairs + i)
        )
        kernel = call(
            functools.partial(attend_back_body, first_half=sets_x),
            (pairs, sets_x),
            [
                pl.BlockSpec((SET_ROWS, 3 * LANES), lambda i, s, _: (s, b * pairs + i)),
                pl.BlockSpec((1, SET_ROWS, 1), lambda i, s, _: (s, 0, 0)),
                pl.BlockSpec((1, 1, SET_ROWS), lambda i, s, _: (s, 0, 0)),
                pl.BlockSpec((1, 1, 2, SET_ROWS), lambda i, s, _: (s, b * pairs + i, 0, 0)),
                half_block(0),
                half_block(0),
                half_block(1),
                half_block(1),
            ],
            [
                pl.BlockSpec((SET_ROWS, 3 * LANES), lambda i, s, _: (s, i)),
                pl.BlockSpec((1, 1, 3 * LANES), lambda i, s, _: (i, 0, 0)),
            ],
            [shape((rows_x, width), bf16), shape((pairs, 1, 3 * LANES), f32)],
            [pltpu.VMEM((sets_x, SET_ROWS, SET_ROWS), f32)],
            "attend_back",
        )
        ids = key_ids, query_ids
        return order.run(kernel, qkv, *ids, logs, grad_own, grad_got, grad_own, grad_got)

    def qkv_grad(b, before):
        columns = lambda count: pl.BlockSpec((count, CHUNK), lambda i, _: (0, i))
        kernel = call(
            qkv_grad_body,
            (dim // CHUNK,),
            [
                columns(rows_x),
                whole(rows_x, width),
                columns(half),
                columns(half),
                pl.BlockSpec((half, part), lambda i, info: (info[0], b)),
                pl.BlockSpec((half, part), lambda i, info: (1 - info[0], b)),
            ]
            + [ANY] * len(before),
            pl.BlockSpec((CHUNK, width + part), lambda i, _: (i, b)),
            shape((dim, joint), bf16),
            [],
            "qkv_grad",
            {7 + i: i for i in range(len(before))},
        )
        return order.run(
            kernel,
            first_low,
            grads_qkv[b],
            residual_low,
            residual_other,
            attended,
            attended,
            *before,
        )

    def out_due(i):
        if chips != 2 or i > 3:
            return ()
        if i < 3:
            out_gots.append(across(order.after(next(out_sends)), 1, chips))
        return out_gots[i]

    grads_qkv, grads_other, qkv_sums, begun = {}, {}, {}, ()
    for b in range(1, chips):
        grads_qkv[b], qkv_sums[b] = attend_back(b)
        order.due = mlp_due, residual_other, out_due(b - 1)
        grads_other[b] = partner(order.after(grads_qkv[b]), chips)
        order.due = ()
        mlp_due = next(mlp_ring, ())
        begun = (qkv_grad(b, begun),)
    grads_qkv[0], qkv_sums[0] = attend_back(0)
    order.due = mlp_due, [grads_other[b] for b in range(1, chips)], out_due(1)
    grads_other[0] = partner(order.after(grads_qkv[0]), chips)
    order.due = ()
    mlp_due = next(mlp_ring, ())
    attn_ring = ring.scatter_steps(qkv_grad(0, begun), ranks, order)
    order.due = [grads_other[b] for b in range(chips)]
    next(attn_ring)
    order.due = ()
    for mlp_grad in mlp_ring:
        pass
    expand_part, shrink_part = mlp_grad[:, :ff], mlp_grad[:, ff:].T
    order.due = out_due(2)
    attn_due = next(attn_ring)
    order.due = ()

    kernel = call(
        functools.partial(first_norm_body, chips=chips),
        (1,),
        [own_half(half, width)] * (2 * chips)
        + [own_place(half, dim), whole(half, dim), whole(1, dim)]
        + [HBM] * 2,
        [whole(half, dim), whole(8, dim)],
        [shape((half, dim), bf16), shape((8, dim), f32)],
        [
            pltpu.VMEM((2 * chips, dim, width), bf16),
            pltpu.VMEM((2 * chips, half, width), bf16),
            pltpu.VMEM((half, dim), f32),
            sem((2 * chips,)),
        ],
        "first_norm",
    )
    tokens_low, sums_one = order.run(
        kernel,
        *[grads_qkv[b] for b in range(chips)],
        *[grads_other[b] for b in range(chips)],
        x_rows,
        grad_residual,
        row(first_gain),
        *both_weights,
    )

    def assemble(rows, dtype):
        block = lambda count, at: pl.BlockSpec((count, CHUNK), lambda i, _: (at, i))
        kernel = call(
            functools.partial(assemble_body, base=place_base, sets=sets),
            (dim // CHUNK,),
            [block(half, rows[key][1]) for key in keys],
            block(token_rows, 0),
            shape((token_rows, dim), dtype),
            [
                pltpu.VMEM((slots * SET_ROWS, CHUNK), f32),
                pltpu.VMEM((token_rows + 16, CHUNK), f32),
            ],
            "assemble",
        )
        return order.run(kernel, *[rows[key][0] for key in keys])

    order.due = attn_due, out_due(3)
    tokens_low = order.after(tokens_low)
    order.due = ()
    grads, outs = {(0, 0): (tokens_low, 0)}, {}
    for step in range(1, chips):
        grads[(step, 0)] = across(tokens_low, step, chips), 0
    next(attn_ring)
    if chips == 2:
        out_rows = jnp.concatenate([out_near, out_far]).astype(f32)
        out_rows = out_rows + jnp.concatenate(order.after(out_gots)).astype(f32)
    else:
        out_rows = order.after(residual) + shrink_bias
        for term in out_terms:
            out_rows = out_rows + term.astype(f32)
        low = out_rows.astype(bf16)
        out_rows = jnp.concatenate([low] + [across(low, step, chips) for step in range(1, chips)])
    out_rows = out_rows.astype(bf16)
    out_other = partner(out_rows, chips)
    for step in range(chips):
        outs[(step, 0)], outs[(step, 1)] = (out_rows, step), (out_other, step)

    bias_sums = jnp.stack([qkv_sums[b] for b in range(chips)]).reshape(chips, pairs, 3, LANES)
    bias_sums = jnp.stack([bias_sums[:, :, 0], bias_sums[:, :, 2]], axis=1)
    hidden_sums = jnp.pad(expand_bias_grad, (0, -ff % dim)).reshape(-1, dim)
    shared = jnp.concatenate([sums_one[0:2], sums_two[2:3], sums_two[0:2], sums_two[3:4]])
    shared = shared + partner(shared, chips)
    small = jnp.concatenate([shared, bias_sums.reshape(-1, dim), hidden_sums])
    bits = [1 << i for i in range(ring.count.bit_length() - 1)]

    def add_ranks(small, bit):
        pairs = [(r, r ^ bit) for r in range(ring.count)]
        return small + lax.ppermute(order.after(small), "dp", pairs)

    def add_chips(small):
        shared = small[:6]
        own, *others = small[6:7].reshape(chips, 2 * part)
        if chips == 2:
            sent = jnp.concatenate([shared.reshape(-1), others[0]])
            got = across(order.after(sent), 1, chips)
            shared = shared + got[: 6 * dim].reshape(6, dim)
            own = own + got[6 * dim :]
        else:
            bit = 1
            while bit < chips:
                flips = [(m, m ^ (2 * bit)) for m in range(2 * chips)]
                shared = shared + lax.ppermute(shared, "mp", flips)
                bit *= 2
            for step in range(1, chips):
                own = own + across(others[step - 1], chips - step, chips)
        own = jnp.pad(own, (0, dim - 2 * part)).reshape(1, dim)
        return jnp.concatenate([shared, own, small[7:]])

    outputs = assemble(outs, bf16)
    small = add_ranks(small, bits[0])
    order.hold = (small, expand_part, shrink_part)
    next(attn_ring)
    grads[(0, 1)] = partner(order.after(tokens_low), chips), 0
    for step in range(1, chips):
        grads[(step, 1)] = partner(order.after(grads[(step, 0)][0]), chips), 0
    small = add_chips(small)
    grad_tokens = assemble(grads, f32)
    for attn_sum in attn_ring:
        pass
    for bit in bits[1:]:
        small = add_ranks(small, bit)
    shared = small[:6]
    bias_own = small[6, : 2 * part].reshape(2, part)
    expand_bias_grad = small[7:].reshape(-1)[:ff]
    attn_part = attn_sum[:, : width + part]
    for step in range(1, chips):
        sent = attn_sum[:, step * (width + part) : (step + 1) * (width + part)].astype(bf16)
        attn_part = attn_part + across(sent, chips - step, chips).astype(f32)

    qkv_part = attn_part[:, :width].reshape(unit_rows, pairs, 3, LANES)
    qkv_part = qkv_part.transpose(0, 2, 1, 3).reshape(unit_rows, 3, part)
    return (
        outputs,
        grad_tokens,
        shared[0],
        shared[1],
        qkv_part,
        bias_own,
        attn_part[:, width:].T,
        shared[2],
        shared[3],
        shared[4],
        expand_part,
        expand_bias_grad,
        shrink_part,
        shared[5],
    )


def solution(mesh):
    placed = (
        P("dp", None),
        P("dp", None),
        P(),
        P(),
        P("dp", None, "mp"),
        P(None, "mp"),
        P("mp", "dp"),
        P(),
        P(),
        P(),
        P("dp", "mp"),
        P("mp"),
        P("mp", "dp"),
        P(),
        P("dp", None),
    )
    return jax.shard_map(
        shards,
        mesh=mesh,
        in_specs=placed,
        out_specs=(
            P("dp", None),
            P("dp", None),
            P(),
            P(),
            P("dp", None, "mp"),
            P(None, "mp"),
            P("mp", "dp"),
            P(),
            P(),
            P(),
            P("dp", "mp"),
            P("mp"),
            P("mp", "dp"),
            P(),
        ),
        check_vma=False,
    )
```

```python
import functools

import jax
import jax.numpy as jnp
import numpy as np
from jax import lax
from jax.experimental import pallas as pl
from jax.experimental.pallas import tpu as pltpu
from jax.sharding import PartitionSpec as P

HEAD_DIM = 64
SET_TOKENS = 345
SET_ROWS = 352
LANES = 128
CHUNK = 256

norm_eps = 1e-06
masked_score = -1e30
root_half = 0.7071067811865476
density_scale = 0.3989422804014327
f32 = jnp.float32
bf16 = jnp.bfloat16
NN = (((1,), (0,)), ((), ()))
NT = (((1,), (1,)), ((), ()))
TN = (((0,), (0,)), ((), ()))
ANY = pl.BlockSpec(memory_space=pl.ANY)
HBM = pl.BlockSpec(memory_space=pltpu.HBM)


def dot(left, right, dims=NN):
    return lax.dot_general(left, right, dims, preferred_element_type=f32)


ROOM = {
    "ring_first": 4,
    "ring_add": 10,
    "ring_last": 8,
    "ring_end": 8,
    "qkv": 20,
    "pad": 20,
    "assemble": 58,
    "first_low": 10,
    "attend": 10,
    "attend_back": 12,
    "proj_norm": 20,
    "mlp": 58,
    "mlp_grad": 58,
    "residual_back": 16,
    "qkv_grad": 20,
    "first_norm": 58,
}


COST = {"ring_end": 2 * 10**10}


def call(body, grid, in_specs, out_specs, out_shape, scratch, name, aliases=None):
    return pl.pallas_call(
        body,
        grid_spec=pltpu.PrefetchScalarGridSpec(
            num_scalar_prefetch=1,
            grid=grid,
            in_specs=in_specs,
            out_specs=out_specs,
            scratch_shapes=scratch,
        ),
        out_shape=out_shape,
        compiler_params=pltpu.CompilerParams(
            dimension_semantics=("arbitrary",) * len(grid), vmem_limit_bytes=ROOM[name] * 2**20
        ),
        cost_estimate=pl.CostEstimate(
            flops=COST.get(name, 1), bytes_accessed=1, transcendentals=0
        ),
        name=name,
        input_output_aliases=aliases or {},
    )


def tie(value, *earlier):
    return lax.optimization_barrier((value, earlier))[0]


class Order:
    def __init__(self, info):
        self.info = info
        self.now = info
        self.due = ()
        self.hold = ()

    def after(self, value):
        return tie(value, self.now, self.due)

    def run(self, kernel, *values, wait=()):
        out = kernel(tie(self.info, self.now, wait, self.hold), *values)
        self.hold = ()
        self.now = out[0] if isinstance(out, (list, tuple)) else out
        return out


def shape(dims, dtype):
    return jax.ShapeDtypeStruct(tuple(dims), dtype)


def ring_order(count):
    width = 1
    while 2 * (2 * width) ** 2 <= count:
        width *= 2
    length = count // width
    if width == 1:
        return list(range(count))
    path = []
    for z in range(length):
        columns = range(1, width) if z % 2 == 0 else range(width - 1, 0, -1)
        path += [z * width + y for y in columns]
    path += [z * width for z in range(length - 1, -1, -1)]
    return path


class Ring:
    def __init__(self, count):
        self.count = count
        self.order = ring_order(count)
        self.place = {rank: i for i, rank in enumerate(self.order)}
        self.ahead = [(self.order[i], self.order[(i + 1) % count]) for i in range(count)]
        self.behind = [(self.order[i], self.order[(i - 1) % count]) for i in range(count)]

    def rank_at(self, rank, offset):
        return self.order[(self.place[rank] + offset) % self.count]

    def send_ahead(self, value):
        return lax.ppermute(value, "dp", self.ahead)

    def send_behind(self, value):
        return lax.ppermute(value, "dp", self.behind)

    def gather_steps(self, block, axis, order):
        half = block.shape[axis] // 2
        forward = backward = block
        for step in range(1, self.count // 2 + 1):
            if step == self.count // 2:
                forward = lax.slice_in_dim(forward, 0, half, axis=axis)
                backward = lax.slice_in_dim(backward, half, 2 * half, axis=axis)
            forward, backward = order.after((forward, backward))
            forward = self.send_ahead(forward)
            backward = self.send_behind(backward)
            yield forward, backward

    def piece_rows(self, rows):
        table = []
        middle = self.count // 2
        for rank in range(self.count):
            starts = [rank * rows]
            for step in range(1, middle + 1):
                ahead = self.rank_at(rank, -step) * rows
                behind = self.rank_at(rank, step) * rows
                if step == middle:
                    behind += rows // 2
                starts += [ahead, behind]
            table.append(starts)
        return np.array(table, np.int32)

    def block_ranks(self):
        middle = self.count // 2
        return np.array(
            [
                [self.rank_at(rank, d) for d in range(-middle, middle + 1)]
                for rank in range(self.count)
            ],
            np.int32,
        )

    def scatter_steps(self, whole, ranks, order, last="ring_last"):
        middle = self.count // 2
        dim, columns = whole.shape
        rows = dim // self.count
        half = rows // 2
        wide = columns
        grid = (columns // wide,)
        block = lambda d: pl.BlockSpec((rows, wide), lambda j, info: (info[ranks + middle + d], j))
        plain = lambda count: pl.BlockSpec((count, wide), lambda j, _: (0, j))
        kernel = call(
            ring_first_body,
            grid,
            [
                pl.BlockSpec((half, wide), lambda j, info: (2 * info[ranks + 2 * middle], j)),
                pl.BlockSpec((half, wide), lambda j, info: (2 * info[ranks] + 1, j)),
            ],
            [plain(half)] * 2,
            [shape((half, columns), bf16)] * 2,
            [],
            "ring_first",
        )
        forward, backward = order.run(kernel, whole, whole)
        for step in range(1, middle + 1):
            forward = self.send_ahead(order.after(forward))
            backward = self.send_behind(order.after(backward))
            yield forward, backward
            near = middle - step
            if near == 0:
                break
            kernel = call(
                ring_add_body,
                grid,
                [block(near), block(-near)] + [plain(forward.shape[0])] * 2,
                [plain(rows)] * 2,
                [shape((rows, columns), bf16)] * 2,
                [],
                "ring_add",
            )
            forward, backward = order.run(kernel, whole, whole, forward, backward)
        kernel = call(
            ring_last_body,
            grid,
            [block(0)] + [plain(rows)] * 2,
            plain(rows),
            shape((rows, columns), f32),
            [],
            last,
        )
        yield order.run(kernel, whole, forward, backward)


def across(value, step, chips):
    pairs = [
        (x * 2 + core, (x + step) % chips * 2 + core) for x in range(chips) for core in range(2)
    ]
    return lax.ppermute(value, "mp", pairs)


def partner(value, chips):
    return lax.ppermute(value, "mp", [(m, m ^ 1) for m in range(2 * chips)])


def layer_norm(values, gain, shift):
    centre = jnp.mean(values, axis=-1, keepdims=True)
    offset_rows = values - centre
    spread = jnp.mean(offset_rows * offset_rows, axis=-1, keepdims=True)
    return offset_rows * lax.rsqrt(spread + norm_eps) * gain + shift


def start_all(copies, sems):
    moves = [pltpu.make_async_copy(src, dst, sems.at[i]) for i, (src, dst) in enumerate(copies)]
    for move in moves:
        move.start()
    return moves


def wait_all(moves):
    for move in moves:
        move.wait()


def weight_copies(info, base, pieces, unit, targets):
    copies = []
    for i, piece in enumerate(pieces):
        rows = piece.shape[-2]
        place = pl.ds(pl.multiple_of(info[base + i], unit), rows)
        for source, target in targets:
            copies.append((source(piece), target(place)))
    return copies


def ring_first_body(info, ahead_ref, behind_ref, ahead_out, behind_out):
    ahead_out[...] = ahead_ref[...]
    behind_out[...] = behind_ref[...]


def ring_add_body(info, ahead_ref, behind_ref, got_ahead, got_behind, ahead_out, behind_out):
    rows, part = ahead_out.shape[0], got_ahead.shape[0]
    first, last = slice(0, part), slice(rows - part, rows)
    total = ahead_ref[first, :].astype(f32) + got_ahead[...].astype(f32)
    ahead_out[first, :] = total.astype(bf16)
    total = behind_ref[last, :].astype(f32) + got_behind[...].astype(f32)
    behind_out[last, :] = total.astype(bf16)
    if part < rows:
        ahead_out[part:, :] = ahead_ref[part:, :]
        behind_out[: rows - part, :] = behind_ref[: rows - part, :]


def ring_last_body(info, own_ref, got_ahead, got_behind, out_ref):
    both = got_ahead[...].astype(f32) + got_behind[...].astype(f32)
    out_ref[...] = own_ref[...].astype(f32) + both


def qkv_body(info, x_ref, bias_ref, *rest, base, unit, chips, count):
    steps = count // 2 + 1
    own, rest = rest[:count], rest[count:]
    far, (out_ref, whole_ref, weights, sems, out_sem) = (
        rest[: steps * (chips - 1)],
        rest[steps * (chips - 1) :],
    )
    part = weights.shape[1] // chips
    width = out_ref.shape[1] // chips
    keep = pltpu.make_async_copy(weights, whole_ref, out_sem)

    @pl.when(pl.program_id(0) == 0)
    def _():
        copies = []
        for b in range(chips):
            for i, piece in enumerate(own):
                rows = piece.shape[0]
                source = piece
                if b:
                    joined = far[(b - 1) * steps + (i + 1) // 2]
                    source = joined.at[pl.ds(rows if i and i % 2 == 0 else 0, rows)]
                place = pl.ds(pl.multiple_of(info[base + i], unit), rows)
                copies.append((source, weights.at[place, pl.ds(b * part, part)]))
        wait_all(start_all(copies, sems))
        keep.start()

    def columns(b, _):
        to = pl.ds(pl.multiple_of(b * width, LANES), width)
        product = dot(x_ref[...], weights[:, pl.ds(pl.multiple_of(b * part, LANES), width)])
        out_ref[:, to] = (product + bias_ref[:, to]).astype(bf16)
        return 0

    lax.fori_loop(0, chips, columns, 0)

    @pl.when(pl.program_id(0) == pl.num_programs(0) - 1)
    def _():
        keep.wait()


def pad_body(info, in_ref, out_ref, rows, *, sets):
    total = in_ref.shape[0]
    rows[0:total, :] = in_ref[...].astype(f32)
    inside = lax.broadcasted_iota(jnp.int32, (SET_ROWS, 1), 0) < SET_TOKENS
    for g in range(out_ref.shape[0] // SET_ROWS):
        to = slice(g * SET_ROWS, (g + 1) * SET_ROWS)
        if g < sets:
            value = rows[g * SET_TOKENS : g * SET_TOKENS + SET_ROWS, :]
            out_ref[to, :] = jnp.where(inside, value, 0.0).astype(bf16)
        else:
            out_ref[to, :] = jnp.zeros((SET_ROWS, out_ref.shape[1]), bf16)


def assemble_body(info, *refs, base, sets):
    pieces, (out_ref, padded, packed) = refs[:-3], refs[-3:]
    half = pieces[0].shape[0]
    for i, piece in enumerate(pieces):
        place = pl.ds(pl.multiple_of(info[base + i] * half, 16), half)
        padded[place, :] = piece[...].astype(f32)
    target = out_ref if out_ref.dtype == f32 else packed
    for g in range(sets):
        target[g * SET_TOKENS : (g + 1) * SET_TOKENS, :] = padded[
            g * SET_ROWS : g * SET_ROWS + SET_TOKENS, :
        ]
    if out_ref.dtype != f32:
        out_ref[...] = packed[0 : out_ref.shape[0], :].astype(out_ref.dtype)


def first_low_body(info, x_ref, gain_ref, shift_ref, out_ref):
    out_ref[...] = layer_norm(x_ref[...].astype(f32), gain_ref[...], shift_ref[...]).astype(bf16)


def head_mask(head):
    lane = lax.broadcasted_iota(jnp.int32, (1, LANES), 1)
    return (lane < HEAD_DIM) if head == 0 else (lane >= HEAD_DIM)


def keep_head(value, head):
    return jnp.where(head_mask(head), value, jnp.zeros_like(value))


def attend_body(info, qkv_ref, key_ids, query_ids, out_ref, log_ref, block):
    @pl.when(pl.program_id(1) == 0)
    def _():
        block[...] = jnp.where(key_ids[0] == query_ids[0], 0.0, masked_score)

    factor = HEAD_DIM**-0.5
    query = qkv_ref[:, 0:LANES] * jnp.asarray(factor, bf16)
    key = qkv_ref[:, LANES : 2 * LANES]
    value = qkv_ref[:, 2 * LANES : 3 * LANES]
    halves = []
    for head in range(2):
        scores = dot(key, keep_head(query, head), NT) + block[...]
        peak = jnp.max(scores, axis=0, keepdims=True)
        raised = jnp.exp(scores - peak)
        total = jnp.sum(raised, axis=0, keepdims=True)
        mixed = dot(keep_head(value, head), raised.astype(bf16), TN)
        halves.append(mixed * (1.0 / total))
        log_ref[0, 0, head : head + 1, :] = peak + jnp.log(total)
    out_ref[...] = (halves[0] + halves[1]).T.astype(bf16)


def attend_back_body(info, qkv_ref, key_ids, query_ids, log_ref, *rest, first_half):
    grads = rest[:4]
    out_ref, sum_ref, block = rest[-3:]
    turn = pl.program_id(1)

    @pl.when(pl.program_id(0) == 0)
    def _():
        block[turn] = jnp.where(key_ids[0] == query_ids[0], 0.0, masked_score)

    factor = HEAD_DIM**-0.5
    query = qkv_ref[:, 0:LANES] * jnp.asarray(factor, bf16)
    key = qkv_ref[:, LANES : 2 * LANES]
    value = qkv_ref[:, 2 * LANES : 3 * LANES]
    parts = []
    for j in range(2):
        core = ((2 * turn + j) >= first_half).astype(jnp.int32)
        parts.append(jnp.where(core == info[0], grads[2 * j][...], grads[2 * j + 1][...]))
    grad = jnp.concatenate(parts, axis=0)
    grad_query = grad_key = grad_value = 0.0
    for head in range(2):
        query_one = keep_head(query, head)
        grad_one = keep_head(grad, head)
        scores = dot(key, query_one, NT) + block[turn]
        weights = jnp.exp(scores - log_ref[0, 0, head : head + 1, :])
        grad_value += dot(weights.astype(bf16), grad_one)
        grad_weights = dot(value, grad_one, NT)
        centre = jnp.sum(weights * grad_weights, axis=0, keepdims=True)
        low = (weights * (grad_weights - centre)).astype(bf16)
        grad_key += dot(low, query_one)
        grad_query += dot(keep_head(key, head), low, TN)
    grad_query = (grad_query * factor).T
    out_ref[:, 0:LANES] = grad_query.astype(bf16)
    out_ref[:, LANES : 2 * LANES] = grad_key.astype(bf16)
    out_ref[:, 2 * LANES : 3 * LANES] = grad_value.astype(bf16)

    @pl.when(turn == 0)
    def _():
        sum_ref[...] = jnp.zeros_like(sum_ref)

    sum_ref[0, :, 0:LANES] += jnp.sum(grad_query, axis=0, keepdims=True)
    sum_ref[0, :, 2 * LANES : 3 * LANES] += jnp.sum(grad_value, axis=0, keepdims=True)


def proj_moves(wholes, weights, chips, sems):
    width = weights.shape[1] // (2 * chips)
    part = wholes[0].shape[1] // chips
    copies = []
    for j, source in enumerate(wholes):
        for b in range(chips):
            columns = pl.ds((b + 1) * part - width, width)
            target = pl.ds((j * chips + b) * width, width)
            copies.append((source.at[:, columns], weights.at[:, target]))
    return [pltpu.make_async_copy(src, dst, sems.at[i]) for i, (src, dst) in enumerate(copies)]


def proj_norm_body(
    info, own_ref, got_ref, x_ref, bias_ref, gain_ref, shift_ref, *rest, chips
):
    wholes, (residual_ref, low_ref, weights, sems) = rest[:2], rest[2:]
    moves = proj_moves(wholes, weights, chips, sems)
    for move in moves:
        move.start()
    wait_all(moves)
    width = own_ref.shape[1]
    span = 2 * CHUNK

    def columns(i, _):
        at = pl.ds(pl.multiple_of(i * span, span), span)
        own_part = dot(own_ref[...], weights[at, :width], NT)
        residual_ref[:, at] = own_part + dot(got_ref[...], weights[at, width:], NT)
        return 0

    lax.fori_loop(0, residual_ref.shape[1] // span, columns, 0)
    step = row_step(residual_ref.shape[0])

    def rows(i, _):
        at = pl.ds(pl.multiple_of(i * step, 16), step)
        value = residual_ref[at, :] + x_ref[at, :].astype(f32) + bias_ref[...]
        residual_ref[at, :] = value
        low_ref[at, :] = layer_norm(value, gain_ref[...], shift_ref[...]).astype(bf16)
        return 0

    lax.fori_loop(0, residual_ref.shape[0] // step, rows, 0)


def row_step(rows):
    return 176 if rows % 176 == 0 else rows


def mlp_body(info, cot_ref, bias_ref, *rest, base, unit, count, parts, adds):
    pieces, rest = rest[:count], rest[count:]
    seconds, rest = rest[:parts], rest[parts:]
    gots, rest = rest[:adds], rest[adds:]
    hidden_ref, pre_ref, rest = rest[0], rest[1], rest[2:]
    backs, outs, rest = rest[:parts], rest[parts : 2 * parts], rest[2 * parts :]
    sum_ref, expand, shrink, rows, sems, row_sems = rest
    width = expand.shape[1]
    turn = pl.program_id(0)

    @pl.when(turn == 0)
    def _():
        targets = [
            (
                lambda piece: piece.at[:, pl.ds(0, width)],
                lambda place: expand.at[place, :],
            ),
            (
                lambda piece: piece.at[:, pl.ds(width, width)],
                lambda place: shrink.at[place, :],
            ),
        ]
        moves = start_all(weight_copies(info, base, pieces, unit, targets), sems)
        start_all([(seconds[i], rows.at[i]) for i in range(parts)], row_sems)
        wait_all(moves)
        sum_ref[...] = jnp.zeros_like(sum_ref)

    pltpu.make_async_copy(seconds[0], rows.at[turn], row_sems.at[turn]).wait()
    span = 2 * CHUNK if width % (2 * CHUNK) == 0 else LANES

    def columns(i, _):
        at = pl.ds(pl.multiple_of(i * span, span), span)
        pre = dot(rows[turn], expand[:, at]) + bias_ref[:, at]
        below = 0.5 * (1.0 + lax.erf(pre * root_half))
        density = density_scale * jnp.exp(-0.5 * pre * pre)
        hidden_ref[:, at] = (pre * below).astype(bf16)
        grad = dot(cot_ref[...], shrink[:, at]) * (below + pre * density)
        sum_ref[:, at] += jnp.sum(grad, axis=0, keepdims=True)
        pre_ref[:, at] = grad.astype(bf16)
        return 0

    lax.fori_loop(0, width // span, columns, 0)

    def back(i, _):
        at = pl.ds(pl.multiple_of(i * span, span), span)
        for targets, left, right, kind in (
            (backs, pre_ref, expand, 0),
            (outs, hidden_ref, shrink, 1),
        ):
            product = dot(left[...], right[at, :], NT)
            for i in range(parts):

                @pl.when(turn == i)
                def _(i=i, targets=targets, product=product, kind=kind):
                    total = product
                    if adds and kind == 0:
                        total = total + gots[i][:, at].astype(f32)
                    targets[i][:, at] = total.astype(bf16)

        return 0

    lax.fori_loop(0, backs[0].shape[1] // span, back, 0)


def mlp_grad_body(info, cot_ref, *rest, cot_base, parts, groups):
    seconds, rest = rest[:parts], rest[parts:]
    hiddens, pres, rest = rest[:groups], rest[groups : 2 * groups], rest[2 * groups :]
    out_ref, left, right, sems = rest
    phase = pl.program_id(0)
    rows = left.shape[1] // parts
    span = out_ref.shape[0]

    def moves(index):
        pairs = []
        for i in range(parts):
            source = seconds[i]
            if index == 1:
                place = pl.multiple_of(info[cot_base + i] * rows, 16)
                source = cot_ref.at[pl.ds(place, rows)]
            pairs.append((source, left.at[index, pl.ds(i * rows, rows)]))
        start = 0
        for source in (pres, hiddens)[index]:
            pairs.append((source, right.at[index, pl.ds(start, source.shape[0])]))
            start += source.shape[0]
        return [
            pltpu.make_async_copy(src, dst, sems.at[index, i]) for i, (src, dst) in enumerate(pairs)
        ]

    @pl.when((phase == 0) & (pl.program_id(1) == 0))
    def _():
        for index in range(2):
            for move in moves(index):
                move.start()

    for index in range(2):

        @pl.when((phase == index) & (pl.program_id(1) == 0))
        def _(index=index):
            wait_all(moves(index))

    at = pl.ds(pl.multiple_of(pl.program_id(1) * span, span), span)
    out_ref[...] = dot(left[phase, :, at], right[phase], TN).astype(bf16)


def norm_back(value, grad, gain):
    centred = value - jnp.mean(value, axis=-1, keepdims=True)
    spread = jnp.mean(centred * centred, axis=-1, keepdims=True)
    scale = lax.rsqrt(spread + norm_eps)
    normal = centred * scale
    weighted = grad * gain
    middle = jnp.mean(weighted, axis=-1, keepdims=True)
    slope = jnp.mean(weighted * normal, axis=-1, keepdims=True)
    return normal, scale * (weighted - middle - normal * slope)


def residual_back_body(info, residual_ref, cot_ref, gain_ref, *rest, parts, chips):
    grads, rest = rest[:parts], rest[parts:]
    wholes, (grad_ref, low_ref, own_ref, send_ref, sum_ref, weights, sems) = rest[:2], rest[2:]
    moves = proj_moves(wholes, weights, chips, sems)

    @pl.when(pl.program_id(0) == 0)
    def _():
        for move in moves:
            move.start()
        sum_ref[...] = jnp.zeros_like(sum_ref)

    grad = grads[0][...].astype(f32)
    for other in grads[1:]:
        grad += other[...].astype(f32)
    normal, back = norm_back(residual_ref[...], grad, gain_ref[...])
    cotangent = cot_ref[...].astype(f32)
    total = cotangent + back
    grad_ref[...] = total
    low_ref[...] = total.astype(bf16)
    sum_ref[0:1, :] += jnp.sum(grad * normal, axis=0, keepdims=True)
    sum_ref[1:2, :] += jnp.sum(grad, axis=0, keepdims=True)
    sum_ref[2:3, :] += jnp.sum(total, axis=0, keepdims=True)
    sum_ref[3:4, :] += jnp.sum(cotangent, axis=0, keepdims=True)

    @pl.when(pl.program_id(0) == 0)
    def _():
        wait_all(moves)

    both = dot(low_ref[...], weights[...]).astype(bf16)
    width = own_ref.shape[1]
    own_ref[...] = both[:, :width]
    send_ref[...] = both[:, width:]


def qkv_grad_body(info, first_ref, grad_ref, own_ref, got_ref, att_own, att_got, *rest):
    out_ref = rest[-1]
    width = grad_ref.shape[1]
    out_ref[:, :width] = dot(first_ref[...], grad_ref[...], TN).astype(bf16)
    out_ref[:, width:] = (
        dot(own_ref[...], att_own[...], TN) + dot(got_ref[...], att_got[...], TN)
    ).astype(bf16)


def first_norm_body(info, *refs, chips):
    grads, (x_ref, res_ref, gain_ref, *rest) = refs[: 2 * chips], refs[2 * chips :]
    two_ref, biases, hiddens, rest = rest[0], rest[1 : 1 + chips], rest[1 + chips : 4 + chips], rest[4 + chips :]
    wholes, (low_ref, sum_ref, weights, lefts, total, sems) = rest[:2], rest[2:]
    half, width = lefts.shape[1:]
    part = wholes[0].shape[1] // chips

    def move(i):
        return pltpu.make_async_copy(
            wholes[i // chips].at[:, pl.ds(i % chips * part, width)], weights.at[i], sems.at[i]
        )

    for i in range(2 * chips):
        move(i).start()
    for i in range(2 * chips):
        lefts[i] = grads[i][...]
    total[...] = jnp.zeros_like(total)

    def term(i, _):
        pltpu.make_async_copy(
            wholes[0].at[:, pl.ds(0, width)], weights.at[i], sems.at[i]
        ).wait()
        total[...] += dot(lefts[i], weights[i], NT)
        return 0

    lax.fori_loop(0, 2 * chips, term, 0)
    step = row_step(total.shape[0])
    sum_ref[...] = jnp.zeros_like(sum_ref)
    for i, j in enumerate((2, 0, 1, 3)):
        sum_ref[2 + i : 3 + i, :] = two_ref[j : j + 1, :]
    pairs = biases[0].shape[0]
    for b in range(chips):
        for kind in range(2):
            for pair in range(pairs):
                to = ((b * 2 + kind) * pairs + pair) * LANES
                value = biases[b][pair, :, kind * 2 * LANES : (kind * 2 + 1) * LANES]
                sum_ref[6:7, to : to + LANES] = value
    ff = hiddens[0].shape[1]
    sum_ref[7:8, 0:ff] = hiddens[0][...] + hiddens[1][...] + hiddens[2][...]

    def rows(i, _):
        at = pl.ds(pl.multiple_of(i * step, 16), step)
        grad = total[at, :]
        normal, back = norm_back(x_ref[at, :].astype(f32), grad, gain_ref[...])
        low_ref[at, :] = (back + res_ref[at, :]).astype(bf16)
        sum_ref[0:1, :] += jnp.sum(grad * normal, axis=0, keepdims=True)
        sum_ref[1:2, :] += jnp.sum(grad, axis=0, keepdims=True)
        return 0

    lax.fori_loop(0, total.shape[0] // step, rows, 0)


def shards(
    tokens,
    offsets,
    first_gain,
    first_shift,
    qkv_weight,
    qv_bias,
    proj_weight,
    proj_bias,
    second_gain,
    second_shift,
    expand_weight,
    expand_bias,
    shrink_weight,
    shrink_bias,
    cotangent,
):
    token_rows, dim = tokens.shape
    sets = offsets.shape[0]
    part = qkv_weight.shape[2]
    ff = expand_weight.shape[1]
    chips = lax.axis_size("mp") // 2
    ring = Ring(lax.axis_size("dp"))
    dp_index = lax.axis_index("dp")
    mp_index = lax.axis_index("mp")
    x_index, core = mp_index // 2, mp_index % 2
    sets_x = -(-sets // chips)
    slots = sets_x * chips
    rows_x = sets_x * SET_ROWS
    half = rows_x // 2
    pairs = part // LANES
    groups = chips * pairs
    unit_rows = dim // ring.count
    unit = unit_rows // 2
    width = 3 * part
    att_width = groups * LANES
    near = [(0, 0), (0, 1)]
    far_other = [(step, 1) for step in range(1, chips)]
    far_own = [(step, 0) for step in range(1, chips)]
    keys = near + far_other + far_own
    sem = pltpu.SemaphoreType.DMA
    row = lambda value: value.reshape(1, -1)
    whole = lambda *dims: pl.BlockSpec(dims, lambda *_: (0,) * len(dims))

    row_starts = lax.dynamic_index_in_dim(ring.piece_rows(unit_rows), dp_index, 0, False)
    block_ranks = lax.dynamic_index_in_dim(ring.block_ranks(), dp_index, 0, False)
    places = [(x_index - step) % chips * 2 + (core ^ other) for step, other in keys]
    info = jnp.concatenate(
        [jnp.stack([core, x_index, *places]).astype(jnp.int32), row_starts, block_ranks]
    )
    place_base = 2
    base = place_base + len(keys)
    ranks = base + ring.count + 1

    order = Order(info)

    qkv_shard = qkv_weight.astype(bf16).reshape(unit_rows, 3, pairs, LANES)
    qkv_shard = qkv_shard.transpose(0, 2, 1, 3).reshape(unit_rows, width)
    shard = jnp.concatenate([qkv_shard, proj_weight.astype(bf16).T], axis=1)
    bias_shard = jnp.zeros((pairs, 3, LANES), f32)
    bias_shard = bias_shard.at[:, 0].set(qv_bias[0].reshape(pairs, LANES))
    bias_shard = bias_shard.at[:, 2].set(qv_bias[1].reshape(pairs, LANES)).reshape(1, width)
    high = bias_shard.astype(bf16)
    both = jnp.concatenate([high, (bias_shard - high.astype(f32)).astype(bf16)])
    below = jnp.pad(both, ((0, 14), (0, part)))
    joined = jnp.concatenate([shard, below])
    attn_steps = ring.gather_steps(shard, 0, order)
    attn_pieces = [shard]
    far_pieces = {step: [across(joined, step, chips)] for step in range(1, chips)}
    bias_x = [bias_shard]
    for step in range(1, chips):
        got = far_pieces[step][0][unit_rows : unit_rows + 2, :width].astype(f32)
        bias_x.append(got[0:1] + got[1:2])

    def next_step(steps, pieces):
        got = next(steps, None)
        if got is not None:
            pieces += got
        return got

    def send_far(got):
        joined = jnp.concatenate(order.after(got))
        for step in range(1, chips):
            far_pieces[step].append(across(joined, step, chips))

    def last_far(i=-1):
        return [far_pieces[step][i] for step in range(1, chips)]

    def pad_sets(value, wait):
        columns = pl.BlockSpec((token_rows, CHUNK), lambda i, _: (0, i))
        kernel = call(
            functools.partial(pad_body, sets=sets),
            (dim // CHUNK,),
            [columns],
            pl.BlockSpec((slots * SET_ROWS, CHUNK), lambda i, _: (0, i)),
            shape((slots * SET_ROWS, dim), bf16),
            [pltpu.VMEM((token_rows + 16, CHUNK), f32)],
            "pad",
        )
        return order.run(kernel, value, wait=wait)

    got = next_step(attn_steps, attn_pieces)
    order.due = last_far()
    after = next_step(attn_steps, attn_pieces)
    order.due = ()
    send_far(got)
    x_rows = pad_sets(tokens, ())
    order.due = last_far()
    got = next_step(attn_steps, attn_pieces)
    order.due = ()
    send_far(after)
    kernel = call(
        first_low_body,
        (sets_x,),
        [
            pl.BlockSpec((SET_ROWS, dim), lambda i, info: (info[1] * sets_x + i, 0)),
            whole(1, dim),
            whole(1, dim),
        ],
        pl.BlockSpec((SET_ROWS, dim), lambda i, _: (i, 0)),
        shape((rows_x, dim), bf16),
        [],
        "first_low",
    )
    first_low = order.run(kernel, x_rows, row(first_gain), row(first_shift))
    while got:
        order.due = last_far(-2)
        after = next_step(attn_steps, attn_pieces)
        if after is None:
            shrink_shard = tie(shrink_weight, far_pieces[1][0]).astype(bf16).T
            mlp_shard = jnp.concatenate([expand_weight.astype(bf16), shrink_shard], axis=1)
            mlp_pieces = [mlp_shard]
            mlp_steps = ring.gather_steps(tie(mlp_shard, got), 0, order)
            next_step(mlp_steps, mlp_pieces)
        order.due = ()
        send_far(got)
        got = after
    order.due = last_far(-2) + last_far()
    starts = tie(jnp.pad(offsets, ((0, slots - sets), (0, 0))), order.now)
    starts = lax.dynamic_slice_in_dim(starts, x_index * sets_x, sets_x, axis=0)
    positions = jnp.arange(SET_ROWS, dtype=jnp.int32)
    ids = jnp.sum((positions[None, :, None] >= starts[:, None, :]).astype(jnp.int32), axis=-1)
    ids = jnp.where(positions[None, :] < SET_TOKENS, ids, -1)
    key_ids, query_ids = ids[:, :, None], ids[:, None, :]
    cot = pad_sets(cotangent, (key_ids, query_ids))
    next_step(mlp_steps, mlp_pieces)
    order.due = ()
    count = len(attn_pieces)
    copies = count * chips
    far_list = [piece for step in range(1, chips) for piece in far_pieces[step]]

    joint = chips * (width + part)
    kernel = call(
        functools.partial(qkv_body, base=base, unit=unit, chips=chips, count=count),
        (2,),
        [pl.BlockSpec((half, dim), lambda i, _: (i, 0)), whole(1, chips * width)]
        + [ANY] * (count + len(far_list)),
        [pl.BlockSpec((half, chips * width), lambda i, _: (i, 0)), HBM],
        [shape((rows_x, chips * width), bf16), shape((dim, joint), bf16)],
        [pltpu.VMEM((dim, joint), bf16), sem((copies,)), sem],
        "qkv",
    )
    qkv, weights = order.run(kernel, first_low, jnp.concatenate(bias_x, axis=1), *attn_pieces, *far_list)
    order.due = mlp_pieces[-2:]
    both_weights = [weights, partner(order.after(weights), chips)]

    order.due = ()
    next_step(mlp_steps, mlp_pieces)
    kernel = call(
        attend_body,
        (sets_x, groups),
        [
            pl.BlockSpec((SET_ROWS, 3 * LANES), lambda s, i, _: (s, i)),
            pl.BlockSpec((1, SET_ROWS, 1), lambda s, i, _: (s, 0, 0)),
            pl.BlockSpec((1, 1, SET_ROWS), lambda s, i, _: (s, 0, 0)),
        ],
        [
            pl.BlockSpec((SET_ROWS, LANES), lambda s, i, _: (s, i)),
            pl.BlockSpec((1, 1, 2, SET_ROWS), lambda s, i, _: (s, i, 0, 0)),
        ],
        [
            shape((rows_x, att_width), bf16),
            shape((sets_x, groups, 2, SET_ROWS), f32),
        ],
        [pltpu.VMEM((SET_ROWS, SET_ROWS), f32)],
        "attend",
    )
    attended, logs = order.run(kernel, qkv, key_ids, query_ids)
    order.due = [*mlp_pieces[-2:], both_weights[1]]
    attended_other = partner(order.after(attended), chips)
    order.due = ()
    next_step(mlp_steps, mlp_pieces)

    own_half = lambda *dims: pl.BlockSpec(dims, lambda i, info: (info[0], 0))
    own_place = lambda *dims: pl.BlockSpec(dims, lambda i, info: (info[place_base], 0))
    proj_scratch = [pltpu.VMEM((dim, 2 * att_width), bf16), sem((2 * chips,))]
    kernel = call(
        functools.partial(proj_norm_body, chips=chips),
        (1,),
        [own_half(half, att_width)] * 2 + [own_place(half, dim)] + [whole(1, dim)] * 3 + [HBM] * 2,
        [whole(half, dim), whole(half, dim)],
        [shape((half, dim), f32), shape((half, dim), bf16)],
        proj_scratch,
        "proj_norm",
    )
    residual, second_low = order.run(
        kernel,
        attended,
        attended_other,
        x_rows,
        row(proj_bias),
        row(second_gain),
        row(second_shift),
        *both_weights,
    )
    seconds = {(0, 0): second_low}
    for step in range(1, chips):
        seconds[(step, 0)] = across(second_low, step, chips)
    order.due = mlp_pieces[-2:]
    seconds[(0, 1)] = partner(order.after(second_low), chips)
    order.due = ()
    while next_step(mlp_steps, mlp_pieces):
        pass

    def feed(group, gots=()):
        parts = len(group)
        first = keys.index(group[0])
        kernel = call(
            functools.partial(
                mlp_body, base=base, unit=unit, count=count, parts=parts, adds=len(gots)
            ),
            (parts,),
            [
                pl.BlockSpec((half, dim), lambda i, info: (info[place_base + first + i], 0)),
                whole(1, ff),
            ]
            + [HBM] * (count + parts)
            + [whole(half, dim)] * len(gots),
            [pl.BlockSpec((half, ff), lambda i, _: (i, 0))] * 2
            + [whole(half, dim)] * (2 * parts)
            + [whole(1, ff)],
            [shape((parts * half, ff), bf16)] * 2
            + [shape((half, dim), bf16)] * (2 * parts)
            + [shape((1, ff), f32)],
            [
                pltpu.VMEM((dim, ff), bf16),
                pltpu.VMEM((dim, ff), bf16),
                pltpu.VMEM((parts, half, dim), bf16),
                sem((2 * count,)),
                sem((parts,)),
            ],
            "mlp",
        )
        outs = order.run(
            kernel,
            cot,
            row(expand_bias),
            *mlp_pieces,
            *[seconds[key] for key in group],
            *gots,
        )
        backs, rows = outs[2 : 2 + parts], outs[2 + parts : 2 + 2 * parts]
        return outs[0], outs[1], list(backs), list(rows), outs[-1]

    first = feed(near)
    for step in range(1, chips):
        seconds[(step, 1)] = partner(order.after(seconds[(step, 0)]), chips)
    other = feed(far_other)
    own = feed(far_own, [partner(back, chips) for back in other[2]])
    feeds = [first, other, own]

    def along_x(own, sums):
        terms = [own[0], partner(own[1], chips)]
        return terms + [across(value, chips - 1 - i, chips) for i, value in enumerate(sums)]

    back_terms = along_x(first[2], own[2])
    span = 2 * CHUNK
    total_rows = len(keys) * half
    kernel = call(
        functools.partial(mlp_grad_body, cot_base=place_base, parts=len(keys), groups=3),
        (2, dim // span),
        [HBM] * (7 + len(keys)),
        pl.BlockSpec((span, ff), lambda p, i, _: (i, p)),
        shape((dim, 2 * ff), bf16),
        [
            pltpu.VMEM((2, total_rows, dim), bf16),
            pltpu.VMEM((2, total_rows, ff), bf16),
            sem((2, len(keys) + 3)),
        ],
        "mlp_grad",
    )
    mlp_grad = order.run(
        kernel,
        cot,
        *[seconds[key] for key in keys],
        *[outs[0] for outs in feeds],
        *[outs[1] for outs in feeds],
    )
    mlp_ring = ring.scatter_steps(mlp_grad, ranks, order)
    mlp_due = next(mlp_ring)

    step_rows = row_step(half)
    cot_rows = pl.BlockSpec(
        (step_rows, dim), lambda i, info: (info[place_base] * (half // step_rows) + i, 0)
    )
    plain_rows = lambda count: pl.BlockSpec((step_rows, count), lambda i, _: (i, 0))
    kernel = call(
        functools.partial(residual_back_body, parts=len(back_terms), chips=chips),
        (half // step_rows,),
        [plain_rows(dim), cot_rows, whole(1, dim)]
        + [plain_rows(dim)] * len(back_terms)
        + [HBM] * 2,
        [plain_rows(dim)] * 2 + [plain_rows(att_width)] * 2 + [whole(8, dim)],
        [
            shape((half, dim), f32),
            shape((half, dim), bf16),
            shape((half, att_width), bf16),
            shape((half, att_width), bf16),
            shape((8, dim), f32),
        ],
        proj_scratch,
        "residual_back",
    )
    grad_residual, residual_low, grad_own, grad_send, sums_two = order.run(
        kernel, residual, cot, row(second_gain), *back_terms, *both_weights
    )
    order.due = mlp_due
    grad_got = partner(order.after(grad_send), chips)
    residual_other = partner(order.after(residual_low), chips)
    order.due = ()
    mlp_due = next(mlp_ring)
    if chips == 2:
        out_near = order.after(residual) + shrink_bias + first[3][0].astype(f32)
        out_near = (out_near + partner(order.after(first[3][1]), chips).astype(f32)).astype(bf16)
        out_far = own[3][0].astype(f32)
        out_far = (out_far + partner(other[3][0], chips).astype(f32)).astype(bf16)
        out_rows = jnp.concatenate([out_far, out_near])
        cuts = [0, half // 16 * 8, half * 5 // 32 * 8, 2 * half]
        out_sends = iter([out_rows[i:j] for i, j in zip(cuts, cuts[1:])])
        out_gots = [across(order.after(next(out_sends)), 1, chips)]
    else:
        out_own = [
            (mine.astype(f32) + partner(order.after(got), chips).astype(f32)).astype(bf16)
            for mine, got in zip(own[3], other[3])
        ]
        out_terms = along_x(order.after(first[3]), out_own)

    def attend_back(b):
        half_block = lambda j: pl.BlockSpec(
            (row_step(half), LANES), lambda i, s, _: (lax.rem(2 * s + j, sets_x), b * pairs + i)
        )
        kernel = call(
            functools.partial(attend_back_body, first_half=sets_x),
            (pairs, sets_x),
            [
                pl.BlockSpec((SET_ROWS, 3 * LANES), lambda i, s, _: (s, b * pairs + i)),
                pl.BlockSpec((1, SET_ROWS, 1), lambda i, s, _: (s, 0, 0)),
                pl.BlockSpec((1, 1, SET_ROWS), lambda i, s, _: (s, 0, 0)),
                pl.BlockSpec((1, 1, 2, SET_ROWS), lambda i, s, _: (s, b * pairs + i, 0, 0)),
                half_block(0),
                half_block(0),
                half_block(1),
                half_block(1),
            ],
            [
                pl.BlockSpec((SET_ROWS, 3 * LANES), lambda i, s, _: (s, i)),
                pl.BlockSpec((1, 1, 3 * LANES), lambda i, s, _: (i, 0, 0)),
            ],
            [shape((rows_x, width), bf16), shape((pairs, 1, 3 * LANES), f32)],
            [pltpu.VMEM((sets_x, SET_ROWS, SET_ROWS), f32)],
            "attend_back",
        )
        ids = key_ids, query_ids
        return order.run(kernel, qkv, *ids, logs, grad_own, grad_got, grad_own, grad_got)

    def qkv_grad(b, before):
        columns = lambda count: pl.BlockSpec((count, CHUNK), lambda i, _: (0, i))
        kernel = call(
            qkv_grad_body,
            (dim // CHUNK,),
            [
                columns(rows_x),
                whole(rows_x, width),
                columns(half),
                columns(half),
                pl.BlockSpec((half, part), lambda i, info: (info[0], b)),
                pl.BlockSpec((half, part), lambda i, info: (1 - info[0], b)),
            ]
            + [ANY] * len(before),
            pl.BlockSpec((CHUNK, width + part), lambda i, _: (i, b)),
            shape((dim, joint), bf16),
            [],
            "qkv_grad",
            {7 + i: i for i in range(len(before))},
        )
        return order.run(
            kernel,
            first_low,
            grads_qkv[b],
            residual_low,
            residual_other,
            attended,
            attended,
            *before,
        )

    def out_due(i):
        if chips != 2:
            return ()
        if i < 2:
            out_gots.append(across(order.after(next(out_sends)), 1, chips))
        return out_gots[i]

    grads_qkv, grads_other, qkv_sums, begun = {}, {}, {}, ()
    for b in range(1, chips):
        grads_qkv[b], qkv_sums[b] = attend_back(b)
        order.due = mlp_due, residual_other, out_due(b - 1)
        grads_other[b] = partner(order.after(grads_qkv[b]), chips)
        order.due = ()
        mlp_due = next(mlp_ring, ())
        begun = (qkv_grad(b, begun),)
    grads_qkv[0], qkv_sums[0] = attend_back(0)
    order.due = mlp_due, [grads_other[b] for b in range(1, chips)], out_due(1)
    grads_other[0] = partner(order.after(grads_qkv[0]), chips)
    order.due = ()
    mlp_due = next(mlp_ring, ())
    attn_ring = ring.scatter_steps(qkv_grad(0, begun), ranks, order, "ring_end")
    order.due = [grads_other[b] for b in range(chips)]
    order.hold = next(attn_ring)
    order.due = ()
    for mlp_grad in mlp_ring:
        pass
    expand_part, shrink_part = mlp_grad[:, :ff], mlp_grad[:, ff:].T
    out_due(2)
    if chips == 2:
        out_rows = jnp.concatenate([out_near, out_far]).astype(f32)
        out_rows = out_rows + jnp.concatenate(order.after(out_gots)).astype(f32)
    else:
        out_rows = order.after(residual) + shrink_bias
        for term in out_terms:
            out_rows = out_rows + term.astype(f32)
        low = out_rows.astype(bf16)
        out_rows = jnp.concatenate([low] + [across(low, step, chips) for step in range(1, chips)])
    out_rows = out_rows.astype(bf16)
    order.hold = out_rows
    attn_due = next(attn_ring)

    kernel = call(
        functools.partial(first_norm_body, chips=chips),
        (1,),
        [own_half(half, width)] * (2 * chips)
        + [own_place(half, dim), whole(half, dim), whole(1, dim), whole(8, dim)]
        + [whole(pairs, 1, 3 * LANES)] * chips
        + [whole(1, ff)] * 3
        + [HBM] * 2,
        [whole(half, dim), whole(8, dim)],
        [shape((half, dim), bf16), shape((8, dim), f32)],
        [
            pltpu.VMEM((2 * chips, dim, width), bf16),
            pltpu.VMEM((2 * chips, half, width), bf16),
            pltpu.VMEM((half, dim), f32),
            sem((2 * chips,)),
        ],
        "first_norm",
    )
    tokens_low, small = order.run(
        kernel,
        *[grads_qkv[b] for b in range(chips)],
        *[grads_other[b] for b in range(chips)],
        x_rows,
        grad_residual,
        row(first_gain),
        sums_two,
        *[qkv_sums[b] for b in range(chips)],
        first[4],
        other[4],
        own[4],
        *both_weights,
    )

    def assemble(rows, dtype):
        block = lambda count, at: pl.BlockSpec((count, CHUNK), lambda i, _: (at, i))
        kernel = call(
            functools.partial(assemble_body, base=place_base, sets=sets),
            (dim // CHUNK,),
            [block(half, rows[key][1]) for key in keys],
            block(token_rows, 0),
            shape((token_rows, dim), dtype),
            [
                pltpu.VMEM((slots * SET_ROWS, CHUNK), f32),
                pltpu.VMEM((token_rows + 16, CHUNK), f32),
            ],
            "assemble",
        )
        return order.run(kernel, *[rows[key][0] for key in keys])

    bits = [1 << i for i in range(ring.count.bit_length() - 1)]

    def from_rank(small, bit):
        return lax.ppermute(small, "dp", [(r, r ^ bit) for r in range(ring.count)])

    def add_chips(small):
        shared = small[:6] + partner(small[:6], chips)
        own, *others = small[6:7].reshape(chips, 2 * part)
        if chips == 2:
            sent = jnp.concatenate([shared.reshape(-1), others[0]])
            got = across(sent, 1, chips)
            shared = shared + got[: 6 * dim].reshape(6, dim)
            own = own + got[6 * dim :]
        else:
            bit = 1
            while bit < chips:
                flips = [(m, m ^ (2 * bit)) for m in range(2 * chips)]
                shared = shared + lax.ppermute(shared, "mp", flips)
                bit *= 2
            for step in range(1, chips):
                own = own + across(others[step - 1], chips - step, chips)
        own = jnp.pad(own, (0, dim - 2 * part)).reshape(1, dim)
        return jnp.concatenate([shared, own, small[7:]])

    order.due = attn_due
    tokens_low = order.after(tokens_low)
    grads, outs = {(0, 0): (tokens_low, 0)}, {}
    for step in range(1, chips):
        grads[(step, 0)] = across(tokens_low, step, chips), 0
    order.due = ()
    next(attn_ring)
    out_other = partner(order.after(out_rows), chips)
    for step in range(chips):
        outs[(step, 0)], outs[(step, 1)] = (out_rows, step), (out_other, step)

    got = from_rank(order.after(small), bits[0])
    outputs = assemble(outs, bf16)
    small = small + order.after(got)
    order.hold = (expand_part, shrink_part)
    order.due = small
    next(attn_ring)
    order.due = ()
    grads[(0, 1)] = partner(order.after(tokens_low), chips), 0
    for step in range(1, chips):
        grads[(step, 1)] = partner(order.after(grads[(step, 0)][0]), chips), 0
    small = add_chips(order.after(small))
    for attn_sum in attn_ring:
        pass
    small = order.after(small)
    attn_low = order.after(attn_sum.astype(bf16))
    sent = {}
    for step in range(1, chips):
        columns = slice(step * (width + part), (step + 1) * (width + part))
        sent[step] = across(attn_low[:, columns], chips - step, chips)
    got = from_rank(small, bits[1])
    grad_tokens = assemble(grads, f32)
    small = small + order.after(got)
    for bit in bits[2:]:
        small = small + from_rank(small, bit)
    shared = small[:6]
    bias_own = small[6, : 2 * part].reshape(2, part)
    expand_bias_grad = small[7:].reshape(-1)[:ff]
    attn_part = attn_sum[:, : width + part]
    for step in range(1, chips):
        attn_part = attn_part + order.after(sent[step]).astype(f32)

    qkv_part = attn_part[:, :width].reshape(unit_rows, pairs, 3, LANES)
    qkv_part = qkv_part.transpose(0, 2, 1, 3).reshape(unit_rows, 3, part)
    return (
        outputs,
        grad_tokens,
        shared[0],
        shared[1],
        qkv_part,
        bias_own,
        attn_part[:, width:].T,
        shared[2],
        shared[3],
        shared[4],
        expand_part,
        expand_bias_grad,
        shrink_part,
        shared[5],
    )


def solution(mesh):
    placed = (
        P("dp", None),
        P("dp", None),
        P(),
        P(),
        P("dp", None, "mp"),
        P(None, "mp"),
        P("mp", "dp"),
        P(),
        P(),
        P(),
        P("dp", "mp"),
        P("mp"),
        P("mp", "dp"),
        P(),
        P("dp", None),
    )
    return jax.shard_map(
        shards,
        mesh=mesh,
        in_specs=placed,
        out_specs=(
            P("dp", None),
            P("dp", None),
            P(),
            P(),
            P("dp", None, "mp"),
            P(None, "mp"),
            P("mp", "dp"),
            P(),
            P(),
            P(),
            P("dp", "mp"),
            P("mp"),
            P("mp", "dp"),
            P(),
        ),
        check_vma=False,
    )
```

```python
import functools

import jax
import jax.numpy as jnp
import numpy as np
from jax import lax
from jax.experimental import pallas as pl
from jax.experimental.pallas import tpu as pltpu
from jax.sharding import PartitionSpec as P

HEAD_DIM = 64
SET_TOKENS = 345
SET_ROWS = 352
LANES = 128
CHUNK = 256

norm_eps = 1e-06
masked_score = -1e30
root_half = 0.7071067811865476
density_scale = 0.3989422804014327
f32 = jnp.float32
bf16 = jnp.bfloat16
NN = (((1,), (0,)), ((), ()))
NT = (((1,), (1,)), ((), ()))
TN = (((0,), (0,)), ((), ()))
ANY = pl.BlockSpec(memory_space=pl.ANY)
HBM = pl.BlockSpec(memory_space=pltpu.HBM)


def dot(left, right, dims=NN):
    return lax.dot_general(left, right, dims, preferred_element_type=f32)


ROOM = {
    "ring_first": 4,
    "ring_add": 10,
    "ring_last": 8,
    "ring_end": 8,
    "qkv": 20,
    "pad": 20,
    "assemble": 58,
    "first_low": 10,
    "attend": 10,
    "attend_back": 12,
    "proj_norm": 20,
    "mlp": 58,
    "mlp_grad": 54,
    "residual_back": 16,
    "qkv_grad": 20,
    "first_norm": 54,
}


COST = {"ring_end": 2 * 10**10}


def call(body, grid, in_specs, out_specs, out_shape, scratch, name, aliases=None):
    return pl.pallas_call(
        body,
        grid_spec=pltpu.PrefetchScalarGridSpec(
            num_scalar_prefetch=1,
            grid=grid,
            in_specs=in_specs,
            out_specs=out_specs,
            scratch_shapes=scratch,
        ),
        out_shape=out_shape,
        compiler_params=pltpu.CompilerParams(
            dimension_semantics=("arbitrary",) * len(grid), vmem_limit_bytes=ROOM[name] * 2**20
        ),
        cost_estimate=pl.CostEstimate(
            flops=COST.get(name, 1), bytes_accessed=1, transcendentals=0
        ),
        name=name,
        input_output_aliases=aliases or {},
    )


def tie(value, *earlier):
    return lax.optimization_barrier((value, earlier))[0]


class Order:
    def __init__(self, info):
        self.info = info
        self.now = info
        self.due = ()
        self.hold = ()

    def after(self, value):
        return tie(value, self.now, self.due)

    def run(self, kernel, *values, wait=()):
        out = kernel(tie(self.info, self.now, wait, self.hold), *values)
        self.hold = ()
        self.now = out[0] if isinstance(out, (list, tuple)) else out
        return out


def shape(dims, dtype):
    return jax.ShapeDtypeStruct(tuple(dims), dtype)


def ring_order(count):
    width = 1
    while 2 * (2 * width) ** 2 <= count:
        width *= 2
    length = count // width
    if width == 1:
        return list(range(count))
    path = []
    for z in range(length):
        columns = range(1, width) if z % 2 == 0 else range(width - 1, 0, -1)
        path += [z * width + y for y in columns]
    path += [z * width for z in range(length - 1, -1, -1)]
    return path


class Ring:
    def __init__(self, count):
        self.count = count
        self.order = ring_order(count)
        self.place = {rank: i for i, rank in enumerate(self.order)}
        self.ahead = [(self.order[i], self.order[(i + 1) % count]) for i in range(count)]
        self.behind = [(self.order[i], self.order[(i - 1) % count]) for i in range(count)]

    def rank_at(self, rank, offset):
        return self.order[(self.place[rank] + offset) % self.count]

    def send_ahead(self, value):
        return lax.ppermute(value, "dp", self.ahead)

    def send_behind(self, value):
        return lax.ppermute(value, "dp", self.behind)

    def gather_steps(self, block, axis, order):
        half = block.shape[axis] // 2
        forward = backward = block
        for step in range(1, self.count // 2 + 1):
            if step == self.count // 2:
                forward = lax.slice_in_dim(forward, 0, half, axis=axis)
                backward = lax.slice_in_dim(backward, half, 2 * half, axis=axis)
            forward, backward = order.after((forward, backward))
            forward = self.send_ahead(forward)
            backward = self.send_behind(backward)
            yield forward, backward

    def piece_rows(self, rows):
        table = []
        middle = self.count // 2
        for rank in range(self.count):
            starts = [rank * rows]
            for step in range(1, middle + 1):
                ahead = self.rank_at(rank, -step) * rows
                behind = self.rank_at(rank, step) * rows
                if step == middle:
                    behind += rows // 2
                starts += [ahead, behind]
            table.append(starts)
        return np.array(table, np.int32)

    def block_ranks(self):
        middle = self.count // 2
        return np.array(
            [
                [self.rank_at(rank, d) for d in range(-middle, middle + 1)]
                for rank in range(self.count)
            ],
            np.int32,
        )

    def scatter_steps(self, whole, ranks, order, last="ring_last"):
        middle = self.count // 2
        dim, columns = whole.shape
        rows = dim // self.count
        half = rows // 2
        wide = columns
        grid = (columns // wide,)
        block = lambda d: pl.BlockSpec((rows, wide), lambda j, info: (info[ranks + middle + d], j))
        plain = lambda count: pl.BlockSpec((count, wide), lambda j, _: (0, j))
        kernel = call(
            ring_first_body,
            grid,
            [
                pl.BlockSpec((half, wide), lambda j, info: (2 * info[ranks + 2 * middle], j)),
                pl.BlockSpec((half, wide), lambda j, info: (2 * info[ranks] + 1, j)),
            ],
            [plain(half)] * 2,
            [shape((half, columns), bf16)] * 2,
            [],
            "ring_first",
        )
        forward, backward = order.run(kernel, whole, whole)
        for step in range(1, middle + 1):
            forward = self.send_ahead(order.after(forward))
            backward = self.send_behind(order.after(backward))
            yield forward, backward
            near = middle - step
            if near == 0:
                break
            kernel = call(
                ring_add_body,
                grid,
                [block(near), block(-near)] + [plain(forward.shape[0])] * 2,
                [plain(rows)] * 2,
                [shape((rows, columns), bf16)] * 2,
                [],
                "ring_add",
            )
            forward, backward = order.run(kernel, whole, whole, forward, backward)
        kernel = call(
            ring_last_body,
            grid,
            [block(0)] + [plain(rows)] * 2,
            plain(rows),
            shape((rows, columns), f32),
            [],
            last,
        )
        yield order.run(kernel, whole, forward, backward)


def across(value, step, chips):
    pairs = [
        (x * 2 + core, (x + step) % chips * 2 + core) for x in range(chips) for core in range(2)
    ]
    return lax.ppermute(value, "mp", pairs)


def partner(value, chips):
    return lax.ppermute(value, "mp", [(m, m ^ 1) for m in range(2 * chips)])


def layer_norm(values, gain, shift):
    centre = jnp.mean(values, axis=-1, keepdims=True)
    offset_rows = values - centre
    spread = jnp.mean(offset_rows * offset_rows, axis=-1, keepdims=True)
    return offset_rows * lax.rsqrt(spread + norm_eps) * gain + shift


def start_all(copies, sems):
    moves = [pltpu.make_async_copy(src, dst, sems.at[i]) for i, (src, dst) in enumerate(copies)]
    for move in moves:
        move.start()
    return moves


def wait_all(moves):
    for move in moves:
        move.wait()


def weight_copies(info, base, pieces, unit, targets):
    copies = []
    for i, piece in enumerate(pieces):
        rows = piece.shape[-2]
        place = pl.ds(pl.multiple_of(info[base + i], unit), rows)
        for source, target in targets:
            copies.append((source(piece), target(place)))
    return copies


def ring_first_body(info, ahead_ref, behind_ref, ahead_out, behind_out):
    ahead_out[...] = ahead_ref[...]
    behind_out[...] = behind_ref[...]


def ring_add_body(info, ahead_ref, behind_ref, got_ahead, got_behind, ahead_out, behind_out):
    rows, part = ahead_out.shape[0], got_ahead.shape[0]
    first, last = slice(0, part), slice(rows - part, rows)
    total = ahead_ref[first, :].astype(f32) + got_ahead[...].astype(f32)
    ahead_out[first, :] = total.astype(bf16)
    total = behind_ref[last, :].astype(f32) + got_behind[...].astype(f32)
    behind_out[last, :] = total.astype(bf16)
    if part < rows:
        ahead_out[part:, :] = ahead_ref[part:, :]
        behind_out[: rows - part, :] = behind_ref[: rows - part, :]


def ring_last_body(info, own_ref, got_ahead, got_behind, out_ref):
    both = got_ahead[...].astype(f32) + got_behind[...].astype(f32)
    out_ref[...] = own_ref[...].astype(f32) + both


def qkv_body(info, x_ref, bias_ref, *rest, base, unit, chips, count):
    steps = count // 2 + 1
    own, rest = rest[:count], rest[count:]
    far, (out_ref, whole_ref, weights, sems, out_sem) = (
        rest[: steps * (chips - 1)],
        rest[steps * (chips - 1) :],
    )
    part = weights.shape[1] // chips
    width = out_ref.shape[1] // chips
    keep = pltpu.make_async_copy(weights, whole_ref, out_sem)

    @pl.when(pl.program_id(0) == 0)
    def _():
        copies = []
        for b in range(chips):
            for i, piece in enumerate(own):
                rows = piece.shape[0]
                source = piece
                if b:
                    joined = far[(b - 1) * steps + (i + 1) // 2]
                    source = joined.at[pl.ds(rows if i and i % 2 == 0 else 0, rows)]
                place = pl.ds(pl.multiple_of(info[base + i], unit), rows)
                copies.append((source, weights.at[place, pl.ds(b * part, part)]))
        wait_all(start_all(copies, sems))
        keep.start()

    def columns(b, _):
        to = pl.ds(pl.multiple_of(b * width, LANES), width)
        product = dot(x_ref[...], weights[:, pl.ds(pl.multiple_of(b * part, LANES), width)])
        out_ref[:, to] = (product + bias_ref[:, to]).astype(bf16)
        return 0

    lax.fori_loop(0, chips, columns, 0)

    @pl.when(pl.program_id(0) == pl.num_programs(0) - 1)
    def _():
        keep.wait()


def pad_body(info, in_ref, out_ref, rows, *, sets):
    total = in_ref.shape[0]
    rows[0:total, :] = in_ref[...].astype(f32)
    inside = lax.broadcasted_iota(jnp.int32, (SET_ROWS, 1), 0) < SET_TOKENS
    for g in range(out_ref.shape[0] // SET_ROWS):
        to = slice(g * SET_ROWS, (g + 1) * SET_ROWS)
        if g < sets:
            value = rows[g * SET_TOKENS : g * SET_TOKENS + SET_ROWS, :]
            out_ref[to, :] = jnp.where(inside, value, 0.0).astype(bf16)
        else:
            out_ref[to, :] = jnp.zeros((SET_ROWS, out_ref.shape[1]), bf16)


def assemble_body(info, *refs, base, sets):
    pieces, (out_ref, padded, packed) = refs[:-3], refs[-3:]
    half = pieces[0].shape[0]
    for i, piece in enumerate(pieces):
        place = pl.ds(pl.multiple_of(info[base + i] * half, 16), half)
        padded[place, :] = piece[...].astype(f32)
    target = out_ref if out_ref.dtype == f32 else packed
    for g in range(sets):
        target[g * SET_TOKENS : (g + 1) * SET_TOKENS, :] = padded[
            g * SET_ROWS : g * SET_ROWS + SET_TOKENS, :
        ]
    if out_ref.dtype != f32:
        out_ref[...] = packed[0 : out_ref.shape[0], :].astype(out_ref.dtype)


def first_low_body(info, x_ref, gain_ref, shift_ref, out_ref):
    out_ref[...] = layer_norm(x_ref[...].astype(f32), gain_ref[...], shift_ref[...]).astype(bf16)


def head_mask(head):
    lane = lax.broadcasted_iota(jnp.int32, (1, LANES), 1)
    return (lane < HEAD_DIM) if head == 0 else (lane >= HEAD_DIM)


def keep_head(value, head):
    return jnp.where(head_mask(head), value, jnp.zeros_like(value))


def attend_body(info, qkv_ref, key_ids, query_ids, out_ref, log_ref, block):
    @pl.when(pl.program_id(1) == 0)
    def _():
        block[...] = jnp.where(key_ids[0] == query_ids[0], 0.0, masked_score)

    factor = HEAD_DIM**-0.5
    query = qkv_ref[:, 0:LANES] * jnp.asarray(factor, bf16)
    key = qkv_ref[:, LANES : 2 * LANES]
    value = qkv_ref[:, 2 * LANES : 3 * LANES]
    halves = []
    for head in range(2):
        scores = dot(key, keep_head(query, head), NT) + block[...]
        peak = jnp.max(scores, axis=0, keepdims=True)
        raised = jnp.exp(scores - peak)
        total = jnp.sum(raised, axis=0, keepdims=True)
        mixed = dot(keep_head(value, head), raised.astype(bf16), TN)
        halves.append(mixed * (1.0 / total))
        log_ref[0, 0, head : head + 1, :] = peak + jnp.log(total)
    out_ref[...] = (halves[0] + halves[1]).T.astype(bf16)


def attend_back_body(info, qkv_ref, key_ids, query_ids, log_ref, *rest, first_half):
    grads = rest[:4]
    out_ref, sum_ref, block = rest[-3:]
    turn = pl.program_id(1)

    @pl.when(pl.program_id(0) == 0)
    def _():
        block[turn] = jnp.where(key_ids[0] == query_ids[0], 0.0, masked_score)

    factor = HEAD_DIM**-0.5
    query = qkv_ref[:, 0:LANES] * jnp.asarray(factor, bf16)
    key = qkv_ref[:, LANES : 2 * LANES]
    value = qkv_ref[:, 2 * LANES : 3 * LANES]
    parts = []
    for j in range(2):
        core = ((2 * turn + j) >= first_half).astype(jnp.int32)
        parts.append(jnp.where(core == info[0], grads[2 * j][...], grads[2 * j + 1][...]))
    grad = jnp.concatenate(parts, axis=0)
    grad_query = grad_key = grad_value = 0.0
    for head in range(2):
        query_one = keep_head(query, head)
        grad_one = keep_head(grad, head)
        scores = dot(key, query_one, NT) + block[turn]
        weights = jnp.exp(scores - log_ref[0, 0, head : head + 1, :])
        grad_value += dot(weights.astype(bf16), grad_one)
        grad_weights = dot(value, grad_one, NT)
        centre = jnp.sum(weights * grad_weights, axis=0, keepdims=True)
        low = (weights * (grad_weights - centre)).astype(bf16)
        grad_key += dot(low, query_one)
        grad_query += dot(keep_head(key, head), low, TN)
    grad_query = (grad_query * factor).T
    out_ref[:, 0:LANES] = grad_query.astype(bf16)
    out_ref[:, LANES : 2 * LANES] = grad_key.astype(bf16)
    out_ref[:, 2 * LANES : 3 * LANES] = grad_value.astype(bf16)

    @pl.when(turn == 0)
    def _():
        sum_ref[...] = jnp.zeros_like(sum_ref)

    sum_ref[0, :, 0:LANES] += jnp.sum(grad_query, axis=0, keepdims=True)
    sum_ref[0, :, 2 * LANES : 3 * LANES] += jnp.sum(grad_value, axis=0, keepdims=True)


def proj_moves(wholes, weights, chips, sems):
    width = weights.shape[1] // (2 * chips)
    part = wholes[0].shape[1] // chips
    copies = []
    for j, source in enumerate(wholes):
        for b in range(chips):
            columns = pl.ds((b + 1) * part - width, width)
            target = pl.ds((j * chips + b) * width, width)
            copies.append((source.at[:, columns], weights.at[:, target]))
    return [pltpu.make_async_copy(src, dst, sems.at[i]) for i, (src, dst) in enumerate(copies)]


def proj_norm_body(
    info, own_ref, got_ref, x_ref, bias_ref, gain_ref, shift_ref, *rest, chips
):
    wholes, (residual_ref, low_ref, weights, sems) = rest[:2], rest[2:]
    moves = proj_moves(wholes, weights, chips, sems)
    for move in moves:
        move.start()
    wait_all(moves)
    width = own_ref.shape[1]
    span = 2 * CHUNK

    def columns(i, _):
        at = pl.ds(pl.multiple_of(i * span, span), span)
        own_part = dot(own_ref[...], weights[at, :width], NT)
        residual_ref[:, at] = own_part + dot(got_ref[...], weights[at, width:], NT)
        return 0

    lax.fori_loop(0, residual_ref.shape[1] // span, columns, 0)
    step = row_step(residual_ref.shape[0])

    def rows(i, _):
        at = pl.ds(pl.multiple_of(i * step, 16), step)
        value = residual_ref[at, :] + x_ref[at, :].astype(f32) + bias_ref[...]
        residual_ref[at, :] = value
        low_ref[at, :] = layer_norm(value, gain_ref[...], shift_ref[...]).astype(bf16)
        return 0

    lax.fori_loop(0, residual_ref.shape[0] // step, rows, 0)


def row_step(rows):
    return 176 if rows % 176 == 0 else rows


def mlp_body(info, cot_ref, bias_ref, *rest, base, unit, count, parts, adds):
    pieces, rest = rest[:count], rest[count:]
    seconds, rest = rest[:parts], rest[parts:]
    gots, rest = rest[:adds], rest[adds:]
    hidden_ref, pre_ref, rest = rest[0], rest[1], rest[2:]
    backs, outs, rest = rest[:parts], rest[parts : 2 * parts], rest[2 * parts :]
    sum_ref, expand, shrink, rows, sems, row_sems = rest
    width = expand.shape[1]
    turn = pl.program_id(0)

    @pl.when(turn == 0)
    def _():
        targets = [
            (
                lambda piece: piece.at[:, pl.ds(0, width)],
                lambda place: expand.at[place, :],
            ),
            (
                lambda piece: piece.at[:, pl.ds(width, width)],
                lambda place: shrink.at[place, :],
            ),
        ]
        moves = start_all(weight_copies(info, base, pieces, unit, targets), sems)
        start_all([(seconds[i], rows.at[i]) for i in range(parts)], row_sems)
        wait_all(moves)
        sum_ref[...] = jnp.zeros_like(sum_ref)

    pltpu.make_async_copy(seconds[0], rows.at[turn], row_sems.at[turn]).wait()
    span = 2 * CHUNK if width % (2 * CHUNK) == 0 else LANES

    def columns(i, _):
        at = pl.ds(pl.multiple_of(i * span, span), span)
        pre = dot(rows[turn], expand[:, at]) + bias_ref[:, at]
        below = 0.5 * (1.0 + lax.erf(pre * root_half))
        density = density_scale * jnp.exp(-0.5 * pre * pre)
        hidden_ref[:, at] = (pre * below).astype(bf16)
        grad = dot(cot_ref[...], shrink[:, at]) * (below + pre * density)
        sum_ref[:, at] += jnp.sum(grad, axis=0, keepdims=True)
        pre_ref[:, at] = grad.astype(bf16)
        return 0

    lax.fori_loop(0, width // span, columns, 0)

    def back(i, _):
        at = pl.ds(pl.multiple_of(i * span, span), span)
        for targets, left, right, kind in (
            (backs, pre_ref, expand, 0),
            (outs, hidden_ref, shrink, 1),
        ):
            product = dot(left[...], right[at, :], NT)
            for i in range(parts):

                @pl.when(turn == i)
                def _(i=i, targets=targets, product=product, kind=kind):
                    total = product
                    if adds and kind == 0:
                        total = total + gots[i][:, at].astype(f32)
                    targets[i][:, at] = total.astype(bf16)

        return 0

    lax.fori_loop(0, backs[0].shape[1] // span, back, 0)


def mlp_grad_body(info, cot_ref, *rest, cot_base, parts, groups):
    seconds, rest = rest[:parts], rest[parts:]
    hiddens, pres, rest = rest[:groups], rest[groups : 2 * groups], rest[2 * groups :]
    out_ref, left, right, sems = rest
    phase = pl.program_id(0)
    rows = left.shape[1] // parts
    span = out_ref.shape[0]

    def moves(index):
        pairs = []
        for i in range(parts):
            source = seconds[i]
            if index == 1:
                place = pl.multiple_of(info[cot_base + i] * rows, 16)
                source = cot_ref.at[pl.ds(place, rows)]
            pairs.append((source, left.at[index, pl.ds(i * rows, rows)]))
        start = 0
        for source in (pres, hiddens)[index]:
            pairs.append((source, right.at[index, pl.ds(start, source.shape[0])]))
            start += source.shape[0]
        return [
            pltpu.make_async_copy(src, dst, sems.at[index, i]) for i, (src, dst) in enumerate(pairs)
        ]

    @pl.when((phase == 0) & (pl.program_id(1) == 0))
    def _():
        for index in range(2):
            for move in moves(index):
                move.start()

    for index in range(2):

        @pl.when((phase == index) & (pl.program_id(1) == 0))
        def _(index=index):
            wait_all(moves(index))

    at = pl.ds(pl.multiple_of(pl.program_id(1) * span, span), span)
    out_ref[...] = dot(left[phase, :, at], right[phase], TN).astype(bf16)


def norm_back(value, grad, gain):
    centred = value - jnp.mean(value, axis=-1, keepdims=True)
    spread = jnp.mean(centred * centred, axis=-1, keepdims=True)
    scale = lax.rsqrt(spread + norm_eps)
    normal = centred * scale
    weighted = grad * gain
    middle = jnp.mean(weighted, axis=-1, keepdims=True)
    slope = jnp.mean(weighted * normal, axis=-1, keepdims=True)
    return normal, scale * (weighted - middle - normal * slope)


def residual_back_body(info, residual_ref, cot_ref, gain_ref, *rest, parts, chips):
    grads, rest = rest[:parts], rest[parts:]
    wholes, (grad_ref, low_ref, own_ref, send_ref, sum_ref, weights, sems) = rest[:2], rest[2:]
    moves = proj_moves(wholes, weights, chips, sems)

    @pl.when(pl.program_id(0) == 0)
    def _():
        for move in moves:
            move.start()
        sum_ref[...] = jnp.zeros_like(sum_ref)

    grad = grads[0][...].astype(f32)
    for other in grads[1:]:
        grad += other[...].astype(f32)
    normal, back = norm_back(residual_ref[...], grad, gain_ref[...])
    cotangent = cot_ref[...].astype(f32)
    total = cotangent + back
    grad_ref[...] = total
    low_ref[...] = total.astype(bf16)
    sum_ref[0:1, :] += jnp.sum(grad * normal, axis=0, keepdims=True)
    sum_ref[1:2, :] += jnp.sum(grad, axis=0, keepdims=True)
    sum_ref[2:3, :] += jnp.sum(total, axis=0, keepdims=True)
    sum_ref[3:4, :] += jnp.sum(cotangent, axis=0, keepdims=True)

    @pl.when(pl.program_id(0) == 0)
    def _():
        wait_all(moves)

    both = dot(low_ref[...], weights[...]).astype(bf16)
    width = own_ref.shape[1]
    own_ref[...] = both[:, :width]
    send_ref[...] = both[:, width:]


def qkv_grad_body(info, first_ref, grad_ref, own_ref, got_ref, att_own, att_got, *rest):
    out_ref = rest[-1]
    width = grad_ref.shape[1]
    out_ref[:, :width] = dot(first_ref[...], grad_ref[...], TN).astype(bf16)
    out_ref[:, width:] = (
        dot(own_ref[...], att_own[...], TN) + dot(got_ref[...], att_got[...], TN)
    ).astype(bf16)


def first_norm_body(info, *refs, chips):
    grads, (x_ref, res_ref, gain_ref, *rest) = refs[: 2 * chips], refs[2 * chips :]
    two_ref, biases, hiddens, rest = rest[0], rest[1 : 1 + chips], rest[1 + chips : 4 + chips], rest[4 + chips :]
    wholes, (low_ref, sum_ref, weights, lefts, total, sems) = rest[:2], rest[2:]
    half, width = lefts.shape[1:]
    part = wholes[0].shape[1] // chips

    def move(i):
        return pltpu.make_async_copy(
            wholes[i // chips].at[:, pl.ds(i % chips * part, width)], weights.at[i], sems.at[i]
        )

    for i in range(2 * chips):
        move(i).start()
    for i in range(2 * chips):
        lefts[i] = grads[i][...]
    total[...] = jnp.zeros_like(total)

    def term(i, _):
        pltpu.make_async_copy(
            wholes[0].at[:, pl.ds(0, width)], weights.at[i], sems.at[i]
        ).wait()
        total[...] += dot(lefts[i], weights[i], NT)
        return 0

    lax.fori_loop(0, 2 * chips, term, 0)
    step = row_step(total.shape[0])
    sum_ref[...] = jnp.zeros_like(sum_ref)
    for i, j in enumerate((2, 0, 1, 3)):
        sum_ref[2 + i : 3 + i, :] = two_ref[j : j + 1, :]
    pairs = biases[0].shape[0]
    for b in range(chips):
        for kind in range(2):
            for pair in range(pairs):
                to = ((b * 2 + kind) * pairs + pair) * LANES
                value = biases[b][pair, :, kind * 2 * LANES : (kind * 2 + 1) * LANES]
                sum_ref[6:7, to : to + LANES] = value
    ff = hiddens[0].shape[1]
    sum_ref[7:8, 0:ff] = hiddens[0][...] + hiddens[1][...] + hiddens[2][...]

    def rows(i, _):
        at = pl.ds(pl.multiple_of(i * step, 16), step)
        grad = total[at, :]
        normal, back = norm_back(x_ref[at, :].astype(f32), grad, gain_ref[...])
        low_ref[at, :] = (back + res_ref[at, :]).astype(bf16)
        sum_ref[0:1, :] += jnp.sum(grad * normal, axis=0, keepdims=True)
        sum_ref[1:2, :] += jnp.sum(grad, axis=0, keepdims=True)
        return 0

    lax.fori_loop(0, total.shape[0] // step, rows, 0)


def shards(
    tokens,
    offsets,
    first_gain,
    first_shift,
    qkv_weight,
    qv_bias,
    proj_weight,
    proj_bias,
    second_gain,
    second_shift,
    expand_weight,
    expand_bias,
    shrink_weight,
    shrink_bias,
    cotangent,
):
    token_rows, dim = tokens.shape
    sets = offsets.shape[0]
    part = qkv_weight.shape[2]
    ff = expand_weight.shape[1]
    chips = lax.axis_size("mp") // 2
    ring = Ring(lax.axis_size("dp"))
    dp_index = lax.axis_index("dp")
    mp_index = lax.axis_index("mp")
    x_index, core = mp_index // 2, mp_index % 2
    sets_x = -(-sets // chips)
    slots = sets_x * chips
    rows_x = sets_x * SET_ROWS
    half = rows_x // 2
    pairs = part // LANES
    groups = chips * pairs
    unit_rows = dim // ring.count
    unit = unit_rows // 2
    width = 3 * part
    att_width = groups * LANES
    near = [(0, 0), (0, 1)]
    far_other = [(step, 1) for step in range(1, chips)]
    far_own = [(step, 0) for step in range(1, chips)]
    keys = near + far_other + far_own
    sem = pltpu.SemaphoreType.DMA
    row = lambda value: value.reshape(1, -1)
    whole = lambda *dims: pl.BlockSpec(dims, lambda *_: (0,) * len(dims))

    row_starts = lax.dynamic_index_in_dim(ring.piece_rows(unit_rows), dp_index, 0, False)
    block_ranks = lax.dynamic_index_in_dim(ring.block_ranks(), dp_index, 0, False)
    places = [(x_index - step) % chips * 2 + (core ^ other) for step, other in keys]
    info = jnp.concatenate(
        [jnp.stack([core, x_index, *places]).astype(jnp.int32), row_starts, block_ranks]
    )
    place_base = 2
    base = place_base + len(keys)
    ranks = base + ring.count + 1

    order = Order(info)

    qkv_shard = qkv_weight.astype(bf16).reshape(unit_rows, 3, pairs, LANES)
    qkv_shard = qkv_shard.transpose(0, 2, 1, 3).reshape(unit_rows, width)
    shard = jnp.concatenate([qkv_shard, proj_weight.astype(bf16).T], axis=1)
    bias_shard = jnp.zeros((pairs, 3, LANES), f32)
    bias_shard = bias_shard.at[:, 0].set(qv_bias[0].reshape(pairs, LANES))
    bias_shard = bias_shard.at[:, 2].set(qv_bias[1].reshape(pairs, LANES)).reshape(1, width)
    high = bias_shard.astype(bf16)
    both = jnp.concatenate([high, (bias_shard - high.astype(f32)).astype(bf16)])
    below = jnp.pad(both, ((0, 14), (0, part)))
    joined = jnp.concatenate([shard, below])
    attn_steps = ring.gather_steps(shard, 0, order)
    attn_pieces = [shard]
    far_pieces = {step: [across(joined, step, chips)] for step in range(1, chips)}
    bias_x = [bias_shard]
    for step in range(1, chips):
        got = far_pieces[step][0][unit_rows : unit_rows + 2, :width].astype(f32)
        bias_x.append(got[0:1] + got[1:2])

    def next_step(steps, pieces):
        got = next(steps, None)
        if got is not None:
            pieces += got
        return got

    def send_far(got):
        joined = jnp.concatenate(order.after(got))
        for step in range(1, chips):
            far_pieces[step].append(across(joined, step, chips))

    def last_far(i=-1):
        return [far_pieces[step][i] for step in range(1, chips)]

    def pad_sets(value, wait):
        columns = pl.BlockSpec((token_rows, CHUNK), lambda i, _: (0, i))
        kernel = call(
            functools.partial(pad_body, sets=sets),
            (dim // CHUNK,),
            [columns],
            pl.BlockSpec((slots * SET_ROWS, CHUNK), lambda i, _: (0, i)),
            shape((slots * SET_ROWS, dim), bf16),
            [pltpu.VMEM((token_rows + 16, CHUNK), f32)],
            "pad",
        )
        return order.run(kernel, value, wait=wait)

    got = next_step(attn_steps, attn_pieces)
    order.due = last_far()
    after = next_step(attn_steps, attn_pieces)
    order.due = ()
    send_far(got)
    x_rows = pad_sets(tokens, ())
    order.due = last_far()
    got = next_step(attn_steps, attn_pieces)
    order.due = ()
    send_far(after)
    kernel = call(
        first_low_body,
        (sets_x,),
        [
            pl.BlockSpec((SET_ROWS, dim), lambda i, info: (info[1] * sets_x + i, 0)),
            whole(1, dim),
            whole(1, dim),
        ],
        pl.BlockSpec((SET_ROWS, dim), lambda i, _: (i, 0)),
        shape((rows_x, dim), bf16),
        [],
        "first_low",
    )
    first_low = order.run(kernel, x_rows, row(first_gain), row(first_shift))
    while got:
        order.due = last_far(-2)
        after = next_step(attn_steps, attn_pieces)
        if after is None:
            shrink_shard = tie(shrink_weight, far_pieces[1][0]).astype(bf16).T
            mlp_shard = jnp.concatenate([expand_weight.astype(bf16), shrink_shard], axis=1)
            mlp_pieces = [mlp_shard]
            mlp_steps = ring.gather_steps(tie(mlp_shard, got), 0, order)
            next_step(mlp_steps, mlp_pieces)
        order.due = ()
        send_far(got)
        got = after
    order.due = last_far(-2) + last_far()
    starts = tie(jnp.pad(offsets, ((0, slots - sets), (0, 0))), order.now)
    starts = lax.dynamic_slice_in_dim(starts, x_index * sets_x, sets_x, axis=0)
    positions = jnp.arange(SET_ROWS, dtype=jnp.int32)
    ids = jnp.sum((positions[None, :, None] >= starts[:, None, :]).astype(jnp.int32), axis=-1)
    ids = jnp.where(positions[None, :] < SET_TOKENS, ids, -1)
    key_ids, query_ids = ids[:, :, None], ids[:, None, :]
    cot = pad_sets(cotangent, (key_ids, query_ids))
    next_step(mlp_steps, mlp_pieces)
    order.due = ()
    count = len(attn_pieces)
    copies = count * chips
    far_list = [piece for step in range(1, chips) for piece in far_pieces[step]]

    joint = chips * (width + part)
    kernel = call(
        functools.partial(qkv_body, base=base, unit=unit, chips=chips, count=count),
        (2,),
        [pl.BlockSpec((half, dim), lambda i, _: (i, 0)), whole(1, chips * width)]
        + [ANY] * (count + len(far_list)),
        [pl.BlockSpec((half, chips * width), lambda i, _: (i, 0)), HBM],
        [shape((rows_x, chips * width), bf16), shape((dim, joint), bf16)],
        [pltpu.VMEM((dim, joint), bf16), sem((copies,)), sem],
        "qkv",
    )
    qkv, weights = order.run(kernel, first_low, jnp.concatenate(bias_x, axis=1), *attn_pieces, *far_list)
    order.due = mlp_pieces[-2:]
    both_weights = [weights, partner(order.after(weights), chips)]

    order.due = ()
    next_step(mlp_steps, mlp_pieces)
    kernel = call(
        attend_body,
        (sets_x, groups),
        [
            pl.BlockSpec((SET_ROWS, 3 * LANES), lambda s, i, _: (s, i)),
            pl.BlockSpec((1, SET_ROWS, 1), lambda s, i, _: (s, 0, 0)),
            pl.BlockSpec((1, 1, SET_ROWS), lambda s, i, _: (s, 0, 0)),
        ],
        [
            pl.BlockSpec((SET_ROWS, LANES), lambda s, i, _: (s, i)),
            pl.BlockSpec((1, 1, 2, SET_ROWS), lambda s, i, _: (s, i, 0, 0)),
        ],
        [
            shape((rows_x, att_width), bf16),
            shape((sets_x, groups, 2, SET_ROWS), f32),
        ],
        [pltpu.VMEM((SET_ROWS, SET_ROWS), f32)],
        "attend",
    )
    attended, logs = order.run(kernel, qkv, key_ids, query_ids)
    order.due = [*mlp_pieces[-2:], both_weights[1]]
    attended_other = partner(order.after(attended), chips)
    order.due = ()
    next_step(mlp_steps, mlp_pieces)

    own_half = lambda *dims: pl.BlockSpec(dims, lambda i, info: (info[0], 0))
    own_place = lambda *dims: pl.BlockSpec(dims, lambda i, info: (info[place_base], 0))
    proj_scratch = [pltpu.VMEM((dim, 2 * att_width), bf16), sem((2 * chips,))]
    kernel = call(
        functools.partial(proj_norm_body, chips=chips),
        (1,),
        [own_half(half, att_width)] * 2 + [own_place(half, dim)] + [whole(1, dim)] * 3 + [HBM] * 2,
        [whole(half, dim), whole(half, dim)],
        [shape((half, dim), f32), shape((half, dim), bf16)],
        proj_scratch,
        "proj_norm",
    )
    residual, second_low = order.run(
        kernel,
        attended,
        attended_other,
        x_rows,
        row(proj_bias),
        row(second_gain),
        row(second_shift),
        *both_weights,
    )
    seconds = {(0, 0): second_low}
    for step in range(1, chips):
        seconds[(step, 0)] = across(second_low, step, chips)
    order.due = mlp_pieces[-2:]
    seconds[(0, 1)] = partner(order.after(second_low), chips)
    order.due = ()
    while next_step(mlp_steps, mlp_pieces):
        pass

    def feed(group, gots=()):
        parts = len(group)
        first = keys.index(group[0])
        kernel = call(
            functools.partial(
                mlp_body, base=base, unit=unit, count=count, parts=parts, adds=len(gots)
            ),
            (parts,),
            [
                pl.BlockSpec((half, dim), lambda i, info: (info[place_base + first + i], 0)),
                whole(1, ff),
            ]
            + [HBM] * (count + parts)
            + [whole(half, dim)] * len(gots),
            [pl.BlockSpec((half, ff), lambda i, _: (i, 0))] * 2
            + [whole(half, dim)] * (2 * parts)
            + [whole(1, ff)],
            [shape((parts * half, ff), bf16)] * 2
            + [shape((half, dim), bf16)] * (2 * parts)
            + [shape((1, ff), f32)],
            [
                pltpu.VMEM((dim, ff), bf16),
                pltpu.VMEM((dim, ff), bf16),
                pltpu.VMEM((parts, half, dim), bf16),
                sem((2 * count,)),
                sem((parts,)),
            ],
            "mlp",
        )
        outs = order.run(
            kernel,
            cot,
            row(expand_bias),
            *mlp_pieces,
            *[seconds[key] for key in group],
            *gots,
        )
        backs, rows = outs[2 : 2 + parts], outs[2 + parts : 2 + 2 * parts]
        return outs[0], outs[1], list(backs), list(rows), outs[-1]

    first = feed(near)
    for step in range(1, chips):
        seconds[(step, 1)] = partner(order.after(seconds[(step, 0)]), chips)
    other = feed(far_other)
    own = feed(far_own, [partner(back, chips) for back in other[2]])
    feeds = [first, other, own]

    def along_x(own, sums):
        terms = [own[0], partner(own[1], chips)]
        return terms + [across(value, chips - 1 - i, chips) for i, value in enumerate(sums)]

    back_terms = along_x(first[2], own[2])
    span = 2 * CHUNK
    total_rows = len(keys) * half
    kernel = call(
        functools.partial(mlp_grad_body, cot_base=place_base, parts=len(keys), groups=3),
        (2, dim // span),
        [HBM] * (7 + len(keys)),
        pl.BlockSpec((span, ff), lambda p, i, _: (i, p)),
        shape((dim, 2 * ff), bf16),
        [
            pltpu.VMEM((2, total_rows, dim), bf16),
            pltpu.VMEM((2, total_rows, ff), bf16),
            sem((2, len(keys) + 3)),
        ],
        "mlp_grad",
    )
    mlp_grad = order.run(
        kernel,
        cot,
        *[seconds[key] for key in keys],
        *[outs[0] for outs in feeds],
        *[outs[1] for outs in feeds],
    )
    mlp_ring = ring.scatter_steps(mlp_grad, ranks, order)
    mlp_due = next(mlp_ring)

    if chips == 2:
        out_far = own[3][0].astype(f32)
        out_far = (out_far + partner(other[3][0], chips).astype(f32)).astype(bf16)
        out_near = order.after(residual) + shrink_bias + first[3][0].astype(f32)
        out_near = (out_near + partner(first[3][1], chips).astype(f32)).astype(bf16)
        order.hold = out_far, out_near
    step_rows = row_step(half)
    cot_rows = pl.BlockSpec(
        (step_rows, dim), lambda i, info: (info[place_base] * (half // step_rows) + i, 0)
    )
    plain_rows = lambda count: pl.BlockSpec((step_rows, count), lambda i, _: (i, 0))
    kernel = call(
        functools.partial(residual_back_body, parts=len(back_terms), chips=chips),
        (half // step_rows,),
        [plain_rows(dim), cot_rows, whole(1, dim)]
        + [plain_rows(dim)] * len(back_terms)
        + [HBM] * 2,
        [plain_rows(dim)] * 2 + [plain_rows(att_width)] * 2 + [whole(8, dim)],
        [
            shape((half, dim), f32),
            shape((half, dim), bf16),
            shape((half, att_width), bf16),
            shape((half, att_width), bf16),
            shape((8, dim), f32),
        ],
        proj_scratch,
        "residual_back",
    )
    grad_residual, residual_low, grad_own, grad_send, sums_two = order.run(
        kernel, residual, cot, row(second_gain), *back_terms, *both_weights
    )
    order.due = mlp_due
    grad_got = partner(order.after(grad_send), chips)
    residual_other = partner(order.after(residual_low), chips)
    order.due = ()
    mlp_due = next(mlp_ring)
    if chips == 2:
        out_rows = jnp.concatenate([out_far, out_near])
        cuts = [0, half // 16 * 8, half * 5 // 32 * 8, 2 * half]
        out_sends = iter([out_rows[i:j] for i, j in zip(cuts, cuts[1:])])
        out_gots = [across(order.after(next(out_sends)), 1, chips)]
    else:
        out_own = [
            (mine.astype(f32) + partner(order.after(got), chips).astype(f32)).astype(bf16)
            for mine, got in zip(own[3], other[3])
        ]
        out_terms = along_x(order.after(first[3]), out_own)

    def attend_back(b):
        half_block = lambda j: pl.BlockSpec(
            (row_step(half), LANES), lambda i, s, _: (lax.rem(2 * s + j, sets_x), b * pairs + i)
        )
        kernel = call(
            functools.partial(attend_back_body, first_half=sets_x),
            (pairs, sets_x),
            [
                pl.BlockSpec((SET_ROWS, 3 * LANES), lambda i, s, _: (s, b * pairs + i)),
                pl.BlockSpec((1, SET_ROWS, 1), lambda i, s, _: (s, 0, 0)),
                pl.BlockSpec((1, 1, SET_ROWS), lambda i, s, _: (s, 0, 0)),
                pl.BlockSpec((1, 1, 2, SET_ROWS), lambda i, s, _: (s, b * pairs + i, 0, 0)),
                half_block(0),
                half_block(0),
                half_block(1),
                half_block(1),
            ],
            [
                pl.BlockSpec((SET_ROWS, 3 * LANES), lambda i, s, _: (s, i)),
                pl.BlockSpec((1, 1, 3 * LANES), lambda i, s, _: (i, 0, 0)),
            ],
            [shape((rows_x, width), bf16), shape((pairs, 1, 3 * LANES), f32)],
            [pltpu.VMEM((sets_x, SET_ROWS, SET_ROWS), f32)],
            "attend_back",
        )
        ids = key_ids, query_ids
        return order.run(kernel, qkv, *ids, logs, grad_own, grad_got, grad_own, grad_got)

    def qkv_grad(b, before):
        columns = lambda count: pl.BlockSpec((count, CHUNK), lambda i, _: (0, i))
        kernel = call(
            qkv_grad_body,
            (dim // CHUNK,),
            [
                columns(rows_x),
                whole(rows_x, width),
                columns(half),
                columns(half),
                pl.BlockSpec((half, part), lambda i, info: (info[0], b)),
                pl.BlockSpec((half, part), lambda i, info: (1 - info[0], b)),
            ]
            + [ANY] * len(before),
            pl.BlockSpec((CHUNK, width + part), lambda i, _: (i, b)),
            shape((dim, joint), bf16),
            [],
            "qkv_grad",
            {7 + i: i for i in range(len(before))},
        )
        return order.run(
            kernel,
            first_low,
            grads_qkv[b],
            residual_low,
            residual_other,
            attended,
            attended,
            *before,
        )

    def out_due(i):
        if chips != 2:
            return ()
        if i < 2:
            out_gots.append(across(order.after(next(out_sends)), 1, chips))
        return out_gots[i]

    grads_qkv, grads_other, qkv_sums, begun = {}, {}, {}, ()
    for b in range(1, chips):
        grads_qkv[b], qkv_sums[b] = attend_back(b)
        order.due = mlp_due, residual_other, out_due(b - 1)
        grads_other[b] = partner(order.after(grads_qkv[b]), chips)
        order.due = ()
        mlp_due = next(mlp_ring, ())
        begun = (qkv_grad(b, begun),)
    grads_qkv[0], qkv_sums[0] = attend_back(0)
    order.due = mlp_due, [grads_other[b] for b in range(1, chips)], out_due(1)
    grads_other[0] = partner(order.after(grads_qkv[0]), chips)
    order.due = ()
    mlp_due = next(mlp_ring, ())
    attn_ring = ring.scatter_steps(qkv_grad(0, begun), ranks, order, "ring_end")
    order.due = [grads_other[b] for b in range(chips)]
    order.hold = next(attn_ring)
    order.due = ()
    for mlp_grad in mlp_ring:
        pass
    expand_part, shrink_part = mlp_grad[:, :ff], mlp_grad[:, ff:].T
    out_due(2)
    if chips == 2:
        out_rows = jnp.concatenate([out_near, out_far]).astype(f32)
        out_rows = out_rows + jnp.concatenate(order.after(out_gots)).astype(f32)
    else:
        out_rows = order.after(residual) + shrink_bias
        for term in out_terms:
            out_rows = out_rows + term.astype(f32)
        low = out_rows.astype(bf16)
        out_rows = jnp.concatenate([low] + [across(low, step, chips) for step in range(1, chips)])
    out_rows = out_rows.astype(bf16)
    order.hold = out_rows
    attn_due = next(attn_ring)

    kernel = call(
        functools.partial(first_norm_body, chips=chips),
        (1,),
        [own_half(half, width)] * (2 * chips)
        + [own_place(half, dim), whole(half, dim), whole(1, dim), whole(8, dim)]
        + [whole(pairs, 1, 3 * LANES)] * chips
        + [whole(1, ff)] * 3
        + [HBM] * 2,
        [whole(half, dim), whole(8, dim)],
        [shape((half, dim), bf16), shape((8, dim), f32)],
        [
            pltpu.VMEM((2 * chips, dim, width), bf16),
            pltpu.VMEM((2 * chips, half, width), bf16),
            pltpu.VMEM((half, dim), f32),
            sem((2 * chips,)),
        ],
        "first_norm",
    )
    tokens_low, small = order.run(
        kernel,
        *[grads_qkv[b] for b in range(chips)],
        *[grads_other[b] for b in range(chips)],
        x_rows,
        grad_residual,
        row(first_gain),
        sums_two,
        *[qkv_sums[b] for b in range(chips)],
        first[4],
        other[4],
        own[4],
        *both_weights,
    )

    def assemble(rows, dtype):
        block = lambda count, at: pl.BlockSpec((count, CHUNK), lambda i, _: (at, i))
        kernel = call(
            functools.partial(assemble_body, base=place_base, sets=sets),
            (dim // CHUNK,),
            [block(half, rows[key][1]) for key in keys],
            block(token_rows, 0),
            shape((token_rows, dim), dtype),
            [
                pltpu.VMEM((slots * SET_ROWS, CHUNK), f32),
                pltpu.VMEM((token_rows + 16, CHUNK), f32),
            ],
            "assemble",
        )
        return order.run(kernel, *[rows[key][0] for key in keys])

    bits = [1 << i for i in range(ring.count.bit_length() - 1)]

    def from_rank(small, bit):
        return lax.ppermute(small, "dp", [(r, r ^ bit) for r in range(ring.count)])

    def add_chips(small):
        shared = small[:6] + partner(small[:6], chips)
        own, *others = small[6:7].reshape(chips, 2 * part)
        if chips == 2:
            sent = jnp.concatenate([shared.reshape(-1), others[0]])
            got = across(sent, 1, chips)
            shared = shared + got[: 6 * dim].reshape(6, dim)
            own = own + got[6 * dim :]
        else:
            bit = 1
            while bit < chips:
                flips = [(m, m ^ (2 * bit)) for m in range(2 * chips)]
                shared = shared + lax.ppermute(shared, "mp", flips)
                bit *= 2
            for step in range(1, chips):
                own = own + across(others[step - 1], chips - step, chips)
        own = jnp.pad(own, (0, dim - 2 * part)).reshape(1, dim)
        return jnp.concatenate([shared, own, small[7:]])

    order.due = attn_due
    tokens_low = order.after(tokens_low)
    grads, outs = {(0, 0): (tokens_low, 0)}, {}
    for step in range(1, chips):
        grads[(step, 0)] = across(tokens_low, step, chips), 0
    order.due = ()
    next(attn_ring)
    out_other = partner(order.after(out_rows), chips)
    for step in range(chips):
        outs[(step, 0)], outs[(step, 1)] = (out_rows, step), (out_other, step)

    got = from_rank(order.after(small), bits[0])
    outputs = assemble(outs, bf16)
    small = small + order.after(got)
    order.hold = (expand_part, shrink_part)
    order.due = small
    next(attn_ring)
    order.due = ()
    grads[(0, 1)] = partner(order.after(tokens_low), chips), 0
    for step in range(1, chips):
        grads[(step, 1)] = partner(order.after(grads[(step, 0)][0]), chips), 0
    small = add_chips(order.after(small))
    for attn_sum in attn_ring:
        pass
    small = order.after(small)
    attn_low = order.after(attn_sum.astype(bf16))
    sent = {}
    for step in range(1, chips):
        columns = slice(step * (width + part), (step + 1) * (width + part))
        sent[step] = across(attn_low[:, columns], chips - step, chips)
    got = from_rank(small, bits[1])
    grad_tokens = assemble(grads, f32)
    small = small + order.after(got)
    for bit in bits[2:]:
        small = small + from_rank(small, bit)
    shared = small[:6]
    bias_own = small[6, : 2 * part].reshape(2, part)
    expand_bias_grad = small[7:].reshape(-1)[:ff]
    attn_part = attn_sum[:, : width + part]
    for step in range(1, chips):
        attn_part = attn_part + order.after(sent[step]).astype(f32)

    qkv_part = attn_part[:, :width].reshape(unit_rows, pairs, 3, LANES)
    qkv_part = qkv_part.transpose(0, 2, 1, 3).reshape(unit_rows, 3, part)
    return (
        outputs,
        grad_tokens,
        shared[0],
        shared[1],
        qkv_part,
        bias_own,
        attn_part[:, width:].T,
        shared[2],
        shared[3],
        shared[4],
        expand_part,
        expand_bias_grad,
        shrink_part,
        shared[5],
    )


def solution(mesh):
    placed = (
        P("dp", None),
        P("dp", None),
        P(),
        P(),
        P("dp", None, "mp"),
        P(None, "mp"),
        P("mp", "dp"),
        P(),
        P(),
        P(),
        P("dp", "mp"),
        P("mp"),
        P("mp", "dp"),
        P(),
        P("dp", None),
    )
    return jax.shard_map(
        shards,
        mesh=mesh,
        in_specs=placed,
        out_specs=(
            P("dp", None),
            P("dp", None),
            P(),
            P(),
            P("dp", None, "mp"),
            P(None, "mp"),
            P("mp", "dp"),
            P(),
            P(),
            P(),
            P("dp", "mp"),
            P("mp"),
            P("mp", "dp"),
            P(),
        ),
        check_vma=False,
    )
```

```python
import functools

import jax
import jax.numpy as jnp
import numpy as np
from jax import lax
from jax.experimental import pallas as pl
from jax.experimental.pallas import tpu as pltpu
from jax.sharding import PartitionSpec as P

HEAD_DIM = 64
SET_TOKENS = 345
SET_ROWS = 352
LANES = 128
CHUNK = 256

norm_eps = 1e-06
masked_score = -1e30
root_half = 0.7071067811865476
density_scale = 0.3989422804014327
f32 = jnp.float32
bf16 = jnp.bfloat16
NN = (((1,), (0,)), ((), ()))
NT = (((1,), (1,)), ((), ()))
TN = (((0,), (0,)), ((), ()))
ANY = pl.BlockSpec(memory_space=pl.ANY)
HBM = pl.BlockSpec(memory_space=pltpu.HBM)


def dot(left, right, dims=NN):
    return lax.dot_general(left, right, dims, preferred_element_type=f32)


ROOM = {
    "ring_first": 4,
    "ring_add": 10,
    "ring_last": 8,
    "ring_end": 8,
    "qkv": 20,
    "pad": 20,
    "assemble": 58,
    "first_low": 10,
    "attend": 10,
    "attend_back": 12,
    "proj_norm": 20,
    "mlp": 58,
    "mlp_grad": 54,
    "residual_back": 16,
    "qkv_grad": 20,
    "first_norm": 54,
}


COST = {"ring_end": 2 * 10**10}


def call(body, grid, in_specs, out_specs, out_shape, scratch, name, aliases=None):
    return pl.pallas_call(
        body,
        grid_spec=pltpu.PrefetchScalarGridSpec(
            num_scalar_prefetch=1,
            grid=grid,
            in_specs=in_specs,
            out_specs=out_specs,
            scratch_shapes=scratch,
        ),
        out_shape=out_shape,
        compiler_params=pltpu.CompilerParams(
            dimension_semantics=("arbitrary",) * len(grid), vmem_limit_bytes=ROOM[name] * 2**20
        ),
        cost_estimate=pl.CostEstimate(
            flops=COST.get(name, 1), bytes_accessed=1, transcendentals=0
        ),
        name=name,
        input_output_aliases=aliases or {},
    )


def tie(value, *earlier):
    return lax.optimization_barrier((value, earlier))[0]


class Order:
    def __init__(self, info):
        self.info = info
        self.now = info
        self.due = ()
        self.hold = ()

    def after(self, value):
        return tie(value, self.now, self.due)

    def run(self, kernel, *values, wait=()):
        out = kernel(tie(self.info, self.now, wait, self.hold), *values)
        self.hold = ()
        self.now = out[0] if isinstance(out, (list, tuple)) else out
        return out


def shape(dims, dtype):
    return jax.ShapeDtypeStruct(tuple(dims), dtype)


def ring_order(count):
    width = 1
    while 2 * (2 * width) ** 2 <= count:
        width *= 2
    length = count // width
    if width == 1:
        return list(range(count))
    path = []
    for z in range(length):
        columns = range(1, width) if z % 2 == 0 else range(width - 1, 0, -1)
        path += [z * width + y for y in columns]
    path += [z * width for z in range(length - 1, -1, -1)]
    return path


class Ring:
    def __init__(self, count):
        self.count = count
        self.order = ring_order(count)
        self.place = {rank: i for i, rank in enumerate(self.order)}
        self.ahead = [(self.order[i], self.order[(i + 1) % count]) for i in range(count)]
        self.behind = [(self.order[i], self.order[(i - 1) % count]) for i in range(count)]

    def rank_at(self, rank, offset):
        return self.order[(self.place[rank] + offset) % self.count]

    def send_ahead(self, value):
        return lax.ppermute(value, "dp", self.ahead)

    def send_behind(self, value):
        return lax.ppermute(value, "dp", self.behind)

    def gather_steps(self, block, axis, order):
        half = block.shape[axis] // 2
        forward = backward = block
        for step in range(1, self.count // 2 + 1):
            if step == self.count // 2:
                forward = lax.slice_in_dim(forward, 0, half, axis=axis)
                backward = lax.slice_in_dim(backward, half, 2 * half, axis=axis)
            forward, backward = order.after((forward, backward))
            forward = self.send_ahead(forward)
            backward = self.send_behind(backward)
            yield forward, backward

    def piece_rows(self, rows):
        table = []
        middle = self.count // 2
        for rank in range(self.count):
            starts = [rank * rows]
            for step in range(1, middle + 1):
                ahead = self.rank_at(rank, -step) * rows
                behind = self.rank_at(rank, step) * rows
                if step == middle:
                    behind += rows // 2
                starts += [ahead, behind]
            table.append(starts)
        return np.array(table, np.int32)

    def block_ranks(self):
        middle = self.count // 2
        return np.array(
            [
                [self.rank_at(rank, d) for d in range(-middle, middle + 1)]
                for rank in range(self.count)
            ],
            np.int32,
        )

    def scatter_steps(self, whole, ranks, order, last="ring_last"):
        middle = self.count // 2
        dim, columns = whole.shape
        rows = dim // self.count
        half = rows // 2
        wide = columns
        grid = (columns // wide,)
        block = lambda d: pl.BlockSpec((rows, wide), lambda j, info: (info[ranks + middle + d], j))
        plain = lambda count: pl.BlockSpec((count, wide), lambda j, _: (0, j))
        kernel = call(
            ring_first_body,
            grid,
            [
                pl.BlockSpec((half, wide), lambda j, info: (2 * info[ranks + 2 * middle], j)),
                pl.BlockSpec((half, wide), lambda j, info: (2 * info[ranks] + 1, j)),
            ],
            [plain(half)] * 2,
            [shape((half, columns), bf16)] * 2,
            [],
            "ring_first",
        )
        forward, backward = order.run(kernel, whole, whole)
        for step in range(1, middle + 1):
            forward = self.send_ahead(order.after(forward))
            backward = self.send_behind(order.after(backward))
            yield forward, backward
            near = middle - step
            if near == 0:
                break
            final = near == 1
            kernel = call(
                ring_add_body,
                grid,
                [block(near), block(-near)] + [block(0)] * final + [plain(forward.shape[0])] * 2,
                [plain(rows)] * (2 + final),
                [shape((rows, columns), bf16)] * (2 + final),
                [],
                "ring_add",
            )
            forward, backward, *own = order.run(kernel, *[whole] * (2 + final), forward, backward)
        kernel = call(
            ring_last_body,
            grid,
            [plain(rows)] * 3,
            plain(rows),
            shape((rows, columns), f32),
            [],
            last,
        )
        yield order.run(kernel, *own, forward, backward)


def across(value, step, chips):
    pairs = [
        (x * 2 + core, (x + step) % chips * 2 + core) for x in range(chips) for core in range(2)
    ]
    return lax.ppermute(value, "mp", pairs)


def partner(value, chips):
    return lax.ppermute(value, "mp", [(m, m ^ 1) for m in range(2 * chips)])


def layer_norm(values, gain, shift):
    centre = jnp.mean(values, axis=-1, keepdims=True)
    offset_rows = values - centre
    spread = jnp.mean(offset_rows * offset_rows, axis=-1, keepdims=True)
    return offset_rows * lax.rsqrt(spread + norm_eps) * gain + shift


def start_all(copies, sems):
    moves = [pltpu.make_async_copy(src, dst, sems.at[i]) for i, (src, dst) in enumerate(copies)]
    for move in moves:
        move.start()
    return moves


def wait_all(moves):
    for move in moves:
        move.wait()


def weight_copies(info, base, pieces, unit, targets):
    copies = []
    for i, piece in enumerate(pieces):
        rows = piece.shape[-2]
        place = pl.ds(pl.multiple_of(info[base + i], unit), rows)
        for source, target in targets:
            copies.append((source(piece), target(place)))
    return copies


def ring_first_body(info, ahead_ref, behind_ref, ahead_out, behind_out):
    ahead_out[...] = ahead_ref[...]
    behind_out[...] = behind_ref[...]


def ring_add_body(info, ahead_ref, behind_ref, *rest):
    if len(rest) == 6:
        own_ref, *rest, own_out = rest
        own_out[...] = own_ref[...]
    got_ahead, got_behind, ahead_out, behind_out = rest
    rows, part = ahead_out.shape[0], got_ahead.shape[0]
    first, last = slice(0, part), slice(rows - part, rows)
    total = ahead_ref[first, :].astype(f32) + got_ahead[...].astype(f32)
    ahead_out[first, :] = total.astype(bf16)
    total = behind_ref[last, :].astype(f32) + got_behind[...].astype(f32)
    behind_out[last, :] = total.astype(bf16)
    if part < rows:
        ahead_out[part:, :] = ahead_ref[part:, :]
        behind_out[: rows - part, :] = behind_ref[: rows - part, :]


def ring_last_body(info, own_ref, got_ahead, got_behind, out_ref):
    both = got_ahead[...].astype(f32) + got_behind[...].astype(f32)
    out_ref[...] = own_ref[...].astype(f32) + both


def qkv_body(info, x_ref, bias_ref, *rest, base, unit, chips, count):
    steps = count // 2 + 1
    own, rest = rest[:count], rest[count:]
    far, (out_ref, whole_ref, weights, sems, out_sem) = (
        rest[: steps * (chips - 1)],
        rest[steps * (chips - 1) :],
    )
    part = weights.shape[1] // chips
    width = out_ref.shape[1] // chips
    keep = pltpu.make_async_copy(weights, whole_ref, out_sem)

    @pl.when(pl.program_id(0) == 0)
    def _():
        copies = []
        for b in range(chips):
            for i, piece in enumerate(own):
                rows = piece.shape[0]
                source = piece
                if b:
                    joined = far[(b - 1) * steps + (i + 1) // 2]
                    source = joined.at[pl.ds(rows if i and i % 2 == 0 else 0, rows)]
                place = pl.ds(pl.multiple_of(info[base + i], unit), rows)
                copies.append((source, weights.at[place, pl.ds(b * part, part)]))
        wait_all(start_all(copies, sems))
        keep.start()

    def columns(b, _):
        to = pl.ds(pl.multiple_of(b * width, LANES), width)
        product = dot(x_ref[...], weights[:, pl.ds(pl.multiple_of(b * part, LANES), width)])
        out_ref[:, to] = (product + bias_ref[:, to]).astype(bf16)
        return 0

    lax.fori_loop(0, chips, columns, 0)

    @pl.when(pl.program_id(0) == pl.num_programs(0) - 1)
    def _():
        keep.wait()


def pad_body(info, in_ref, out_ref, rows, *, sets):
    total = in_ref.shape[0]
    rows[0:total, :] = in_ref[...].astype(f32)
    inside = lax.broadcasted_iota(jnp.int32, (SET_ROWS, 1), 0) < SET_TOKENS
    for g in range(out_ref.shape[0] // SET_ROWS):
        to = slice(g * SET_ROWS, (g + 1) * SET_ROWS)
        if g < sets:
            value = rows[g * SET_TOKENS : g * SET_TOKENS + SET_ROWS, :]
            out_ref[to, :] = jnp.where(inside, value, 0.0).astype(bf16)
        else:
            out_ref[to, :] = jnp.zeros((SET_ROWS, out_ref.shape[1]), bf16)


def assemble_body(info, *refs, base, sets):
    pieces, (out_ref, padded, packed) = refs[:-3], refs[-3:]
    half = pieces[0].shape[0]
    for i, piece in enumerate(pieces):
        place = pl.ds(pl.multiple_of(info[base + i] * half, 16), half)
        padded[place, :] = piece[...].astype(f32)
    target = out_ref if out_ref.dtype == f32 else packed
    for g in range(sets):
        target[g * SET_TOKENS : (g + 1) * SET_TOKENS, :] = padded[
            g * SET_ROWS : g * SET_ROWS + SET_TOKENS, :
        ]
    if out_ref.dtype != f32:
        out_ref[...] = packed[0 : out_ref.shape[0], :].astype(out_ref.dtype)


def first_low_body(info, x_ref, gain_ref, shift_ref, out_ref):
    out_ref[...] = layer_norm(x_ref[...].astype(f32), gain_ref[...], shift_ref[...]).astype(bf16)


def head_mask(head):
    lane = lax.broadcasted_iota(jnp.int32, (1, LANES), 1)
    return (lane < HEAD_DIM) if head == 0 else (lane >= HEAD_DIM)


def keep_head(value, head):
    return jnp.where(head_mask(head), value, jnp.zeros_like(value))


def attend_body(info, qkv_ref, key_ids, query_ids, out_ref, log_ref, block):
    @pl.when(pl.program_id(1) == 0)
    def _():
        block[...] = jnp.where(key_ids[0] == query_ids[0], 0.0, masked_score)

    factor = HEAD_DIM**-0.5
    query = qkv_ref[:, 0:LANES] * jnp.asarray(factor, bf16)
    key = qkv_ref[:, LANES : 2 * LANES]
    value = qkv_ref[:, 2 * LANES : 3 * LANES]
    halves = []
    for head in range(2):
        scores = dot(key, keep_head(query, head), NT) + block[...]
        peak = jnp.max(scores, axis=0, keepdims=True)
        raised = jnp.exp(scores - peak)
        total = jnp.sum(raised, axis=0, keepdims=True)
        mixed = dot(keep_head(value, head), raised.astype(bf16), TN)
        halves.append(mixed * (1.0 / total))
        log_ref[0, 0, head : head + 1, :] = peak + jnp.log(total)
    out_ref[...] = (halves[0] + halves[1]).T.astype(bf16)


def attend_back_body(info, qkv_ref, key_ids, query_ids, log_ref, *rest, first_half):
    grads = rest[:4]
    out_ref, sum_ref, block = rest[-3:]
    turn = pl.program_id(1)

    @pl.when(pl.program_id(0) == 0)
    def _():
        block[turn] = jnp.where(key_ids[0] == query_ids[0], 0.0, masked_score)

    factor = HEAD_DIM**-0.5
    query = qkv_ref[:, 0:LANES] * jnp.asarray(factor, bf16)
    key = qkv_ref[:, LANES : 2 * LANES]
    value = qkv_ref[:, 2 * LANES : 3 * LANES]
    parts = []
    for j in range(2):
        core = ((2 * turn + j) >= first_half).astype(jnp.int32)
        parts.append(jnp.where(core == info[0], grads[2 * j][...], grads[2 * j + 1][...]))
    grad = jnp.concatenate(parts, axis=0)
    grad_query = grad_key = grad_value = 0.0
    for head in range(2):
        query_one = keep_head(query, head)
        grad_one = keep_head(grad, head)
        scores = dot(key, query_one, NT) + block[turn]
        weights = jnp.exp(scores - log_ref[0, 0, head : head + 1, :])
        grad_value += dot(weights.astype(bf16), grad_one)
        grad_weights = dot(value, grad_one, NT)
        centre = jnp.sum(weights * grad_weights, axis=0, keepdims=True)
        low = (weights * (grad_weights - centre)).astype(bf16)
        grad_key += dot(low, query_one)
        grad_query += dot(keep_head(key, head), low, TN)
    grad_query = (grad_query * factor).T
    out_ref[:, 0:LANES] = grad_query.astype(bf16)
    out_ref[:, LANES : 2 * LANES] = grad_key.astype(bf16)
    out_ref[:, 2 * LANES : 3 * LANES] = grad_value.astype(bf16)

    @pl.when(turn == 0)
    def _():
        sum_ref[...] = jnp.zeros_like(sum_ref)

    sum_ref[0, :, 0:LANES] += jnp.sum(grad_query, axis=0, keepdims=True)
    sum_ref[0, :, 2 * LANES : 3 * LANES] += jnp.sum(grad_value, axis=0, keepdims=True)


def proj_moves(wholes, weights, chips, sems):
    width = weights.shape[1] // (2 * chips)
    part = wholes[0].shape[1] // chips
    copies = []
    for j, source in enumerate(wholes):
        for b in range(chips):
            columns = pl.ds((b + 1) * part - width, width)
            target = pl.ds((j * chips + b) * width, width)
            copies.append((source.at[:, columns], weights.at[:, target]))
    return [pltpu.make_async_copy(src, dst, sems.at[i]) for i, (src, dst) in enumerate(copies)]


def proj_norm_body(
    info, own_ref, got_ref, x_ref, bias_ref, gain_ref, shift_ref, *rest, chips
):
    wholes, (residual_ref, low_ref, weights, sems) = rest[:2], rest[2:]
    moves = proj_moves(wholes, weights, chips, sems)
    for move in moves:
        move.start()
    wait_all(moves)
    width = own_ref.shape[1]
    span = 2 * CHUNK

    def columns(i, _):
        at = pl.ds(pl.multiple_of(i * span, span), span)
        own_part = dot(own_ref[...], weights[at, :width], NT)
        residual_ref[:, at] = own_part + dot(got_ref[...], weights[at, width:], NT)
        return 0

    lax.fori_loop(0, residual_ref.shape[1] // span, columns, 0)
    step = row_step(residual_ref.shape[0])

    def rows(i, _):
        at = pl.ds(pl.multiple_of(i * step, 16), step)
        value = residual_ref[at, :] + x_ref[at, :].astype(f32) + bias_ref[...]
        residual_ref[at, :] = value
        low_ref[at, :] = layer_norm(value, gain_ref[...], shift_ref[...]).astype(bf16)
        return 0

    lax.fori_loop(0, residual_ref.shape[0] // step, rows, 0)


def row_step(rows):
    return 176 if rows % 176 == 0 else rows


def mlp_body(info, cot_ref, bias_ref, *rest, base, unit, count, parts, adds):
    pieces, rest = rest[:count], rest[count:]
    seconds, rest = rest[:parts], rest[parts:]
    gots, rest = rest[:adds], rest[adds:]
    hidden_ref, pre_ref, rest = rest[0], rest[1], rest[2:]
    backs, outs, rest = rest[:parts], rest[parts : 2 * parts], rest[2 * parts :]
    sum_ref, expand, shrink, rows, sems, row_sems = rest
    width = expand.shape[1]
    turn = pl.program_id(0)

    @pl.when(turn == 0)
    def _():
        targets = [
            (
                lambda piece: piece.at[:, pl.ds(0, width)],
                lambda place: expand.at[place, :],
            ),
            (
                lambda piece: piece.at[:, pl.ds(width, width)],
                lambda place: shrink.at[place, :],
            ),
        ]
        moves = start_all(weight_copies(info, base, pieces, unit, targets), sems)
        start_all([(seconds[i], rows.at[i]) for i in range(parts)], row_sems)
        wait_all(moves)
        sum_ref[...] = jnp.zeros_like(sum_ref)

    pltpu.make_async_copy(seconds[0], rows.at[turn], row_sems.at[turn]).wait()
    span = 2 * CHUNK if width % (2 * CHUNK) == 0 else LANES

    def columns(i, _):
        at = pl.ds(pl.multiple_of(i * span, span), span)
        pre = dot(rows[turn], expand[:, at]) + bias_ref[:, at]
        below = 0.5 * (1.0 + lax.erf(pre * root_half))
        density = density_scale * jnp.exp(-0.5 * pre * pre)
        hidden_ref[:, at] = (pre * below).astype(bf16)
        grad = dot(cot_ref[...], shrink[:, at]) * (below + pre * density)
        sum_ref[:, at] += jnp.sum(grad, axis=0, keepdims=True)
        pre_ref[:, at] = grad.astype(bf16)
        return 0

    lax.fori_loop(0, width // span, columns, 0)

    def back(i, _):
        at = pl.ds(pl.multiple_of(i * span, span), span)
        for targets, left, right, kind in (
            (backs, pre_ref, expand, 0),
            (outs, hidden_ref, shrink, 1),
        ):
            product = dot(left[...], right[at, :], NT)
            for i in range(parts):

                @pl.when(turn == i)
                def _(i=i, targets=targets, product=product, kind=kind):
                    total = product
                    if adds and kind == 0:
                        total = total + gots[i][:, at].astype(f32)
                    targets[i][:, at] = total.astype(bf16)

        return 0

    lax.fori_loop(0, backs[0].shape[1] // span, back, 0)


def mlp_grad_body(info, cot_ref, *rest, cot_base, parts, groups):
    seconds, rest = rest[:parts], rest[parts:]
    hiddens, pres, rest = rest[:groups], rest[groups : 2 * groups], rest[2 * groups :]
    out_ref, left, right, sems = rest
    phase = pl.program_id(0)
    rows = left.shape[1] // parts
    span = out_ref.shape[0]

    def moves(index):
        pairs = []
        for i in range(parts):
            source = seconds[i]
            if index == 1:
                place = pl.multiple_of(info[cot_base + i] * rows, 16)
                source = cot_ref.at[pl.ds(place, rows)]
            pairs.append((source, left.at[index, pl.ds(i * rows, rows)]))
        start = 0
        for source in (pres, hiddens)[index]:
            pairs.append((source, right.at[index, pl.ds(start, source.shape[0])]))
            start += source.shape[0]
        return [
            pltpu.make_async_copy(src, dst, sems.at[index, i]) for i, (src, dst) in enumerate(pairs)
        ]

    @pl.when((phase == 0) & (pl.program_id(1) == 0))
    def _():
        for index in range(2):
            for move in moves(index):
                move.start()

    for index in range(2):

        @pl.when((phase == index) & (pl.program_id(1) == 0))
        def _(index=index):
            wait_all(moves(index))

    at = pl.ds(pl.multiple_of(pl.program_id(1) * span, span), span)
    out_ref[...] = dot(left[phase, :, at], right[phase], TN).astype(bf16)


def norm_back(value, grad, gain):
    centred = value - jnp.mean(value, axis=-1, keepdims=True)
    spread = jnp.mean(centred * centred, axis=-1, keepdims=True)
    scale = lax.rsqrt(spread + norm_eps)
    normal = centred * scale
    weighted = grad * gain
    middle = jnp.mean(weighted, axis=-1, keepdims=True)
    slope = jnp.mean(weighted * normal, axis=-1, keepdims=True)
    return normal, scale * (weighted - middle - normal * slope)


def residual_back_body(info, residual_ref, cot_ref, gain_ref, *rest, parts, chips):
    grads, rest = rest[:parts], rest[parts:]
    wholes, (grad_ref, low_ref, own_ref, send_ref, sum_ref, weights, sems) = rest[:2], rest[2:]
    moves = proj_moves(wholes, weights, chips, sems)

    @pl.when(pl.program_id(0) == 0)
    def _():
        for move in moves:
            move.start()
        sum_ref[...] = jnp.zeros_like(sum_ref)

    grad = grads[0][...].astype(f32)
    for other in grads[1:]:
        grad += other[...].astype(f32)
    normal, back = norm_back(residual_ref[...], grad, gain_ref[...])
    cotangent = cot_ref[...].astype(f32)
    total = cotangent + back
    grad_ref[...] = total
    low_ref[...] = total.astype(bf16)
    sum_ref[0:1, :] += jnp.sum(grad * normal, axis=0, keepdims=True)
    sum_ref[1:2, :] += jnp.sum(grad, axis=0, keepdims=True)
    sum_ref[2:3, :] += jnp.sum(total, axis=0, keepdims=True)
    sum_ref[3:4, :] += jnp.sum(cotangent, axis=0, keepdims=True)

    @pl.when(pl.program_id(0) == 0)
    def _():
        wait_all(moves)

    both = dot(low_ref[...], weights[...]).astype(bf16)
    width = own_ref.shape[1]
    own_ref[...] = both[:, :width]
    send_ref[...] = both[:, width:]


def qkv_grad_body(info, first_ref, grad_ref, own_ref, got_ref, att_own, att_got, *rest):
    out_ref = rest[-1]
    width = grad_ref.shape[1]
    out_ref[:, :width] = dot(first_ref[...], grad_ref[...], TN).astype(bf16)
    out_ref[:, width:] = (
        dot(own_ref[...], att_own[...], TN) + dot(got_ref[...], att_got[...], TN)
    ).astype(bf16)


def first_norm_body(info, *refs, chips):
    grads, (x_ref, res_ref, gain_ref, *rest) = refs[: 2 * chips], refs[2 * chips :]
    two_ref, biases, hiddens, rest = rest[0], rest[1 : 1 + chips], rest[1 + chips : 4 + chips], rest[4 + chips :]
    wholes, (low_ref, sum_ref, weights, lefts, total, sems) = rest[:2], rest[2:]
    half, width = lefts.shape[1:]
    part = wholes[0].shape[1] // chips

    def move(i):
        return pltpu.make_async_copy(
            wholes[i // chips].at[:, pl.ds(i % chips * part, width)], weights.at[i], sems.at[i]
        )

    for i in range(2 * chips):
        move(i).start()
    for i in range(2 * chips):
        lefts[i] = grads[i][...]
    total[...] = jnp.zeros_like(total)

    def term(i, _):
        pltpu.make_async_copy(
            wholes[0].at[:, pl.ds(0, width)], weights.at[i], sems.at[i]
        ).wait()
        total[...] += dot(lefts[i], weights[i], NT)
        return 0

    lax.fori_loop(0, 2 * chips, term, 0)
    step = row_step(total.shape[0])
    sum_ref[...] = jnp.zeros_like(sum_ref)
    for i, j in enumerate((2, 0, 1, 3)):
        sum_ref[2 + i : 3 + i, :] = two_ref[j : j + 1, :]
    pairs = biases[0].shape[0]
    for b in range(chips):
        for kind in range(2):
            for pair in range(pairs):
                to = ((b * 2 + kind) * pairs + pair) * LANES
                value = biases[b][pair, :, kind * 2 * LANES : (kind * 2 + 1) * LANES]
                sum_ref[6:7, to : to + LANES] = value
    ff = hiddens[0].shape[1]
    sum_ref[7:8, 0:ff] = hiddens[0][...] + hiddens[1][...] + hiddens[2][...]

    def rows(i, _):
        at = pl.ds(pl.multiple_of(i * step, 16), step)
        grad = total[at, :]
        normal, back = norm_back(x_ref[at, :].astype(f32), grad, gain_ref[...])
        low_ref[at, :] = (back + res_ref[at, :]).astype(bf16)
        sum_ref[0:1, :] += jnp.sum(grad * normal, axis=0, keepdims=True)
        sum_ref[1:2, :] += jnp.sum(grad, axis=0, keepdims=True)
        return 0

    lax.fori_loop(0, total.shape[0] // step, rows, 0)


def shards(
    tokens,
    offsets,
    first_gain,
    first_shift,
    qkv_weight,
    qv_bias,
    proj_weight,
    proj_bias,
    second_gain,
    second_shift,
    expand_weight,
    expand_bias,
    shrink_weight,
    shrink_bias,
    cotangent,
):
    token_rows, dim = tokens.shape
    sets = offsets.shape[0]
    part = qkv_weight.shape[2]
    ff = expand_weight.shape[1]
    chips = lax.axis_size("mp") // 2
    ring = Ring(lax.axis_size("dp"))
    dp_index = lax.axis_index("dp")
    mp_index = lax.axis_index("mp")
    x_index, core = mp_index // 2, mp_index % 2
    sets_x = -(-sets // chips)
    slots = sets_x * chips
    rows_x = sets_x * SET_ROWS
    half = rows_x // 2
    pairs = part // LANES
    groups = chips * pairs
    unit_rows = dim // ring.count
    unit = unit_rows // 2
    width = 3 * part
    att_width = groups * LANES
    near = [(0, 0), (0, 1)]
    far_other = [(step, 1) for step in range(1, chips)]
    far_own = [(step, 0) for step in range(1, chips)]
    keys = near + far_other + far_own
    sem = pltpu.SemaphoreType.DMA
    row = lambda value: value.reshape(1, -1)
    whole = lambda *dims: pl.BlockSpec(dims, lambda *_: (0,) * len(dims))

    row_starts = lax.dynamic_index_in_dim(ring.piece_rows(unit_rows), dp_index, 0, False)
    block_ranks = lax.dynamic_index_in_dim(ring.block_ranks(), dp_index, 0, False)
    places = [(x_index - step) % chips * 2 + (core ^ other) for step, other in keys]
    info = jnp.concatenate(
        [jnp.stack([core, x_index, *places]).astype(jnp.int32), row_starts, block_ranks]
    )
    place_base = 2
    base = place_base + len(keys)
    ranks = base + ring.count + 1

    order = Order(info)

    qkv_shard = qkv_weight.astype(bf16).reshape(unit_rows, 3, pairs, LANES)
    qkv_shard = qkv_shard.transpose(0, 2, 1, 3).reshape(unit_rows, width)
    shard = jnp.concatenate([qkv_shard, proj_weight.astype(bf16).T], axis=1)
    bias_shard = jnp.zeros((pairs, 3, LANES), f32)
    bias_shard = bias_shard.at[:, 0].set(qv_bias[0].reshape(pairs, LANES))
    bias_shard = bias_shard.at[:, 2].set(qv_bias[1].reshape(pairs, LANES)).reshape(1, width)
    high = bias_shard.astype(bf16)
    both = jnp.concatenate([high, (bias_shard - high.astype(f32)).astype(bf16)])
    below = jnp.pad(both, ((0, 14), (0, part)))
    joined = jnp.concatenate([shard, below])
    attn_steps = ring.gather_steps(shard, 0, order)
    attn_pieces = [shard]
    far_pieces = {step: [across(joined, step, chips)] for step in range(1, chips)}
    bias_x = [bias_shard]
    for step in range(1, chips):
        got = far_pieces[step][0][unit_rows : unit_rows + 2, :width].astype(f32)
        bias_x.append(got[0:1] + got[1:2])

    def next_step(steps, pieces):
        got = next(steps, None)
        if got is not None:
            pieces += got
        return got

    def send_far(got):
        joined = jnp.concatenate(order.after(got))
        for step in range(1, chips):
            far_pieces[step].append(across(joined, step, chips))

    def last_far(i=-1):
        return [far_pieces[step][i] for step in range(1, chips)]

    def pad_sets(value, wait):
        columns = pl.BlockSpec((token_rows, CHUNK), lambda i, _: (0, i))
        kernel = call(
            functools.partial(pad_body, sets=sets),
            (dim // CHUNK,),
            [columns],
            pl.BlockSpec((slots * SET_ROWS, CHUNK), lambda i, _: (0, i)),
            shape((slots * SET_ROWS, dim), bf16),
            [pltpu.VMEM((token_rows + 16, CHUNK), f32)],
            "pad",
        )
        return order.run(kernel, value, wait=wait)

    got = next_step(attn_steps, attn_pieces)
    order.due = last_far()
    after = next_step(attn_steps, attn_pieces)
    order.due = ()
    send_far(got)
    x_rows = pad_sets(tokens, ())
    order.due = last_far()
    got = next_step(attn_steps, attn_pieces)
    order.due = ()
    send_far(after)
    kernel = call(
        first_low_body,
        (sets_x,),
        [
            pl.BlockSpec((SET_ROWS, dim), lambda i, info: (info[1] * sets_x + i, 0)),
            whole(1, dim),
            whole(1, dim),
        ],
        pl.BlockSpec((SET_ROWS, dim), lambda i, _: (i, 0)),
        shape((rows_x, dim), bf16),
        [],
        "first_low",
    )
    first_low = order.run(kernel, x_rows, row(first_gain), row(first_shift))
    while got:
        order.due = last_far(-2)
        after = next_step(attn_steps, attn_pieces)
        if after is None:
            shrink_shard = tie(shrink_weight, far_pieces[1][0]).astype(bf16).T
            mlp_shard = jnp.concatenate([expand_weight.astype(bf16), shrink_shard], axis=1)
            mlp_pieces = [mlp_shard]
            mlp_steps = ring.gather_steps(tie(mlp_shard, got), 0, order)
            next_step(mlp_steps, mlp_pieces)
        order.due = ()
        send_far(got)
        got = after
    order.due = last_far(-2) + last_far()
    starts = tie(jnp.pad(offsets, ((0, slots - sets), (0, 0))), order.now)
    starts = lax.dynamic_slice_in_dim(starts, x_index * sets_x, sets_x, axis=0)
    positions = jnp.arange(SET_ROWS, dtype=jnp.int32)
    ids = jnp.sum((positions[None, :, None] >= starts[:, None, :]).astype(jnp.int32), axis=-1)
    ids = jnp.where(positions[None, :] < SET_TOKENS, ids, -1)
    key_ids, query_ids = ids[:, :, None], ids[:, None, :]
    cot = pad_sets(cotangent, (key_ids, query_ids))
    next_step(mlp_steps, mlp_pieces)
    order.due = ()
    count = len(attn_pieces)
    copies = count * chips
    far_list = [piece for step in range(1, chips) for piece in far_pieces[step]]

    joint = chips * (width + part)
    kernel = call(
        functools.partial(qkv_body, base=base, unit=unit, chips=chips, count=count),
        (2,),
        [pl.BlockSpec((half, dim), lambda i, _: (i, 0)), whole(1, chips * width)]
        + [ANY] * (count + len(far_list)),
        [pl.BlockSpec((half, chips * width), lambda i, _: (i, 0)), HBM],
        [shape((rows_x, chips * width), bf16), shape((dim, joint), bf16)],
        [pltpu.VMEM((dim, joint), bf16), sem((copies,)), sem],
        "qkv",
    )
    qkv, weights = order.run(kernel, first_low, jnp.concatenate(bias_x, axis=1), *attn_pieces, *far_list)
    order.due = mlp_pieces[-2:]
    both_weights = [weights, partner(order.after(weights), chips)]

    order.due = ()
    next_step(mlp_steps, mlp_pieces)
    kernel = call(
        attend_body,
        (sets_x, groups),
        [
            pl.BlockSpec((SET_ROWS, 3 * LANES), lambda s, i, _: (s, i)),
            pl.BlockSpec((1, SET_ROWS, 1), lambda s, i, _: (s, 0, 0)),
            pl.BlockSpec((1, 1, SET_ROWS), lambda s, i, _: (s, 0, 0)),
        ],
        [
            pl.BlockSpec((SET_ROWS, LANES), lambda s, i, _: (s, i)),
            pl.BlockSpec((1, 1, 2, SET_ROWS), lambda s, i, _: (s, i, 0, 0)),
        ],
        [
            shape((rows_x, att_width), bf16),
            shape((sets_x, groups, 2, SET_ROWS), f32),
        ],
        [pltpu.VMEM((SET_ROWS, SET_ROWS), f32)],
        "attend",
    )
    attended, logs = order.run(kernel, qkv, key_ids, query_ids)
    order.due = [*mlp_pieces[-2:], both_weights[1]]
    attended_other = partner(order.after(attended), chips)
    order.due = ()
    next_step(mlp_steps, mlp_pieces)

    own_half = lambda *dims: pl.BlockSpec(dims, lambda i, info: (info[0], 0))
    own_place = lambda *dims: pl.BlockSpec(dims, lambda i, info: (info[place_base], 0))
    proj_scratch = [pltpu.VMEM((dim, 2 * att_width), bf16), sem((2 * chips,))]
    kernel = call(
        functools.partial(proj_norm_body, chips=chips),
        (1,),
        [own_half(half, att_width)] * 2 + [own_place(half, dim)] + [whole(1, dim)] * 3 + [HBM] * 2,
        [whole(half, dim), whole(half, dim)],
        [shape((half, dim), f32), shape((half, dim), bf16)],
        proj_scratch,
        "proj_norm",
    )
    residual, second_low = order.run(
        kernel,
        attended,
        attended_other,
        x_rows,
        row(proj_bias),
        row(second_gain),
        row(second_shift),
        *both_weights,
    )
    seconds = {(0, 0): second_low}
    for step in range(1, chips):
        seconds[(step, 0)] = across(second_low, step, chips)
    order.due = mlp_pieces[-2:]
    seconds[(0, 1)] = partner(order.after(second_low), chips)
    order.due = ()
    while next_step(mlp_steps, mlp_pieces):
        pass

    def feed(group, gots=()):
        parts = len(group)
        first = keys.index(group[0])
        kernel = call(
            functools.partial(
                mlp_body, base=base, unit=unit, count=count, parts=parts, adds=len(gots)
            ),
            (parts,),
            [
                pl.BlockSpec((half, dim), lambda i, info: (info[place_base + first + i], 0)),
                whole(1, ff),
            ]
            + [HBM] * (count + parts)
            + [whole(half, dim)] * len(gots),
            [pl.BlockSpec((half, ff), lambda i, _: (i, 0))] * 2
            + [whole(half, dim)] * (2 * parts)
            + [whole(1, ff)],
            [shape((parts * half, ff), bf16)] * 2
            + [shape((half, dim), bf16)] * (2 * parts)
            + [shape((1, ff), f32)],
            [
                pltpu.VMEM((dim, ff), bf16),
                pltpu.VMEM((dim, ff), bf16),
                pltpu.VMEM((parts, half, dim), bf16),
                sem((2 * count,)),
                sem((parts,)),
            ],
            "mlp",
        )
        outs = order.run(
            kernel,
            cot,
            row(expand_bias),
            *mlp_pieces,
            *[seconds[key] for key in group],
            *gots,
        )
        backs, rows = outs[2 : 2 + parts], outs[2 + parts : 2 + 2 * parts]
        return outs[0], outs[1], list(backs), list(rows), outs[-1]

    first = feed(near)
    for step in range(1, chips):
        seconds[(step, 1)] = partner(order.after(seconds[(step, 0)]), chips)
    other = feed(far_other)
    own = feed(far_own, [partner(back, chips) for back in other[2]])
    feeds = [first, other, own]

    def along_x(own, sums):
        terms = [own[0], partner(own[1], chips)]
        return terms + [across(value, chips - 1 - i, chips) for i, value in enumerate(sums)]

    back_terms = along_x(first[2], own[2])
    span = 2 * CHUNK
    total_rows = len(keys) * half
    kernel = call(
        functools.partial(mlp_grad_body, cot_base=place_base, parts=len(keys), groups=3),
        (2, dim // span),
        [HBM] * (7 + len(keys)),
        pl.BlockSpec((span, ff), lambda p, i, _: (i, p)),
        shape((dim, 2 * ff), bf16),
        [
            pltpu.VMEM((2, total_rows, dim), bf16),
            pltpu.VMEM((2, total_rows, ff), bf16),
            sem((2, len(keys) + 3)),
        ],
        "mlp_grad",
    )
    mlp_grad = order.run(
        kernel,
        cot,
        *[seconds[key] for key in keys],
        *[outs[0] for outs in feeds],
        *[outs[1] for outs in feeds],
    )
    mlp_ring = ring.scatter_steps(mlp_grad, ranks, order)
    mlp_due = next(mlp_ring)

    if chips == 2:
        out_far = own[3][0].astype(f32)
        out_far = (out_far + partner(other[3][0], chips).astype(f32)).astype(bf16)
        out_near = order.after(residual) + shrink_bias + first[3][0].astype(f32)
        out_near = (out_near + partner(first[3][1], chips).astype(f32)).astype(bf16)
        order.hold = out_far, out_near
    step_rows = row_step(half)
    cot_rows = pl.BlockSpec(
        (step_rows, dim), lambda i, info: (info[place_base] * (half // step_rows) + i, 0)
    )
    plain_rows = lambda count: pl.BlockSpec((step_rows, count), lambda i, _: (i, 0))
    kernel = call(
        functools.partial(residual_back_body, parts=len(back_terms), chips=chips),
        (half // step_rows,),
        [plain_rows(dim), cot_rows, whole(1, dim)]
        + [plain_rows(dim)] * len(back_terms)
        + [HBM] * 2,
        [plain_rows(dim)] * 2 + [plain_rows(att_width)] * 2 + [whole(8, dim)],
        [
            shape((half, dim), f32),
            shape((half, dim), bf16),
            shape((half, att_width), bf16),
            shape((half, att_width), bf16),
            shape((8, dim), f32),
        ],
        proj_scratch,
        "residual_back",
    )
    grad_residual, residual_low, grad_own, grad_send, sums_two = order.run(
        kernel, residual, cot, row(second_gain), *back_terms, *both_weights
    )
    order.due = mlp_due
    grad_got = partner(order.after(grad_send), chips)
    residual_other = partner(order.after(residual_low), chips)
    order.due = ()
    mlp_due = next(mlp_ring)
    if chips == 2:
        out_rows = jnp.concatenate([out_far, out_near])
        cuts = [0, half // 16 * 8, half * 5 // 32 * 8, 2 * half]
        out_sends = iter([out_rows[i:j] for i, j in zip(cuts, cuts[1:])])
        out_gots = [across(order.after(next(out_sends)), 1, chips)]
    else:
        out_own = [
            (mine.astype(f32) + partner(order.after(got), chips).astype(f32)).astype(bf16)
            for mine, got in zip(own[3], other[3])
        ]
        out_terms = along_x(order.after(first[3]), out_own)

    def attend_back(b):
        half_block = lambda j: pl.BlockSpec(
            (row_step(half), LANES), lambda i, s, _: (lax.rem(2 * s + j, sets_x), b * pairs + i)
        )
        kernel = call(
            functools.partial(attend_back_body, first_half=sets_x),
            (pairs, sets_x),
            [
                pl.BlockSpec((SET_ROWS, 3 * LANES), lambda i, s, _: (s, b * pairs + i)),
                pl.BlockSpec((1, SET_ROWS, 1), lambda i, s, _: (s, 0, 0)),
                pl.BlockSpec((1, 1, SET_ROWS), lambda i, s, _: (s, 0, 0)),
                pl.BlockSpec((1, 1, 2, SET_ROWS), lambda i, s, _: (s, b * pairs + i, 0, 0)),
                half_block(0),
                half_block(0),
                half_block(1),
                half_block(1),
            ],
            [
                pl.BlockSpec((SET_ROWS, 3 * LANES), lambda i, s, _: (s, i)),
                pl.BlockSpec((1, 1, 3 * LANES), lambda i, s, _: (i, 0, 0)),
            ],
            [shape((rows_x, width), bf16), shape((pairs, 1, 3 * LANES), f32)],
            [pltpu.VMEM((sets_x, SET_ROWS, SET_ROWS), f32)],
            "attend_back",
        )
        ids = key_ids, query_ids
        return order.run(kernel, qkv, *ids, logs, grad_own, grad_got, grad_own, grad_got)

    def qkv_grad(b, before):
        columns = lambda count: pl.BlockSpec((count, CHUNK), lambda i, _: (0, i))
        kernel = call(
            qkv_grad_body,
            (dim // CHUNK,),
            [
                columns(rows_x),
                whole(rows_x, width),
                columns(half),
                columns(half),
                pl.BlockSpec((half, part), lambda i, info: (info[0], b)),
                pl.BlockSpec((half, part), lambda i, info: (1 - info[0], b)),
            ]
            + [ANY] * len(before),
            pl.BlockSpec((CHUNK, width + part), lambda i, _: (i, b)),
            shape((dim, joint), bf16),
            [],
            "qkv_grad",
            {7 + i: i for i in range(len(before))},
        )
        return order.run(
            kernel,
            first_low,
            grads_qkv[b],
            residual_low,
            residual_other,
            attended,
            attended,
            *before,
        )

    def out_due(i):
        if chips != 2:
            return ()
        if i < 2:
            out_gots.append(across(order.after(next(out_sends)), 1, chips))
        return out_gots[i]

    grads_qkv, grads_other, qkv_sums, begun = {}, {}, {}, ()
    for b in range(1, chips):
        grads_qkv[b], qkv_sums[b] = attend_back(b)
        order.due = mlp_due, residual_other, out_due(b - 1)
        grads_other[b] = partner(order.after(grads_qkv[b]), chips)
        order.due = ()
        mlp_due = next(mlp_ring, ())
        begun = (qkv_grad(b, begun),)
    grads_qkv[0], qkv_sums[0] = attend_back(0)
    order.due = mlp_due, [grads_other[b] for b in range(1, chips)], out_due(1)
    grads_other[0] = partner(order.after(grads_qkv[0]), chips)
    order.due = ()
    mlp_due = next(mlp_ring, ())
    attn_ring = ring.scatter_steps(qkv_grad(0, begun), ranks, order, "ring_end")
    order.due = [grads_other[b] for b in range(chips)]
    order.hold = next(attn_ring)
    order.due = ()
    for mlp_grad in mlp_ring:
        pass
    expand_part, shrink_part = mlp_grad[:, :ff], mlp_grad[:, ff:].T
    out_due(2)
    if chips == 2:
        out_rows = jnp.concatenate([out_near, out_far]).astype(f32)
        out_rows = out_rows + jnp.concatenate(order.after(out_gots)).astype(f32)
    else:
        out_rows = order.after(residual) + shrink_bias
        for term in out_terms:
            out_rows = out_rows + term.astype(f32)
        low = out_rows.astype(bf16)
        out_rows = jnp.concatenate([low] + [across(low, step, chips) for step in range(1, chips)])
    out_rows = out_rows.astype(bf16)
    order.hold = out_rows
    attn_due = next(attn_ring)

    kernel = call(
        functools.partial(first_norm_body, chips=chips),
        (1,),
        [own_half(half, width)] * (2 * chips)
        + [own_place(half, dim), whole(half, dim), whole(1, dim), whole(8, dim)]
        + [whole(pairs, 1, 3 * LANES)] * chips
        + [whole(1, ff)] * 3
        + [HBM] * 2,
        [whole(half, dim), whole(8, dim)],
        [shape((half, dim), bf16), shape((8, dim), f32)],
        [
            pltpu.VMEM((2 * chips, dim, width), bf16),
            pltpu.VMEM((2 * chips, half, width), bf16),
            pltpu.VMEM((half, dim), f32),
            sem((2 * chips,)),
        ],
        "first_norm",
    )
    tokens_low, small = order.run(
        kernel,
        *[grads_qkv[b] for b in range(chips)],
        *[grads_other[b] for b in range(chips)],
        x_rows,
        grad_residual,
        row(first_gain),
        sums_two,
        *[qkv_sums[b] for b in range(chips)],
        first[4],
        other[4],
        own[4],
        *both_weights,
    )

    def assemble(rows, dtype):
        block = lambda count, at: pl.BlockSpec((count, CHUNK), lambda i, _: (at, i))
        kernel = call(
            functools.partial(assemble_body, base=place_base, sets=sets),
            (dim // CHUNK,),
            [block(half, rows[key][1]) for key in keys],
            block(token_rows, 0),
            shape((token_rows, dim), dtype),
            [
                pltpu.VMEM((slots * SET_ROWS, CHUNK), f32),
                pltpu.VMEM((token_rows + 16, CHUNK), f32),
            ],
            "assemble",
        )
        return order.run(kernel, *[rows[key][0] for key in keys])

    bits = [1 << i for i in range(ring.count.bit_length() - 1)]

    def from_rank(small, bit):
        return lax.ppermute(small, "dp", [(r, r ^ bit) for r in range(ring.count)])

    def add_chips(small):
        shared = small[:6] + partner(small[:6], chips)
        own, *others = small[6:7].reshape(chips, 2 * part)
        if chips == 2:
            sent = jnp.concatenate([shared.reshape(-1), others[0]])
            got = across(sent, 1, chips)
            shared = shared + got[: 6 * dim].reshape(6, dim)
            own = own + got[6 * dim :]
        else:
            bit = 1
            while bit < chips:
                flips = [(m, m ^ (2 * bit)) for m in range(2 * chips)]
                shared = shared + lax.ppermute(shared, "mp", flips)
                bit *= 2
            for step in range(1, chips):
                own = own + across(others[step - 1], chips - step, chips)
        own = jnp.pad(own, (0, dim - 2 * part)).reshape(1, dim)
        return jnp.concatenate([shared, own, small[7:]])

    order.due = attn_due
    tokens_low = order.after(tokens_low)
    grads, outs = {(0, 0): (tokens_low, 0)}, {}
    for step in range(1, chips):
        grads[(step, 0)] = across(tokens_low, step, chips), 0
    order.due = ()
    next(attn_ring)
    out_other = partner(order.after(out_rows), chips)
    for step in range(chips):
        outs[(step, 0)], outs[(step, 1)] = (out_rows, step), (out_other, step)

    got = from_rank(order.after(small), bits[0])
    outputs = assemble(outs, bf16)
    small = small + order.after(got)
    order.hold = (expand_part, shrink_part)
    order.due = small
    next(attn_ring)
    order.due = ()
    grads[(0, 1)] = partner(order.after(tokens_low), chips), 0
    for step in range(1, chips):
        grads[(step, 1)] = partner(order.after(grads[(step, 0)][0]), chips), 0
    small = add_chips(order.after(small))
    for attn_sum in attn_ring:
        pass
    small = order.after(small)
    attn_low = order.after(attn_sum.astype(bf16))
    sent = {}
    for step in range(1, chips):
        columns = slice(step * (width + part), (step + 1) * (width + part))
        sent[step] = across(attn_low[:, columns], chips - step, chips)
    got = from_rank(small, bits[1])
    grad_tokens = assemble(grads, f32)
    small = small + order.after(got)
    for bit in bits[2:]:
        small = small + from_rank(small, bit)
    shared = small[:6]
    bias_own = small[6, : 2 * part].reshape(2, part)
    expand_bias_grad = small[7:].reshape(-1)[:ff]
    attn_part = attn_sum[:, : width + part]
    for step in range(1, chips):
        attn_part = attn_part + order.after(sent[step]).astype(f32)

    qkv_part = attn_part[:, :width].reshape(unit_rows, pairs, 3, LANES)
    qkv_part = qkv_part.transpose(0, 2, 1, 3).reshape(unit_rows, 3, part)
    return (
        outputs,
        grad_tokens,
        shared[0],
        shared[1],
        qkv_part,
        bias_own,
        attn_part[:, width:].T,
        shared[2],
        shared[3],
        shared[4],
        expand_part,
        expand_bias_grad,
        shrink_part,
        shared[5],
    )


def solution(mesh):
    placed = (
        P("dp", None),
        P("dp", None),
        P(),
        P(),
        P("dp", None, "mp"),
        P(None, "mp"),
        P("mp", "dp"),
        P(),
        P(),
        P(),
        P("dp", "mp"),
        P("mp"),
        P("mp", "dp"),
        P(),
        P("dp", None),
    )
    return jax.shard_map(
        shards,
        mesh=mesh,
        in_specs=placed,
        out_specs=(
            P("dp", None),
            P("dp", None),
            P(),
            P(),
            P("dp", None, "mp"),
            P(None, "mp"),
            P("mp", "dp"),
            P(),
            P(),
            P(),
            P("dp", "mp"),
            P("mp"),
            P("mp", "dp"),
            P(),
        ),
        check_vma=False,
    )
```

```python
import functools

import jax
import jax.numpy as jnp
import numpy as np
from jax import lax
from jax.experimental import pallas as pl
from jax.experimental.pallas import tpu as pltpu
from jax.sharding import PartitionSpec as P

HEAD_DIM = 64
SET_TOKENS = 345
SET_ROWS = 352
LANES = 128
CHUNK = 256

norm_eps = 1e-06
masked_score = -1e30
root_half = 0.7071067811865476
density_scale = 0.3989422804014327
f32 = jnp.float32
bf16 = jnp.bfloat16
NN = (((1,), (0,)), ((), ()))
NT = (((1,), (1,)), ((), ()))
TN = (((0,), (0,)), ((), ()))
ANY = pl.BlockSpec(memory_space=pl.ANY)
HBM = pl.BlockSpec(memory_space=pltpu.HBM)


def dot(left, right, dims=NN):
    return lax.dot_general(left, right, dims, preferred_element_type=f32)


ROOM = {
    "ring_first": 4,
    "ring_add": 10,
    "ring_last": 8,
    "ring_end": 8,
    "qkv": 20,
    "pad": 20,
    "assemble": 58,
    "first_low": 10,
    "attend": 10,
    "attend_back": 12,
    "proj_norm": 20,
    "mlp": 58,
    "mlp_grad": 54,
    "residual_back": 16,
    "qkv_grad": 20,
    "first_norm": 54,
}


COST = {"ring_end": 2 * 10**10}


def call(body, grid, in_specs, out_specs, out_shape, scratch, name, aliases=None):
    return pl.pallas_call(
        body,
        grid_spec=pltpu.PrefetchScalarGridSpec(
            num_scalar_prefetch=1,
            grid=grid,
            in_specs=in_specs,
            out_specs=out_specs,
            scratch_shapes=scratch,
        ),
        out_shape=out_shape,
        compiler_params=pltpu.CompilerParams(
            dimension_semantics=("arbitrary",) * len(grid), vmem_limit_bytes=ROOM[name] * 2**20
        ),
        cost_estimate=pl.CostEstimate(
            flops=COST.get(name, 1), bytes_accessed=1, transcendentals=0
        ),
        name=name,
        input_output_aliases=aliases or {},
    )


def tie(value, *earlier):
    return lax.optimization_barrier((value, earlier))[0]


class Order:
    def __init__(self, info):
        self.info = info
        self.now = info
        self.due = ()
        self.hold = ()

    def after(self, value):
        return tie(value, self.now, self.due)

    def run(self, kernel, *values, wait=()):
        out = kernel(tie(self.info, self.now, wait, self.hold), *values)
        self.hold = ()
        self.now = out[0] if isinstance(out, (list, tuple)) else out
        return out


def shape(dims, dtype):
    return jax.ShapeDtypeStruct(tuple(dims), dtype)


def ring_order(count):
    width = 1
    while 2 * (2 * width) ** 2 <= count:
        width *= 2
    length = count // width
    if width == 1:
        return list(range(count))
    path = []
    for z in range(length):
        columns = range(1, width) if z % 2 == 0 else range(width - 1, 0, -1)
        path += [z * width + y for y in columns]
    path += [z * width for z in range(length - 1, -1, -1)]
    return path


class Ring:
    def __init__(self, count):
        self.count = count
        self.order = ring_order(count)
        self.place = {rank: i for i, rank in enumerate(self.order)}
        self.ahead = [(self.order[i], self.order[(i + 1) % count]) for i in range(count)]
        self.behind = [(self.order[i], self.order[(i - 1) % count]) for i in range(count)]

    def rank_at(self, rank, offset):
        return self.order[(self.place[rank] + offset) % self.count]

    def send_ahead(self, value):
        return lax.ppermute(value, "dp", self.ahead)

    def send_behind(self, value):
        return lax.ppermute(value, "dp", self.behind)

    def gather_steps(self, block, axis, order):
        half = block.shape[axis] // 2
        forward = backward = block
        for step in range(1, self.count // 2 + 1):
            if step == self.count // 2:
                forward = lax.slice_in_dim(forward, 0, half, axis=axis)
                backward = lax.slice_in_dim(backward, half, 2 * half, axis=axis)
            forward, backward = order.after((forward, backward))
            forward = self.send_ahead(forward)
            backward = self.send_behind(backward)
            yield forward, backward

    def piece_rows(self, rows):
        table = []
        middle = self.count // 2
        for rank in range(self.count):
            starts = [rank * rows]
            for step in range(1, middle + 1):
                ahead = self.rank_at(rank, -step) * rows
                behind = self.rank_at(rank, step) * rows
                if step == middle:
                    behind += rows // 2
                starts += [ahead, behind]
            table.append(starts)
        return np.array(table, np.int32)

    def block_ranks(self):
        middle = self.count // 2
        return np.array(
            [
                [self.rank_at(rank, d) for d in range(-middle, middle + 1)]
                for rank in range(self.count)
            ],
            np.int32,
        )

    def scatter_steps(self, whole, ranks, order, last="ring_last"):
        middle = self.count // 2
        dim, columns = whole.shape
        rows = dim // self.count
        half = rows // 2
        wide = columns
        grid = (columns // wide,)
        block = lambda d: pl.BlockSpec((rows, wide), lambda j, info: (info[ranks + middle + d], j))
        plain = lambda count: pl.BlockSpec((count, wide), lambda j, _: (0, j))
        kernel = call(
            ring_first_body,
            grid,
            [
                pl.BlockSpec((half, wide), lambda j, info: (2 * info[ranks + 2 * middle], j)),
                pl.BlockSpec((half, wide), lambda j, info: (2 * info[ranks] + 1, j)),
            ],
            [plain(half)] * 2,
            [shape((half, columns), bf16)] * 2,
            [],
            "ring_first",
        )
        forward, backward = order.run(kernel, whole, whole)
        for step in range(1, middle + 1):
            forward = self.send_ahead(order.after(forward))
            backward = self.send_behind(order.after(backward))
            yield forward, backward
            near = middle - step
            if near == 0:
                break
            final = near == 1
            kernel = call(
                ring_add_body,
                grid,
                [block(near), block(-near)] + [block(0)] * final + [plain(forward.shape[0])] * 2,
                [plain(rows)] * (2 + final),
                [shape((rows, columns), bf16)] * (2 + final),
                [],
                "ring_add",
            )
            forward, backward, *own = order.run(kernel, *[whole] * (2 + final), forward, backward)
        kernel = call(
            ring_last_body,
            grid,
            [plain(rows)] * 3,
            plain(rows),
            shape((rows, columns), f32),
            [],
            last,
        )
        yield order.run(kernel, *own, forward, backward)


def across(value, step, chips):
    pairs = [
        (x * 2 + core, (x + step) % chips * 2 + core) for x in range(chips) for core in range(2)
    ]
    return lax.ppermute(value, "mp", pairs)


def partner(value, chips):
    return lax.ppermute(value, "mp", [(m, m ^ 1) for m in range(2 * chips)])


def layer_norm(values, gain, shift):
    centre = jnp.mean(values, axis=-1, keepdims=True)
    offset_rows = values - centre
    spread = jnp.mean(offset_rows * offset_rows, axis=-1, keepdims=True)
    return offset_rows * lax.rsqrt(spread + norm_eps) * gain + shift


def start_all(copies, sems):
    moves = [pltpu.make_async_copy(src, dst, sems.at[i]) for i, (src, dst) in enumerate(copies)]
    for move in moves:
        move.start()
    return moves


def wait_all(moves):
    for move in moves:
        move.wait()


def weight_copies(info, base, pieces, unit, targets):
    copies = []
    for i, piece in enumerate(pieces):
        rows = piece.shape[-2]
        place = pl.ds(pl.multiple_of(info[base + i], unit), rows)
        for source, target in targets:
            copies.append((source(piece), target(place)))
    return copies


def ring_first_body(info, ahead_ref, behind_ref, ahead_out, behind_out):
    ahead_out[...] = ahead_ref[...]
    behind_out[...] = behind_ref[...]


def ring_add_body(info, ahead_ref, behind_ref, *rest):
    if len(rest) == 6:
        own_ref, *rest, own_out = rest
        own_out[...] = own_ref[...]
    got_ahead, got_behind, ahead_out, behind_out = rest
    rows, part = ahead_out.shape[0], got_ahead.shape[0]
    first, last = slice(0, part), slice(rows - part, rows)
    total = ahead_ref[first, :].astype(f32) + got_ahead[...].astype(f32)
    ahead_out[first, :] = total.astype(bf16)
    total = behind_ref[last, :].astype(f32) + got_behind[...].astype(f32)
    behind_out[last, :] = total.astype(bf16)
    if part < rows:
        ahead_out[part:, :] = ahead_ref[part:, :]
        behind_out[: rows - part, :] = behind_ref[: rows - part, :]


def ring_last_body(info, own_ref, got_ahead, got_behind, out_ref):
    both = got_ahead[...].astype(f32) + got_behind[...].astype(f32)
    out_ref[...] = own_ref[...].astype(f32) + both


def qkv_body(info, x_ref, bias_ref, *rest, base, unit, chips, count):
    steps = count // 2 + 1
    own, rest = rest[:count], rest[count:]
    far, (out_ref, whole_ref, weights, sems, out_sem) = (
        rest[: steps * (chips - 1)],
        rest[steps * (chips - 1) :],
    )
    part = weights.shape[1] // chips
    width = out_ref.shape[1] // chips
    keep = pltpu.make_async_copy(weights, whole_ref, out_sem)

    @pl.when(pl.program_id(0) == 0)
    def _():
        copies = []
        for b in range(chips):
            for i, piece in enumerate(own):
                rows = piece.shape[0]
                source = piece
                if b:
                    joined = far[(b - 1) * steps + (i + 1) // 2]
                    source = joined.at[pl.ds(rows if i and i % 2 == 0 else 0, rows)]
                place = pl.ds(pl.multiple_of(info[base + i], unit), rows)
                copies.append((source, weights.at[place, pl.ds(b * part, part)]))
        wait_all(start_all(copies, sems))
        keep.start()

    def columns(b, _):
        to = pl.ds(pl.multiple_of(b * width, LANES), width)
        product = dot(x_ref[...], weights[:, pl.ds(pl.multiple_of(b * part, LANES), width)])
        out_ref[:, to] = (product + bias_ref[:, to]).astype(bf16)
        return 0

    lax.fori_loop(0, chips, columns, 0)

    @pl.when(pl.program_id(0) == pl.num_programs(0) - 1)
    def _():
        keep.wait()


def pad_body(info, in_ref, out_ref, rows, *, sets):
    total = in_ref.shape[0]
    rows[0:total, :] = in_ref[...].astype(f32)
    inside = lax.broadcasted_iota(jnp.int32, (SET_ROWS, 1), 0) < SET_TOKENS
    for g in range(out_ref.shape[0] // SET_ROWS):
        to = slice(g * SET_ROWS, (g + 1) * SET_ROWS)
        if g < sets:
            value = rows[g * SET_TOKENS : g * SET_TOKENS + SET_ROWS, :]
            out_ref[to, :] = jnp.where(inside, value, 0.0).astype(bf16)
        else:
            out_ref[to, :] = jnp.zeros((SET_ROWS, out_ref.shape[1]), bf16)


def assemble_body(info, *refs, base, sets):
    pieces, (out_ref, padded, packed) = refs[:-3], refs[-3:]
    half = pieces[0].shape[0]
    for i, piece in enumerate(pieces):
        place = pl.ds(pl.multiple_of(info[base + i] * half, 16), half)
        padded[place, :] = piece[...].astype(f32)
    target = out_ref if out_ref.dtype == f32 else packed
    for g in range(sets):
        target[g * SET_TOKENS : (g + 1) * SET_TOKENS, :] = padded[
            g * SET_ROWS : g * SET_ROWS + SET_TOKENS, :
        ]
    if out_ref.dtype != f32:
        out_ref[...] = packed[0 : out_ref.shape[0], :].astype(out_ref.dtype)


def first_low_body(info, x_ref, gain_ref, shift_ref, out_ref):
    out_ref[...] = layer_norm(x_ref[...].astype(f32), gain_ref[...], shift_ref[...]).astype(bf16)


def head_mask(head):
    lane = lax.broadcasted_iota(jnp.int32, (1, LANES), 1)
    return (lane < HEAD_DIM) if head == 0 else (lane >= HEAD_DIM)


def keep_head(value, head):
    return jnp.where(head_mask(head), value, jnp.zeros_like(value))


def attend_body(info, qkv_ref, key_ids, query_ids, out_ref, log_ref, block):
    @pl.when(pl.program_id(1) == 0)
    def _():
        block[...] = jnp.where(key_ids[0] == query_ids[0], 0.0, masked_score)

    factor = HEAD_DIM**-0.5
    query = qkv_ref[:, 0:LANES] * jnp.asarray(factor, bf16)
    key = qkv_ref[:, LANES : 2 * LANES]
    value = qkv_ref[:, 2 * LANES : 3 * LANES]
    halves = []
    for head in range(2):
        scores = dot(key, keep_head(query, head), NT) + block[...]
        peak = jnp.max(scores, axis=0, keepdims=True)
        raised = jnp.exp(scores - peak)
        total = jnp.sum(raised, axis=0, keepdims=True)
        mixed = dot(keep_head(value, head), raised.astype(bf16), TN)
        halves.append(mixed * (1.0 / total))
        log_ref[0, 0, head : head + 1, :] = peak + jnp.log(total)
    out_ref[...] = (halves[0] + halves[1]).T.astype(bf16)


def attend_back_body(info, qkv_ref, key_ids, query_ids, log_ref, *rest, first_half):
    grads = rest[:4]
    out_ref, sum_ref, block = rest[-3:]
    turn = pl.program_id(1)

    @pl.when(pl.program_id(0) == 0)
    def _():
        block[turn] = jnp.where(key_ids[0] == query_ids[0], 0.0, masked_score)

    factor = HEAD_DIM**-0.5
    query = qkv_ref[:, 0:LANES] * jnp.asarray(factor, bf16)
    key = qkv_ref[:, LANES : 2 * LANES]
    value = qkv_ref[:, 2 * LANES : 3 * LANES]
    parts = []
    for j in range(2):
        core = ((2 * turn + j) >= first_half).astype(jnp.int32)
        parts.append(jnp.where(core == info[0], grads[2 * j][...], grads[2 * j + 1][...]))
    grad = jnp.concatenate(parts, axis=0)
    grad_query = grad_key = grad_value = 0.0
    for head in range(2):
        query_one = keep_head(query, head)
        grad_one = keep_head(grad, head)
        scores = dot(key, query_one, NT) + block[turn]
        weights = jnp.exp(scores - log_ref[0, 0, head : head + 1, :])
        grad_value += dot(weights.astype(bf16), grad_one)
        grad_weights = dot(value, grad_one, NT)
        centre = jnp.sum(weights * grad_weights, axis=0, keepdims=True)
        low = (weights * (grad_weights - centre)).astype(bf16)
        grad_key += dot(low, query_one)
        grad_query += dot(keep_head(key, head), low, TN)
    grad_query = (grad_query * factor).T
    out_ref[:, 0:LANES] = grad_query.astype(bf16)
    out_ref[:, LANES : 2 * LANES] = grad_key.astype(bf16)
    out_ref[:, 2 * LANES : 3 * LANES] = grad_value.astype(bf16)

    @pl.when(turn == 0)
    def _():
        sum_ref[...] = jnp.zeros_like(sum_ref)

    sum_ref[0, :, 0:LANES] += jnp.sum(grad_query, axis=0, keepdims=True)
    sum_ref[0, :, 2 * LANES : 3 * LANES] += jnp.sum(grad_value, axis=0, keepdims=True)


def proj_moves(wholes, weights, chips, sems):
    width = weights.shape[1] // (2 * chips)
    part = wholes[0].shape[1] // chips
    copies = []
    for j, source in enumerate(wholes):
        for b in range(chips):
            columns = pl.ds((b + 1) * part - width, width)
            target = pl.ds((j * chips + b) * width, width)
            copies.append((source.at[:, columns], weights.at[:, target]))
    return [pltpu.make_async_copy(src, dst, sems.at[i]) for i, (src, dst) in enumerate(copies)]


def proj_norm_body(
    info, own_ref, got_ref, x_ref, bias_ref, gain_ref, shift_ref, *rest, chips
):
    wholes, (residual_ref, low_ref, weights, sems) = rest[:2], rest[2:]
    moves = proj_moves(wholes, weights, chips, sems)
    for move in moves:
        move.start()
    wait_all(moves)
    width = own_ref.shape[1]
    span = 2 * CHUNK

    def columns(i, _):
        at = pl.ds(pl.multiple_of(i * span, span), span)
        own_part = dot(own_ref[...], weights[at, :width], NT)
        residual_ref[:, at] = own_part + dot(got_ref[...], weights[at, width:], NT)
        return 0

    lax.fori_loop(0, residual_ref.shape[1] // span, columns, 0)
    step = row_step(residual_ref.shape[0])

    def rows(i, _):
        at = pl.ds(pl.multiple_of(i * step, 16), step)
        value = residual_ref[at, :] + x_ref[at, :].astype(f32) + bias_ref[...]
        residual_ref[at, :] = value
        low_ref[at, :] = layer_norm(value, gain_ref[...], shift_ref[...]).astype(bf16)
        return 0

    lax.fori_loop(0, residual_ref.shape[0] // step, rows, 0)


def row_step(rows):
    return 176 if rows % 176 == 0 else rows


def mlp_body(info, cot_ref, bias_ref, *rest, base, unit, count, parts, adds):
    pieces, rest = rest[:count], rest[count:]
    seconds, rest = rest[:parts], rest[parts:]
    gots, rest = rest[:adds], rest[adds:]
    hidden_ref, pre_ref, rest = rest[0], rest[1], rest[2:]
    backs, outs, rest = rest[:parts], rest[parts : 2 * parts], rest[2 * parts :]
    sum_ref, expand, shrink, rows, sems, row_sems = rest
    width = expand.shape[1]
    turn = pl.program_id(0)

    @pl.when(turn == 0)
    def _():
        targets = [
            (
                lambda piece: piece.at[:, pl.ds(0, width)],
                lambda place: expand.at[place, :],
            ),
            (
                lambda piece: piece.at[:, pl.ds(width, width)],
                lambda place: shrink.at[place, :],
            ),
        ]
        moves = start_all(weight_copies(info, base, pieces, unit, targets), sems)
        start_all([(seconds[i], rows.at[i]) for i in range(parts)], row_sems)
        wait_all(moves)
        sum_ref[...] = jnp.zeros_like(sum_ref)

    pltpu.make_async_copy(seconds[0], rows.at[turn], row_sems.at[turn]).wait()
    span = 2 * CHUNK if width % (2 * CHUNK) == 0 else LANES

    def columns(i, _):
        at = pl.ds(pl.multiple_of(i * span, span), span)
        pre = dot(rows[turn], expand[:, at]) + bias_ref[:, at]
        below = 0.5 * (1.0 + lax.erf(pre * root_half))
        density = density_scale * jnp.exp(-0.5 * pre * pre)
        hidden_ref[:, at] = (pre * below).astype(bf16)
        grad = dot(cot_ref[...], shrink[:, at]) * (below + pre * density)
        sum_ref[:, at] += jnp.sum(grad, axis=0, keepdims=True)
        pre_ref[:, at] = grad.astype(bf16)
        return 0

    lax.fori_loop(0, width // span, columns, 0)

    def back(i, _):
        at = pl.ds(pl.multiple_of(i * span, span), span)
        for targets, left, right, kind in (
            (backs, pre_ref, expand, 0),
            (outs, hidden_ref, shrink, 1),
        ):
            product = dot(left[...], right[at, :], NT)
            for i in range(parts):

                @pl.when(turn == i)
                def _(i=i, targets=targets, product=product, kind=kind):
                    total = product
                    if adds and kind == 0:
                        total = total + gots[i][:, at].astype(f32)
                    targets[i][:, at] = total.astype(bf16)

        return 0

    lax.fori_loop(0, backs[0].shape[1] // span, back, 0)


def mlp_grad_body(info, cot_ref, *rest, cot_base, parts, groups):
    seconds, rest = rest[:parts], rest[parts:]
    hiddens, pres, rest = rest[:groups], rest[groups : 2 * groups], rest[2 * groups :]
    out_ref, left, right, sems = rest
    phase = pl.program_id(0)
    rows = left.shape[1] // parts
    span = out_ref.shape[0]

    def moves(index):
        pairs = []
        for i in range(parts):
            source = seconds[i]
            if index == 1:
                place = pl.multiple_of(info[cot_base + i] * rows, 16)
                source = cot_ref.at[pl.ds(place, rows)]
            pairs.append((source, left.at[index, pl.ds(i * rows, rows)]))
        start = 0
        for source in (pres, hiddens)[index]:
            pairs.append((source, right.at[index, pl.ds(start, source.shape[0])]))
            start += source.shape[0]
        return [
            pltpu.make_async_copy(src, dst, sems.at[index, i]) for i, (src, dst) in enumerate(pairs)
        ]

    @pl.when((phase == 0) & (pl.program_id(1) == 0))
    def _():
        for index in range(2):
            for move in moves(index):
                move.start()

    for index in range(2):

        @pl.when((phase == index) & (pl.program_id(1) == 0))
        def _(index=index):
            wait_all(moves(index))

    at = pl.ds(pl.multiple_of(pl.program_id(1) * span, span), span)
    out_ref[...] = dot(left[phase, :, at], right[phase], TN).astype(bf16)


def norm_back(value, grad, gain):
    centred = value - jnp.mean(value, axis=-1, keepdims=True)
    spread = jnp.mean(centred * centred, axis=-1, keepdims=True)
    scale = lax.rsqrt(spread + norm_eps)
    normal = centred * scale
    weighted = grad * gain
    middle = jnp.mean(weighted, axis=-1, keepdims=True)
    slope = jnp.mean(weighted * normal, axis=-1, keepdims=True)
    return normal, scale * (weighted - middle - normal * slope)


def residual_back_body(info, residual_ref, cot_ref, gain_ref, *rest, parts, chips):
    grads, rest = rest[:parts], rest[parts:]
    wholes, (grad_ref, low_ref, own_ref, send_ref, sum_ref, weights, sems) = rest[:2], rest[2:]
    moves = proj_moves(wholes, weights, chips, sems)

    @pl.when(pl.program_id(0) == 0)
    def _():
        for move in moves:
            move.start()
        sum_ref[...] = jnp.zeros_like(sum_ref)

    grad = grads[0][...].astype(f32)
    for other in grads[1:]:
        grad += other[...].astype(f32)
    normal, back = norm_back(residual_ref[...], grad, gain_ref[...])
    cotangent = cot_ref[...].astype(f32)
    total = cotangent + back
    grad_ref[...] = total
    low_ref[...] = total.astype(bf16)
    sum_ref[0:1, :] += jnp.sum(grad * normal, axis=0, keepdims=True)
    sum_ref[1:2, :] += jnp.sum(grad, axis=0, keepdims=True)
    sum_ref[2:3, :] += jnp.sum(total, axis=0, keepdims=True)
    sum_ref[3:4, :] += jnp.sum(cotangent, axis=0, keepdims=True)

    @pl.when(pl.program_id(0) == 0)
    def _():
        wait_all(moves)

    both = dot(low_ref[...], weights[...]).astype(bf16)
    width = own_ref.shape[1]
    own_ref[...] = both[:, :width]
    send_ref[...] = both[:, width:]


def qkv_grad_body(info, first_ref, grad_ref, own_ref, got_ref, att_own, att_got, *rest):
    out_ref = rest[-1]
    width = grad_ref.shape[1]
    out_ref[:, :width] = dot(first_ref[...], grad_ref[...], TN).astype(bf16)
    out_ref[:, width:] = (
        dot(own_ref[...], att_own[...], TN) + dot(got_ref[...], att_got[...], TN)
    ).astype(bf16)


def first_norm_body(info, *refs, chips):
    grads, (x_ref, res_ref, gain_ref, *rest) = refs[: 2 * chips], refs[2 * chips :]
    two_ref, biases, hiddens, rest = rest[0], rest[1 : 1 + chips], rest[1 + chips : 4 + chips], rest[4 + chips :]
    wholes, (low_ref, sum_ref, weights, lefts, total, sems) = rest[:2], rest[2:]
    half, width = lefts.shape[1:]
    part = wholes[0].shape[1] // chips

    def move(i):
        return pltpu.make_async_copy(
            wholes[i // chips].at[:, pl.ds(i % chips * part, width)], weights.at[i], sems.at[i]
        )

    for i in range(2 * chips):
        move(i).start()
    for i in range(2 * chips):
        lefts[i] = grads[i][...]
    total[...] = jnp.zeros_like(total)

    def term(i, _):
        pltpu.make_async_copy(
            wholes[0].at[:, pl.ds(0, width)], weights.at[i], sems.at[i]
        ).wait()
        total[...] += dot(lefts[i], weights[i], NT)
        return 0

    lax.fori_loop(0, 2 * chips, term, 0)
    step = row_step(total.shape[0])
    sum_ref[...] = jnp.zeros_like(sum_ref)
    for i, j in enumerate((2, 0, 1, 3)):
        sum_ref[2 + i : 3 + i, :] = two_ref[j : j + 1, :]
    pairs = biases[0].shape[0]
    for b in range(chips):
        for kind in range(2):
            for pair in range(pairs):
                to = ((b * 2 + kind) * pairs + pair) * LANES
                value = biases[b][pair, :, kind * 2 * LANES : (kind * 2 + 1) * LANES]
                sum_ref[6:7, to : to + LANES] = value
    ff = hiddens[0].shape[1]
    sum_ref[7:8, 0:ff] = hiddens[0][...] + hiddens[1][...] + hiddens[2][...]

    def rows(i, _):
        at = pl.ds(pl.multiple_of(i * step, 16), step)
        grad = total[at, :]
        normal, back = norm_back(x_ref[at, :].astype(f32), grad, gain_ref[...])
        low_ref[at, :] = (back + res_ref[at, :]).astype(bf16)
        sum_ref[0:1, :] += jnp.sum(grad * normal, axis=0, keepdims=True)
        sum_ref[1:2, :] += jnp.sum(grad, axis=0, keepdims=True)
        return 0

    lax.fori_loop(0, total.shape[0] // step, rows, 0)


def shards(
    tokens,
    offsets,
    first_gain,
    first_shift,
    qkv_weight,
    qv_bias,
    proj_weight,
    proj_bias,
    second_gain,
    second_shift,
    expand_weight,
    expand_bias,
    shrink_weight,
    shrink_bias,
    cotangent,
):
    token_rows, dim = tokens.shape
    sets = offsets.shape[0]
    part = qkv_weight.shape[2]
    ff = expand_weight.shape[1]
    chips = lax.axis_size("mp") // 2
    ring = Ring(lax.axis_size("dp"))
    dp_index = lax.axis_index("dp")
    mp_index = lax.axis_index("mp")
    x_index, core = mp_index // 2, mp_index % 2
    sets_x = -(-sets // chips)
    slots = sets_x * chips
    rows_x = sets_x * SET_ROWS
    half = rows_x // 2
    pairs = part // LANES
    groups = chips * pairs
    unit_rows = dim // ring.count
    unit = unit_rows // 2
    width = 3 * part
    att_width = groups * LANES
    near = [(0, 0), (0, 1)]
    far_other = [(step, 1) for step in range(1, chips)]
    far_own = [(step, 0) for step in range(1, chips)]
    keys = near + far_other + far_own
    sem = pltpu.SemaphoreType.DMA
    row = lambda value: value.reshape(1, -1)
    whole = lambda *dims: pl.BlockSpec(dims, lambda *_: (0,) * len(dims))

    row_starts = lax.dynamic_index_in_dim(ring.piece_rows(unit_rows), dp_index, 0, False)
    block_ranks = lax.dynamic_index_in_dim(ring.block_ranks(), dp_index, 0, False)
    places = [(x_index - step) % chips * 2 + (core ^ other) for step, other in keys]
    info = jnp.concatenate(
        [jnp.stack([core, x_index, *places]).astype(jnp.int32), row_starts, block_ranks]
    )
    place_base = 2
    base = place_base + len(keys)
    ranks = base + ring.count + 1

    order = Order(info)

    qkv_shard = qkv_weight.astype(bf16).reshape(unit_rows, 3, pairs, LANES)
    qkv_shard = qkv_shard.transpose(0, 2, 1, 3).reshape(unit_rows, width)
    shard = jnp.concatenate([qkv_shard, proj_weight.astype(bf16).T], axis=1)
    bias_shard = jnp.zeros((pairs, 3, LANES), f32)
    bias_shard = bias_shard.at[:, 0].set(qv_bias[0].reshape(pairs, LANES))
    bias_shard = bias_shard.at[:, 2].set(qv_bias[1].reshape(pairs, LANES)).reshape(1, width)
    high = bias_shard.astype(bf16)
    both = jnp.concatenate([high, (bias_shard - high.astype(f32)).astype(bf16)])
    below = jnp.pad(both, ((0, 14), (0, part)))
    joined = jnp.concatenate([shard, below])
    attn_steps = ring.gather_steps(shard, 0, order)
    attn_pieces = [shard]
    far_pieces = {step: [across(joined, step, chips)] for step in range(1, chips)}
    bias_x = [bias_shard]
    for step in range(1, chips):
        got = far_pieces[step][0][unit_rows : unit_rows + 2, :width].astype(f32)
        bias_x.append(got[0:1] + got[1:2])

    def next_step(steps, pieces):
        got = next(steps, None)
        if got is not None:
            pieces += got
        return got

    def send_far(got):
        joined = jnp.concatenate(order.after(got))
        for step in range(1, chips):
            far_pieces[step].append(across(joined, step, chips))

    def last_far(i=-1):
        return [far_pieces[step][i] for step in range(1, chips)]

    def pad_sets(value, wait):
        columns = pl.BlockSpec((token_rows, CHUNK), lambda i, _: (0, i))
        kernel = call(
            functools.partial(pad_body, sets=sets),
            (dim // CHUNK,),
            [columns],
            pl.BlockSpec((slots * SET_ROWS, CHUNK), lambda i, _: (0, i)),
            shape((slots * SET_ROWS, dim), bf16),
            [pltpu.VMEM((token_rows + 16, CHUNK), f32)],
            "pad",
        )
        return order.run(kernel, value, wait=wait)

    got = next_step(attn_steps, attn_pieces)
    order.due = last_far()
    after = next_step(attn_steps, attn_pieces)
    order.due = ()
    send_far(got)
    x_rows = pad_sets(tokens, ())
    order.due = last_far()
    got = next_step(attn_steps, attn_pieces)
    order.due = ()
    send_far(after)
    kernel = call(
        first_low_body,
        (sets_x,),
        [
            pl.BlockSpec((SET_ROWS, dim), lambda i, info: (info[1] * sets_x + i, 0)),
            whole(1, dim),
            whole(1, dim),
        ],
        pl.BlockSpec((SET_ROWS, dim), lambda i, _: (i, 0)),
        shape((rows_x, dim), bf16),
        [],
        "first_low",
    )
    first_low = order.run(kernel, x_rows, row(first_gain), row(first_shift))
    while got:
        order.due = last_far(-2)
        after = next_step(attn_steps, attn_pieces)
        if after is None:
            shrink_shard = tie(shrink_weight, far_pieces[1][0]).astype(bf16).T
            mlp_shard = jnp.concatenate([expand_weight.astype(bf16), shrink_shard], axis=1)
            mlp_pieces = [mlp_shard]
            mlp_steps = ring.gather_steps(tie(mlp_shard, got), 0, order)
            next_step(mlp_steps, mlp_pieces)
        order.due = ()
        send_far(got)
        got = after
    order.due = last_far(-2) + last_far()
    starts = tie(jnp.pad(offsets, ((0, slots - sets), (0, 0))), order.now)
    starts = lax.dynamic_slice_in_dim(starts, x_index * sets_x, sets_x, axis=0)
    positions = jnp.arange(SET_ROWS, dtype=jnp.int32)
    ids = jnp.sum((positions[None, :, None] >= starts[:, None, :]).astype(jnp.int32), axis=-1)
    ids = jnp.where(positions[None, :] < SET_TOKENS, ids, -1)
    key_ids, query_ids = ids[:, :, None], ids[:, None, :]
    cot = pad_sets(cotangent, (key_ids, query_ids))
    next_step(mlp_steps, mlp_pieces)
    order.due = ()
    count = len(attn_pieces)
    copies = count * chips
    far_list = [piece for step in range(1, chips) for piece in far_pieces[step]]

    joint = chips * (width + part)
    kernel = call(
        functools.partial(qkv_body, base=base, unit=unit, chips=chips, count=count),
        (2,),
        [pl.BlockSpec((half, dim), lambda i, _: (i, 0)), whole(1, chips * width)]
        + [ANY] * (count + len(far_list)),
        [pl.BlockSpec((half, chips * width), lambda i, _: (i, 0)), HBM],
        [shape((rows_x, chips * width), bf16), shape((dim, joint), bf16)],
        [pltpu.VMEM((dim, joint), bf16), sem((copies,)), sem],
        "qkv",
    )
    qkv, weights = order.run(kernel, first_low, jnp.concatenate(bias_x, axis=1), *attn_pieces, *far_list)
    order.due = mlp_pieces[-2:]
    both_weights = [weights, partner(order.after(weights), chips)]

    order.due = ()
    next_step(mlp_steps, mlp_pieces)
    kernel = call(
        attend_body,
        (sets_x, groups),
        [
            pl.BlockSpec((SET_ROWS, 3 * LANES), lambda s, i, _: (s, i)),
            pl.BlockSpec((1, SET_ROWS, 1), lambda s, i, _: (s, 0, 0)),
            pl.BlockSpec((1, 1, SET_ROWS), lambda s, i, _: (s, 0, 0)),
        ],
        [
            pl.BlockSpec((SET_ROWS, LANES), lambda s, i, _: (s, i)),
            pl.BlockSpec((1, 1, 2, SET_ROWS), lambda s, i, _: (s, i, 0, 0)),
        ],
        [
            shape((rows_x, att_width), bf16),
            shape((sets_x, groups, 2, SET_ROWS), f32),
        ],
        [pltpu.VMEM((SET_ROWS, SET_ROWS), f32)],
        "attend",
    )
    attended, logs = order.run(kernel, qkv, key_ids, query_ids)
    order.due = [*mlp_pieces[-2:], both_weights[1]]
    attended_other = partner(order.after(attended), chips)
    order.due = ()
    next_step(mlp_steps, mlp_pieces)

    own_half = lambda *dims: pl.BlockSpec(dims, lambda i, info: (info[0], 0))
    own_place = lambda *dims: pl.BlockSpec(dims, lambda i, info: (info[place_base], 0))
    proj_scratch = [pltpu.VMEM((dim, 2 * att_width), bf16), sem((2 * chips,))]
    kernel = call(
        functools.partial(proj_norm_body, chips=chips),
        (1,),
        [own_half(half, att_width)] * 2 + [own_place(half, dim)] + [whole(1, dim)] * 3 + [HBM] * 2,
        [whole(half, dim), whole(half, dim)],
        [shape((half, dim), f32), shape((half, dim), bf16)],
        proj_scratch,
        "proj_norm",
    )
    residual, second_low = order.run(
        kernel,
        attended,
        attended_other,
        x_rows,
        row(proj_bias),
        row(second_gain),
        row(second_shift),
        *both_weights,
    )
    seconds = {(0, 0): second_low}
    for step in range(1, chips):
        seconds[(step, 0)] = across(second_low, step, chips)
    order.due = mlp_pieces[-2:]
    seconds[(0, 1)] = partner(order.after(second_low), chips)
    order.due = ()
    while next_step(mlp_steps, mlp_pieces):
        pass

    def feed(group, gots=()):
        parts = len(group)
        first = keys.index(group[0])
        kernel = call(
            functools.partial(
                mlp_body, base=base, unit=unit, count=count, parts=parts, adds=len(gots)
            ),
            (parts,),
            [
                pl.BlockSpec((half, dim), lambda i, info: (info[place_base + first + i], 0)),
                whole(1, ff),
            ]
            + [HBM] * (count + parts)
            + [whole(half, dim)] * len(gots),
            [pl.BlockSpec((half, ff), lambda i, _: (i, 0))] * 2
            + [whole(half, dim)] * (2 * parts)
            + [whole(1, ff)],
            [shape((parts * half, ff), bf16)] * 2
            + [shape((half, dim), bf16)] * (2 * parts)
            + [shape((1, ff), f32)],
            [
                pltpu.VMEM((dim, ff), bf16),
                pltpu.VMEM((dim, ff), bf16),
                pltpu.VMEM((parts, half, dim), bf16),
                sem((2 * count,)),
                sem((parts,)),
            ],
            "mlp",
        )
        outs = order.run(
            kernel,
            cot,
            row(expand_bias),
            *mlp_pieces,
            *[seconds[key] for key in group],
            *gots,
        )
        backs, rows = outs[2 : 2 + parts], outs[2 + parts : 2 + 2 * parts]
        return outs[0], outs[1], list(backs), list(rows), outs[-1]

    first = feed(near)
    for step in range(1, chips):
        seconds[(step, 1)] = partner(order.after(seconds[(step, 0)]), chips)
    own = feed(far_own)
    other = feed(far_other)
    back_sums = [
        (mine.astype(f32) + partner(got, chips).astype(f32)).astype(bf16)
        for mine, got in zip(own[2], other[2])
    ]
    feeds = [first, other, own]

    def along_x(own, sums):
        terms = [own[0], partner(own[1], chips)]
        return terms + [across(value, chips - 1 - i, chips) for i, value in enumerate(sums)]

    back_terms = along_x(first[2], back_sums)
    span = 2 * CHUNK
    total_rows = len(keys) * half
    kernel = call(
        functools.partial(mlp_grad_body, cot_base=place_base, parts=len(keys), groups=3),
        (2, dim // span),
        [HBM] * (7 + len(keys)),
        pl.BlockSpec((span, ff), lambda p, i, _: (i, p)),
        shape((dim, 2 * ff), bf16),
        [
            pltpu.VMEM((2, total_rows, dim), bf16),
            pltpu.VMEM((2, total_rows, ff), bf16),
            sem((2, len(keys) + 3)),
        ],
        "mlp_grad",
    )
    mlp_grad = order.run(
        kernel,
        cot,
        *[seconds[key] for key in keys],
        *[outs[0] for outs in feeds],
        *[outs[1] for outs in feeds],
    )
    mlp_ring = ring.scatter_steps(mlp_grad, ranks, order)
    mlp_due = next(mlp_ring)

    if chips == 2:
        out_far = own[3][0].astype(f32)
        out_far = (out_far + partner(other[3][0], chips).astype(f32)).astype(bf16)
        out_near = order.after(residual) + shrink_bias + first[3][0].astype(f32)
        out_near = (out_near + partner(first[3][1], chips).astype(f32)).astype(bf16)
        order.hold = out_far, out_near
    step_rows = row_step(half)
    cot_rows = pl.BlockSpec(
        (step_rows, dim), lambda i, info: (info[place_base] * (half // step_rows) + i, 0)
    )
    plain_rows = lambda count: pl.BlockSpec((step_rows, count), lambda i, _: (i, 0))
    kernel = call(
        functools.partial(residual_back_body, parts=len(back_terms), chips=chips),
        (half // step_rows,),
        [plain_rows(dim), cot_rows, whole(1, dim)]
        + [plain_rows(dim)] * len(back_terms)
        + [HBM] * 2,
        [plain_rows(dim)] * 2 + [plain_rows(att_width)] * 2 + [whole(8, dim)],
        [
            shape((half, dim), f32),
            shape((half, dim), bf16),
            shape((half, att_width), bf16),
            shape((half, att_width), bf16),
            shape((8, dim), f32),
        ],
        proj_scratch,
        "residual_back",
    )
    grad_residual, residual_low, grad_own, grad_send, sums_two = order.run(
        kernel, residual, cot, row(second_gain), *back_terms, *both_weights
    )
    order.due = mlp_due
    grad_got = partner(order.after(grad_send), chips)
    residual_other = partner(order.after(residual_low), chips)
    order.due = ()
    mlp_due = next(mlp_ring)
    if chips == 2:
        out_rows = jnp.concatenate([out_far, out_near])
        cuts = [0, half // 16 * 8, half * 5 // 32 * 8, 2 * half]
        out_sends = iter([out_rows[i:j] for i, j in zip(cuts, cuts[1:])])
        out_gots = [across(order.after(next(out_sends)), 1, chips)]
    else:
        out_own = [
            (mine.astype(f32) + partner(order.after(got), chips).astype(f32)).astype(bf16)
            for mine, got in zip(own[3], other[3])
        ]
        out_terms = along_x(order.after(first[3]), out_own)

    def attend_back(b):
        half_block = lambda j: pl.BlockSpec(
            (row_step(half), LANES), lambda i, s, _: (lax.rem(2 * s + j, sets_x), b * pairs + i)
        )
        kernel = call(
            functools.partial(attend_back_body, first_half=sets_x),
            (pairs, sets_x),
            [
                pl.BlockSpec((SET_ROWS, 3 * LANES), lambda i, s, _: (s, b * pairs + i)),
                pl.BlockSpec((1, SET_ROWS, 1), lambda i, s, _: (s, 0, 0)),
                pl.BlockSpec((1, 1, SET_ROWS), lambda i, s, _: (s, 0, 0)),
                pl.BlockSpec((1, 1, 2, SET_ROWS), lambda i, s, _: (s, b * pairs + i, 0, 0)),
                half_block(0),
                half_block(0),
                half_block(1),
                half_block(1),
            ],
            [
                pl.BlockSpec((SET_ROWS, 3 * LANES), lambda i, s, _: (s, i)),
                pl.BlockSpec((1, 1, 3 * LANES), lambda i, s, _: (i, 0, 0)),
            ],
            [shape((rows_x, width), bf16), shape((pairs, 1, 3 * LANES), f32)],
            [pltpu.VMEM((sets_x, SET_ROWS, SET_ROWS), f32)],
            "attend_back",
        )
        ids = key_ids, query_ids
        return order.run(kernel, qkv, *ids, logs, grad_own, grad_got, grad_own, grad_got)

    def qkv_grad(b, before):
        columns = lambda count: pl.BlockSpec((count, CHUNK), lambda i, _: (0, i))
        kernel = call(
            qkv_grad_body,
            (dim // CHUNK,),
            [
                columns(rows_x),
                whole(rows_x, width),
                columns(half),
                columns(half),
                pl.BlockSpec((half, part), lambda i, info: (info[0], b)),
                pl.BlockSpec((half, part), lambda i, info: (1 - info[0], b)),
            ]
            + [ANY] * len(before),
            pl.BlockSpec((CHUNK, width + part), lambda i, _: (i, b)),
            shape((dim, joint), bf16),
            [],
            "qkv_grad",
            {7 + i: i for i in range(len(before))},
        )
        return order.run(
            kernel,
            first_low,
            grads_qkv[b],
            residual_low,
            residual_other,
            attended,
            attended,
            *before,
        )

    def out_due(i):
        if chips != 2:
            return ()
        if i < 2:
            out_gots.append(across(order.after(next(out_sends)), 1, chips))
        return out_gots[i]

    grads_qkv, grads_other, qkv_sums, begun = {}, {}, {}, ()
    for b in range(1, chips):
        grads_qkv[b], qkv_sums[b] = attend_back(b)
        order.due = mlp_due, residual_other, out_due(b - 1)
        grads_other[b] = partner(order.after(grads_qkv[b]), chips)
        order.due = ()
        mlp_due = next(mlp_ring, ())
        begun = (qkv_grad(b, begun),)
    grads_qkv[0], qkv_sums[0] = attend_back(0)
    order.due = mlp_due, [grads_other[b] for b in range(1, chips)], out_due(1)
    grads_other[0] = partner(order.after(grads_qkv[0]), chips)
    order.due = ()
    mlp_due = next(mlp_ring, ())
    attn_ring = ring.scatter_steps(qkv_grad(0, begun), ranks, order, "ring_end")
    order.due = [grads_other[b] for b in range(chips)]
    order.hold = next(attn_ring)
    order.due = ()
    for mlp_grad in mlp_ring:
        pass
    expand_part, shrink_part = mlp_grad[:, :ff], mlp_grad[:, ff:].T
    out_due(2)
    if chips == 2:
        out_rows = jnp.concatenate([out_near, out_far]).astype(f32)
        out_rows = out_rows + jnp.concatenate(order.after(out_gots)).astype(f32)
    else:
        out_rows = order.after(residual) + shrink_bias
        for term in out_terms:
            out_rows = out_rows + term.astype(f32)
        low = out_rows.astype(bf16)
        out_rows = jnp.concatenate([low] + [across(low, step, chips) for step in range(1, chips)])
    out_rows = out_rows.astype(bf16)
    order.hold = out_rows
    attn_due = next(attn_ring)

    kernel = call(
        functools.partial(first_norm_body, chips=chips),
        (1,),
        [own_half(half, width)] * (2 * chips)
        + [own_place(half, dim), whole(half, dim), whole(1, dim), whole(8, dim)]
        + [whole(pairs, 1, 3 * LANES)] * chips
        + [whole(1, ff)] * 3
        + [HBM] * 2,
        [whole(half, dim), whole(8, dim)],
        [shape((half, dim), bf16), shape((8, dim), f32)],
        [
            pltpu.VMEM((2 * chips, dim, width), bf16),
            pltpu.VMEM((2 * chips, half, width), bf16),
            pltpu.VMEM((half, dim), f32),
            sem((2 * chips,)),
        ],
        "first_norm",
    )
    tokens_low, small = order.run(
        kernel,
        *[grads_qkv[b] for b in range(chips)],
        *[grads_other[b] for b in range(chips)],
        x_rows,
        grad_residual,
        row(first_gain),
        sums_two,
        *[qkv_sums[b] for b in range(chips)],
        first[4],
        other[4],
        own[4],
        *both_weights,
    )

    def assemble(rows, dtype):
        block = lambda count, at: pl.BlockSpec((count, CHUNK), lambda i, _: (at, i))
        kernel = call(
            functools.partial(assemble_body, base=place_base, sets=sets),
            (dim // CHUNK,),
            [block(half, rows[key][1]) for key in keys],
            block(token_rows, 0),
            shape((token_rows, dim), dtype),
            [
                pltpu.VMEM((slots * SET_ROWS, CHUNK), f32),
                pltpu.VMEM((token_rows + 16, CHUNK), f32),
            ],
            "assemble",
        )
        return order.run(kernel, *[rows[key][0] for key in keys])

    bits = [1 << i for i in range(ring.count.bit_length() - 1)]

    def from_rank(small, bit):
        return lax.ppermute(small, "dp", [(r, r ^ bit) for r in range(ring.count)])

    def add_chips(small):
        shared = small[:6] + partner(small[:6], chips)
        own, *others = small[6:7].reshape(chips, 2 * part)
        if chips == 2:
            sent = jnp.concatenate([shared.reshape(-1), others[0]])
            got = across(sent, 1, chips)
            shared = shared + got[: 6 * dim].reshape(6, dim)
            own = own + got[6 * dim :]
        else:
            bit = 1
            while bit < chips:
                flips = [(m, m ^ (2 * bit)) for m in range(2 * chips)]
                shared = shared + lax.ppermute(shared, "mp", flips)
                bit *= 2
            for step in range(1, chips):
                own = own + across(others[step - 1], chips - step, chips)
        own = jnp.pad(own, (0, dim - 2 * part)).reshape(1, dim)
        return jnp.concatenate([shared, own, small[7:]])

    order.due = attn_due
    tokens_low = order.after(tokens_low)
    grads, outs = {(0, 0): (tokens_low, 0)}, {}
    for step in range(1, chips):
        grads[(step, 0)] = across(tokens_low, step, chips), 0
    order.due = ()
    next(attn_ring)
    out_other = partner(order.after(out_rows), chips)
    for step in range(chips):
        outs[(step, 0)], outs[(step, 1)] = (out_rows, step), (out_other, step)

    got = from_rank(order.after(small), bits[0])
    outputs = assemble(outs, bf16)
    small = small + order.after(got)
    order.hold = (expand_part, shrink_part)
    order.due = small
    next(attn_ring)
    order.due = ()
    grads[(0, 1)] = partner(order.after(tokens_low), chips), 0
    for step in range(1, chips):
        grads[(step, 1)] = partner(order.after(grads[(step, 0)][0]), chips), 0
    small = add_chips(order.after(small))
    for attn_sum in attn_ring:
        pass
    small = order.after(small)
    attn_low = order.after(attn_sum.astype(bf16))
    sent = {}
    for step in range(1, chips):
        columns = slice(step * (width + part), (step + 1) * (width + part))
        sent[step] = across(attn_low[:, columns], chips - step, chips)
    got = from_rank(small, bits[1])
    grad_tokens = assemble(grads, f32)
    small = small + order.after(got)
    for bit in bits[2:]:
        small = small + from_rank(small, bit)
    shared = small[:6]
    bias_own = small[6, : 2 * part].reshape(2, part)
    expand_bias_grad = small[7:].reshape(-1)[:ff]
    attn_part = attn_sum[:, : width + part]
    for step in range(1, chips):
        attn_part = attn_part + order.after(sent[step]).astype(f32)

    qkv_part = attn_part[:, :width].reshape(unit_rows, pairs, 3, LANES)
    qkv_part = qkv_part.transpose(0, 2, 1, 3).reshape(unit_rows, 3, part)
    return (
        outputs,
        grad_tokens,
        shared[0],
        shared[1],
        qkv_part,
        bias_own,
        attn_part[:, width:].T,
        shared[2],
        shared[3],
        shared[4],
        expand_part,
        expand_bias_grad,
        shrink_part,
        shared[5],
    )


def solution(mesh):
    placed = (
        P("dp", None),
        P("dp", None),
        P(),
        P(),
        P("dp", None, "mp"),
        P(None, "mp"),
        P("mp", "dp"),
        P(),
        P(),
        P(),
        P("dp", "mp"),
        P("mp"),
        P("mp", "dp"),
        P(),
        P("dp", None),
    )
    return jax.shard_map(
        shards,
        mesh=mesh,
        in_specs=placed,
        out_specs=(
            P("dp", None),
            P("dp", None),
            P(),
            P(),
            P("dp", None, "mp"),
            P(None, "mp"),
            P("mp", "dp"),
            P(),
            P(),
            P(),
            P("dp", "mp"),
            P("mp"),
            P("mp", "dp"),
            P(),
        ),
        check_vma=False,
    )
```
